32 devices in a mesh: seq: 4 (over y, core), shard: 8 (over z, x).
Axes of the slice: x: 2, y: 2, z: 4, core: 2. Of those that a mesh axis runs over, the one named last changes fastest.
Arguments:
- tokens: bfloat16 [8, 1024, 1024], P('shard', 'seq'), may hold values from -6 to 6
- doc_starts: int32 [8, 4], P('shard'), may hold values from 0 to 1023, as said below
- pre_gain: bfloat16 [1024], P('shard'), may hold values from 0.099609375 to 1.8984375
- query_weight: bfloat16 [1024, 1024], P('shard'), may hold values from -0.1875 to 0.1875
- key_matrix: bfloat16 [1024, 512], P('shard'), may hold values from -0.1875 to 0.1875
- value_matrix: bfloat16 [1024, 512], P('shard'), may hold values from -0.1875 to 0.1875
- query_gain: bfloat16 [64], P('shard'), may hold values from 0.099609375 to 1.8984375
- key_gain: bfloat16 [64], P('shard'), may hold values from 0.099609375 to 1.8984375
- out_weight: bfloat16 [1024, 1024], P('shard'), may hold values from -0.75 to 0.75
- post_gain: bfloat16 [1024], P('shard'), may hold values from 0.099609375 to 1.8984375
- gate_weight: bfloat16 [1024, 4608], P('shard'), may hold values from -0.1875 to 0.1875
- up_weight: bfloat16 [1024, 4608], P('shard'), may hold values from -0.1875 to 0.1875
- down_weight: bfloat16 [4608, 1024], P('shard'), may hold values from -0.09375 to 0.09375
- cotangent: bfloat16 [8, 1024, 1024], P('shard', 'seq'), may hold values from -6 to 6
Outputs:
- output: bfloat16 [8, 1024, 1024], P('shard', 'seq')
- grad_tokens: float32 [8, 1024, 1024], P('shard', 'seq')
- grad_pregain: float32 [1024], P('shard')
- grad_qweight: float32 [1024, 1024], P('shard')
- grad_kweight: float32 [1024, 512], P('shard')
- grad_vweight: float32 [1024, 512], P('shard')
- grad_qgain: float32 [64], P('shard')
- grad_kgain: float32 [64], P('shard')
- grad_oweight: float32 [1024, 1024], P('shard')
- grad_postgain: float32 [1024], P('shard')
- grad_gate: float32 [1024, 4608], P('shard')
- grad_up: float32 [1024, 4608], P('shard')
- grad_down: float32 [4608, 1024], P('shard')
The draws below stay inside these ranges and needn't reach their ends.
Inputs may be any that keep to these rules, and one draw needn't show every extreme that they name: `doc_starts`: in each packed row the 4 document starts rise strictly; the first is 0.
All inputs are finite; a program needn't handle non-finite values.
Results may differ from the reference program's by a relative error of at most 0.023.
Values may be sent and summed in bfloat16 or wider, within the bound.
No kernel may reach another device: no remote copies, remote signals or barrier semaphores. Data moves between devices by JAX's collectives and lax.ppermute only.
A program may use at most 256 MiB of HBM per device.

```python
import math
import jax
import jax.numpy as jnp
from jax import lax

MODEL_WIDTH = 1024
QUERY_HEADS = 16
KEY_VALUE_HEADS = 8
HEAD_SIZE = 64
FF = 4608
DOCS = 4
PACKED_TOKENS = 1024
SEQS = 8


def draw_doc_starts(key, part):

    def start_row(row_key):
        picks = jax.random.permutation(row_key, PACKED_TOKENS - 1)[:DOCS - 1] + 1
        return jnp.concatenate([jnp.zeros((1,), jnp.int32), jnp.sort(picks).astype(jnp.int32)])
    return jax.vmap(start_row)(jax.random.split(key, SEQS))


def block_scale(own_key, dims, cuts, low, high):
    loudness, own = 1.0, jax.random.fold_in(own_key, 6)
    for axis_at, shards_of in cuts:
        steps = jnp.exp(jax.random.uniform(jax.random.fold_in(own, axis_at), (shards_of,), jnp.float32, low / len(cuts), high / len(cuts)))
        loudness = loudness * jnp.repeat(steps, dims[axis_at] // shards_of).reshape([-1 if axis == axis_at else 1 for axis in range(len(dims))])
    return loudness


def normal_values(stream_key, extent, deviation, most, cuts=(), kind=jnp.bfloat16):
    result = jax.random.normal(stream_key, extent, jnp.float32) * deviation
    if len(cuts) > 0:
        result = block_scale(stream_key, extent, cuts, -0.22, 0.18) * result
    return jnp.clip(result, min=-most, max=most).astype(kind)


def setup_inputs(seed: int = 0) -> dict:
    splits = jax.random.split(jax.random.key(seed), 15)
    tokens = normal_values(splits[0], (SEQS, PACKED_TOKENS, MODEL_WIDTH), 1.0, 6.0, ((0, 8), (1, 4)))
    doc_starts = draw_doc_starts(jax.random.fold_in(splits[14], 71), 0)
    pre_gain = jnp.clip(1.0 + 0.18 * jax.random.normal(splits[2], (MODEL_WIDTH,), jnp.float32), 0.099609375, 1.8984375).astype(jnp.bfloat16)
    query_weight = normal_values(splits[3], (MODEL_WIDTH, QUERY_HEADS * HEAD_SIZE), MODEL_WIDTH ** -0.5, 0.1875, ((0, 8),))
    key_matrix = normal_values(splits[4], (MODEL_WIDTH, KEY_VALUE_HEADS * HEAD_SIZE), MODEL_WIDTH ** -0.5, 0.1875, ((0, 8),))
    value_matrix = normal_values(splits[5], (MODEL_WIDTH, KEY_VALUE_HEADS * HEAD_SIZE), MODEL_WIDTH ** -0.5, 0.1875, ((0, 8),))
    query_gain = jnp.clip(1.0 + 0.18 * jax.random.normal(splits[6], (HEAD_SIZE,), jnp.float32), 0.099609375, 1.8984375).astype(jnp.bfloat16)
    key_gain = jnp.clip(1.0 + 0.18 * jax.random.normal(splits[7], (HEAD_SIZE,), jnp.float32), 0.099609375, 1.8984375).astype(jnp.bfloat16)
    out_weight = normal_values(splits[8], (QUERY_HEADS * HEAD_SIZE, MODEL_WIDTH), (MODEL_WIDTH // 16) ** -0.5, 0.75, ((0, 8),))
    post_gain = jnp.clip(1.0 + 0.18 * jax.random.normal(splits[9], (MODEL_WIDTH,), jnp.float32), 0.099609375, 1.8984375).astype(jnp.bfloat16)
    gate_weight = normal_values(splits[10], (MODEL_WIDTH, FF), MODEL_WIDTH ** -0.5, 0.1875, ((0, 8),))
    up_weight = normal_values(splits[11], (MODEL_WIDTH, FF), MODEL_WIDTH ** -0.5, 0.1875, ((0, 8),))
    down_weight = normal_values(splits[12], (FF, MODEL_WIDTH), FF ** -0.5, 0.09375, ((0, 8),))
    cotangent = normal_values(splits[13], (SEQS, PACKED_TOKENS, MODEL_WIDTH), 1.0, 6.0, ((0, 8), (1, 4)))
    return {"tokens": tokens, "doc_starts": doc_starts, "pre_gain": pre_gain, "query_weight": query_weight, "key_matrix": key_matrix, "value_matrix": value_matrix, "query_gain": query_gain, "key_gain": key_gain, "out_weight": out_weight, "post_gain": post_gain, "gate_weight": gate_weight, "up_weight": up_weight, "down_weight": down_weight, "cotangent": cotangent}


eps_norm = 1e-05
rope_base = 1000000.0
masked_score = -1e+30

@jax.custom_vjp
def reduced_precision(v):
    return lax.optimization_barrier(v.astype(jnp.bfloat16)).astype(jnp.float32)

@jax.custom_vjp
def reduced_precision_reverse(v):
    return v

def low_keep(v):
    return (reduced_precision(v), None)

def low_pass(kept, grad):
    return (grad,)

def back_keep(v):
    return (v, None)

def back_low(kept, grad):
    return (reduced_precision(grad),)
reduced_precision.defvjp(low_keep, low_pass)
reduced_precision_reverse.defvjp(back_keep, back_low)

def multiply_reduced(left, right):
    return jnp.dot(left, right, precision=lax.Precision.HIGHEST, preferred_element_type=jnp.float32)

def norm_rows(value_tokens, gain):
    return value_tokens * lax.rsqrt(lax.optimization_barrier(jnp.mean(value_tokens * value_tokens, axis=-1, keepdims=True)) + eps_norm) * gain

def rotate(value_tokens, cosine, sine):
    half = HEAD_SIZE // 2
    turned = jnp.concatenate([-value_tokens[..., half:], value_tokens[..., :half]], axis=-1)
    return value_tokens * cosine + turned * sine

def attend_block(first, queries, key_tokens_expanded, value_tokens_expanded, segment, block):
    query_rows = lax.dynamic_slice_in_dim(queries, first, block, 0)
    query_seg = lax.dynamic_slice_in_dim(segment, first, block, 0)
    query_place = first + jnp.arange(block).astype(jnp.int32)
    key_place = jnp.arange(segment.shape[0]).astype(jnp.int32)
    allowed = (query_seg[:, None] == segment[None, :]) & (query_place[:, None] >= key_place[None, :])
    scores = jnp.einsum('qhd,khd->hqk', query_rows, key_tokens_expanded, precision=lax.Precision.HIGHEST) * HEAD_SIZE ** (-0.5)
    scores = reduced_precision_reverse(jnp.where(allowed[None], scores, masked_score))
    weights = reduced_precision(jax.nn.softmax(scores, axis=-1))
    return jnp.einsum('hqk,khd->qhd', weights, value_tokens_expanded, precision=lax.Precision.HIGHEST)
checked_block = jax.checkpoint(attend_block, static_argnums=(5,))

def one_row(params, row, starts):
    pre_gain, query_weight, key_matrix, value_matrix, query_gain, key_gain, out_weight, post_gain, gate_weight, up_weight, down_weight = params
    places = jnp.arange(PACKED_TOKENS).astype(jnp.int32)
    before = starts[None, :] <= places[:, None]
    segment = lax.optimization_barrier(jnp.sum(before.astype(jnp.int32), axis=1))
    begin = lax.optimization_barrier(jnp.max(jnp.where(before, starts[None, :], 0), axis=1))
    inverse = jnp.exp(jnp.arange(HEAD_SIZE // 2).astype(jnp.float32) * (-2.0 * math.log(rope_base) / HEAD_SIZE))
    angle = (places - begin).astype(jnp.float32)[:, None] * inverse[None, :]
    angle = jnp.concatenate([angle, angle], axis=1)
    cosine = jnp.cos(angle)[:, None, :]
    sine = jnp.sin(angle)[:, None, :]
    normalized_input = reduced_precision(norm_rows(row, pre_gain))
    query_proj = reduced_precision_reverse(multiply_reduced(normalized_input, query_weight)).reshape(PACKED_TOKENS, QUERY_HEADS, HEAD_SIZE)
    key_projected = reduced_precision_reverse(multiply_reduced(normalized_input, key_matrix)).reshape(PACKED_TOKENS, KEY_VALUE_HEADS, HEAD_SIZE)
    value_tokens = reduced_precision_reverse(reduced_precision(multiply_reduced(normalized_input, value_matrix))).reshape(PACKED_TOKENS, KEY_VALUE_HEADS, HEAD_SIZE)
    queries = reduced_precision_reverse(reduced_precision(rotate(norm_rows(query_proj, query_gain), cosine, sine)))
    key_tokens = reduced_precision_reverse(reduced_precision(rotate(norm_rows(key_projected, key_gain), cosine, sine)))
    key_tokens_expanded = jnp.repeat(key_tokens, QUERY_HEADS // KEY_VALUE_HEADS, axis=1)
    value_tokens_expanded = jnp.repeat(value_tokens, QUERY_HEADS // KEY_VALUE_HEADS, axis=1)
    block = min(512, PACKED_TOKENS)
    firsts = jnp.arange(PACKED_TOKENS // block).astype(jnp.int32) * block
    attended = lax.map(lambda first: checked_block(first, queries, key_tokens_expanded, value_tokens_expanded, segment, block), firsts)
    attended = reduced_precision_reverse(reduced_precision(attended.reshape(PACKED_TOKENS, QUERY_HEADS * HEAD_SIZE)))
    middle = row + reduced_precision_reverse(multiply_reduced(attended, out_weight))
    normed_mid = reduced_precision(norm_rows(middle, post_gain))
    gate = reduced_precision_reverse(multiply_reduced(normed_mid, gate_weight))
    upper = reduced_precision_reverse(multiply_reduced(normed_mid, up_weight))
    hidden = reduced_precision(jax.nn.silu(gate) * upper)
    return middle + reduced_precision_reverse(multiply_reduced(hidden, down_weight))

def forward(packed_rows, params, starts):
    checked_row = jax.checkpoint(one_row)

    def step(carry, item):
        return (carry, checked_row(params, item[0], item[1]))
    _, outputs = lax.scan(step, jnp.zeros((), jnp.float32), (packed_rows, starts))
    return outputs

def reference(tokens, doc_starts, pre_gain, query_weight, key_matrix, value_matrix, query_gain, key_gain, out_weight, post_gain, gate_weight, up_weight, down_weight, cotangent):
    params = (pre_gain.astype(jnp.float32), query_weight.astype(jnp.float32), key_matrix.astype(jnp.float32), value_matrix.astype(jnp.float32), query_gain.astype(jnp.float32), key_gain.astype(jnp.float32), out_weight.astype(jnp.float32), post_gain.astype(jnp.float32), gate_weight.astype(jnp.float32), up_weight.astype(jnp.float32), down_weight.astype(jnp.float32))

    def run(packed_rows, weights):
        return forward(packed_rows, weights, doc_starts)
    output, pull = jax.vjp(run, tokens.astype(jnp.float32), params)
    grad_rows, grads = pull(cotangent.astype(jnp.float32))
    return (output.astype(jnp.bfloat16), grad_rows, grads[0], grads[1], grads[2], grads[3], grads[4], grads[5], grads[6], grads[7], grads[8], grads[9], grads[10])
```

```python
import math

import jax
import jax.numpy as jnp
from jax import lax
from jax.sharding import PartitionSpec as P

QUERY_HEADS = 16
KEY_VALUE_HEADS = 8
HEAD_SIZE = 64
GROUP = QUERY_HEADS // KEY_VALUE_HEADS


eps_norm = 1e-05
rope_base = 1000000.0
masked_score = -1e30

bf16 = jnp.bfloat16
f32 = jnp.float32


def dot(left, right):
    return jnp.dot(left, right, preferred_element_type=f32)


def times_t(left, right):
    return lax.dot_general(left, right, (((1,), (1,)), ((), ())), preferred_element_type=f32)


def t_times(left, right):
    return lax.dot_general(left, right, (((0,), (0,)), ((), ())), preferred_element_type=f32)


def inverse_root(value_tokens):
    return lax.rsqrt(jnp.mean(value_tokens * value_tokens, axis=-1, keepdims=True) + eps_norm)


def norm_back(grad_scaled, value_tokens, root):
    return root * (
        grad_scaled
        - value_tokens
        * (root * root)
        * jnp.mean(grad_scaled * value_tokens, axis=-1, keepdims=True)
    )


def rope_tables(places):
    inverse = jnp.exp(
        jnp.arange(HEAD_SIZE // 2, dtype=f32) * (-2.0 * math.log(rope_base) / HEAD_SIZE)
    )
    angle = places.astype(f32)[:, None] * inverse[None, :]
    angle = jnp.concatenate([angle, angle], axis=1)
    return (jnp.cos(angle)[:, None, :], jnp.sin(angle)[:, None, :])


def rotate(value_tokens, cosine, sine):
    half = HEAD_SIZE // 2
    turned = jnp.concatenate([-value_tokens[..., half:], value_tokens[..., :half]], axis=-1)
    return value_tokens * cosine + turned * sine


def rotate_back(grads, cosine, sine):
    half = HEAD_SIZE // 2
    scaled = grads * sine
    return grads * cosine + jnp.concatenate([scaled[..., half:], -scaled[..., :half]], axis=-1)


def segment_info(starts, places):
    before = starts[None, :] <= places[:, None]
    segment = jnp.sum(before.astype(jnp.int32), axis=1)
    begin = jnp.max(jnp.where(before, starts[None, :], 0), axis=1)
    return (segment, places - begin)


def per_device(
    tokens,
    doc_starts,
    pre_gain,
    query_weight,
    key_matrix,
    value_matrix,
    query_gain,
    key_gain,
    out_weight,
    post_gain,
    gate_weight,
    up_weight,
    down_weight,
    cotangent,
):
    S = lax.axis_size("seq")
    N = lax.axis_size("shard")
    Q = lax.axis_index("seq")
    T, D = tokens.shape[1:]
    L = S * T
    rows_d = D // N
    qd = QUERY_HEADS * HEAD_SIZE // S
    kd = KEY_VALUE_HEADS * HEAD_SIZE // S
    FF = gate_weight.shape[1]
    piece = FF // N // S
    FQ = FF // S

    def swap(x, step):
        return lax.ppermute(x, "seq", [(i, i ^ step) for i in range(S)])

    def gather_seq(x):
        blocks = x[None]
        step = S // 2
        while step:
            other = swap(blocks, step)
            blocks = jnp.stack([blocks, other], axis=1).reshape((-1,) + x.shape)
            step //= 2
        return blocks

    def gather_rows(x):
        return gather_seq(x).reshape((-1,) + x.shape[1:])

    def scatter_seq(rows):
        def reduce(low, size):
            if size == 2:
                both = rows(low * T, 2 * T)
                return both[:T] + swap(both[T:].astype(bf16), 1).astype(f32)
            half = size // 2
            far = swap(reduce(low + half, half).astype(bf16), half)
            return reduce(low, half) + far.astype(f32)

        return reduce(0, S)

    def order_seq(blocks):
        return jnp.stack([lax.dynamic_index_in_dim(blocks, Q ^ i, 0, False) for i in range(S)])

    starts = doc_starts[0]
    blocks_at = jnp.arange(S, dtype=jnp.int32) ^ Q
    places = (blocks_at[:, None] * T + jnp.arange(T, dtype=jnp.int32)[None, :]).reshape(L)
    segment, inside = segment_info(starts, places)
    cosine, sine = rope_tables(inside)
    allowed = (segment[:, None] == segment[None, :]) & (places[:, None] >= places[None, :])

    width = qd + 2 * kd
    own = jnp.concatenate(
        [
            lax.dynamic_slice_in_dim(query_weight, Q * qd, qd, 1),
            lax.dynamic_slice_in_dim(key_matrix, Q * kd, kd, 1),
            lax.dynamic_slice_in_dim(value_matrix, Q * kd, kd, 1),
            lax.dynamic_slice_in_dim(out_weight, Q * (D // S), D // S, 1),
        ],
        axis=1,
    )
    gains = jnp.concatenate([pre_gain, post_gain, query_gain, key_gain])
    gains_rows = jnp.zeros((16, own.shape[1]), bf16)
    gains_rows = gains_rows.at[0, : gains.shape[0]].set(gains)
    packed = lax.all_gather(jnp.concatenate([own, gains_rows], axis=0), "shard", axis=0)
    full_qkv = packed[:, :rows_d, :width].reshape(D, width)
    out_columns = packed[:, :rows_d, width:].reshape(D, D // S)
    full_gains = packed[:, rows_d, : gains.shape[0]]
    at = 0
    pieces = []
    for size in (rows_d, rows_d, HEAD_SIZE // N, HEAD_SIZE // N):
        pieces.append(full_gains[:, at : at + size].reshape(-1).astype(f32))
        at += size
    full_pre, full_post, full_qgain, full_kgain = pieces
    out_blocks = out_columns.reshape(S, qd, D // S)
    out_rows = [lax.dynamic_index_in_dim(out_blocks, Q, 0, False)]
    for r in range(1, S):
        out_rows.append(swap(lax.dynamic_index_in_dim(out_blocks, Q ^ r, 0, False), r))
    full_out = order_seq(jnp.stack(out_rows)).transpose(1, 0, 2).reshape(qd, D)

    def own_columns(weight):
        return lax.dynamic_index_in_dim(
            weight.reshape(rows_d, N, S, piece), Q, 2, False
        ).reshape(rows_d, FQ)

    both_columns = jnp.concatenate([own_columns(gate_weight), own_columns(up_weight)], axis=1)
    full_both = lax.all_gather(both_columns, "shard", axis=0, tiled=True)
    full_down = lax.all_gather(
        lax.dynamic_slice_in_dim(down_weight, Q * piece, piece, 0), "shard", axis=0, tiled=True
    )

    all_tokens = gather_rows(tokens[0])
    cot = cotangent[0]
    all_cot = gather_rows(cot)
    wide = all_tokens.astype(f32)
    root_in = inverse_root(wide)
    scaled_in = wide * root_in
    normed_in = (scaled_in * full_pre).astype(bf16)
    projected = dot(normed_in, full_qkv)
    query_proj = projected[:, :qd].reshape(L, -1, HEAD_SIZE)
    key_proj = projected[:, qd : qd + kd].reshape(L, -1, HEAD_SIZE)
    values = projected[:, qd + kd :].astype(bf16).reshape(L, -1, HEAD_SIZE)
    query_root = inverse_root(query_proj)
    key_root = inverse_root(key_proj)
    queries = rotate(query_proj * query_root * full_qgain, cosine, sine).astype(bf16)
    keys = rotate(key_proj * key_root * full_kgain, cosine, sine).astype(bf16)
    queries = queries.reshape(L, -1, GROUP, HEAD_SIZE)
    scale = HEAD_SIZE ** (-0.5)
    scores = jnp.einsum("qngd,knd->ngqk", queries, keys, preferred_element_type=f32) * scale
    scores = jnp.where(allowed, scores, masked_score)
    probs = jax.nn.softmax(scores, axis=-1)
    attended = (
        jnp.einsum("ngqk,knd->qngd", probs.astype(bf16), values, preferred_element_type=f32)
        .astype(bf16)
        .reshape(L, qd)
    )
    local = tokens[0].astype(f32)
    middle = local + scatter_seq(
        lambda first, count: dot(attended[first : first + count], full_out)
    )

    root_mid = inverse_root(middle)
    scaled_mid = middle * root_mid
    normed_mid = gather_rows((scaled_mid * full_post).astype(bf16))
    both = dot(normed_mid, full_both)
    gate, upper = both[:, :FQ], both[:, FQ:]
    sigmoid = jax.nn.sigmoid(gate)
    swish = gate * sigmoid
    hidden = (swish * upper).astype(bf16)
    term_down = t_times(hidden, all_cot)
    shard_down = lax.psum_scatter(
        term_down.astype(bf16), "shard", scatter_dimension=0, tiled=True
    )
    grad_hidden = times_t(all_cot, full_down)
    grad_both = jnp.concatenate(
        [
            (grad_hidden * upper * (sigmoid * (1.0 + gate * (1.0 - sigmoid)))).astype(bf16),
            (grad_hidden * swish).astype(bf16),
        ],
        axis=1,
    )
    grad_nmid = scatter_seq(
        lambda first, count: times_t(grad_both[first : first + count], full_both)
    )
    term_both = t_times(normed_mid, grad_both)
    shard_both = lax.psum_scatter(
        term_both.astype(bf16), "shard", scatter_dimension=0, tiled=True
    )
    output = middle + scatter_seq(
        lambda first, count: dot(hidden[first : first + count], full_down)
    )
    term_post = jnp.sum(grad_nmid * scaled_mid, axis=0)
    grad_middle = cot.astype(f32) + norm_back(grad_nmid * full_post, middle, root_mid)

    grad_branch = gather_rows(grad_middle.astype(bf16))
    grad_attended = times_t(grad_branch, full_out).astype(bf16)
    term_out = t_times(attended, grad_branch).astype(bf16)
    grad_heads = grad_attended.reshape(L, -1, GROUP, HEAD_SIZE)
    delta = jnp.sum(
        grad_heads.astype(f32) * attended.reshape(grad_heads.shape).astype(f32), axis=-1
    ).transpose(1, 2, 0)
    grad_probs = jnp.einsum("qngd,knd->ngqk", grad_heads, values, preferred_element_type=f32)
    grad_scores = (probs * (grad_probs - delta[..., None])).astype(bf16)
    grad_queries = (
        jnp.einsum("ngqk,knd->qngd", grad_scores, keys, preferred_element_type=f32) * scale
    ).astype(bf16)
    grad_keys = (
        jnp.einsum("ngqk,qngd->knd", grad_scores, queries, preferred_element_type=f32) * scale
    ).astype(bf16)
    grad_values = jnp.einsum(
        "ngqk,qngd->knd", probs.astype(bf16), grad_heads, preferred_element_type=f32
    ).astype(bf16)
    grad_qnorm = rotate_back(
        grad_queries.reshape(L, -1, HEAD_SIZE).astype(f32), cosine, sine
    )
    grad_knorm = rotate_back(grad_keys.astype(f32), cosine, sine)
    term_qgain = jnp.sum(grad_qnorm * query_proj * query_root, axis=(0, 1))
    term_kgain = jnp.sum(grad_knorm * key_proj * key_root, axis=(0, 1))
    grad_qproj = norm_back(grad_qnorm * full_qgain, query_proj, query_root).astype(bf16)
    grad_kproj = norm_back(grad_knorm * full_kgain, key_proj, key_root).astype(bf16)
    grad_proj = jnp.concatenate(
        [grad_qproj.reshape(L, qd), grad_kproj.reshape(L, kd), grad_values.reshape(L, kd)], axis=1
    )
    term_qkv = t_times(normed_in, grad_proj).astype(bf16)
    partial_nin = times_t(grad_proj, full_qkv)
    term_pre = jnp.sum(partial_nin * scaled_in, axis=0)
    grad_nin = scatter_seq(lambda first, count: partial_nin[first : first + count])
    grad_tokens = grad_middle + norm_back(grad_nin * full_pre, local, root_in[:T])

    out_parts = term_out.reshape(qd, S, D // S).transpose(1, 0, 2)
    parts = [lax.dynamic_index_in_dim(out_parts, Q, 0, False)]
    for r in range(1, S):
        parts.append(swap(lax.dynamic_index_in_dim(out_parts, Q ^ r, 0, False), r))
    term_columns = order_seq(jnp.stack(parts)).reshape(D, D // S)
    term_gains = jnp.concatenate(
        [
            term_pre.reshape(N, rows_d),
            term_post.reshape(N, rows_d),
            term_qgain.reshape(N, -1),
            term_kgain.reshape(N, -1),
        ],
        axis=1,
    ).astype(bf16)
    term_packed = jnp.concatenate([term_qkv, term_columns], axis=1).reshape(N, rows_d, -1)
    gains_part = jnp.pad(
        term_gains[:, None, :], ((0, 0), (0, 15), (0, term_packed.shape[2] - term_gains.shape[1]))
    )
    shard_packed = lax.psum_scatter(
        jnp.concatenate([term_packed, gains_part], axis=1), "shard", scatter_dimension=0
    )

    down_all = order_seq(gather_seq(shard_down))
    grad_down = down_all.reshape(-1, D).astype(f32)
    both_all = order_seq(gather_seq(shard_both)).reshape(S, rows_d, 2, N, piece)
    both_all = both_all.transpose(2, 1, 3, 0, 4).reshape(2, rows_d, FF).astype(f32)
    packed_all = order_seq(gather_seq(shard_packed))
    gains_all = jnp.sum(packed_all[:, rows_d, :].astype(f32), axis=0)

    def columns(first, count):
        return (
            packed_all[:, :rows_d, first : first + count]
            .transpose(1, 0, 2)
            .reshape(rows_d, S * count)
            .astype(f32)
        )

    small = HEAD_SIZE // N
    return (
        output.astype(bf16)[None],
        grad_tokens[None],
        gains_all[:rows_d],
        columns(0, qd),
        columns(qd, kd),
        columns(qd + kd, kd),
        gains_all[2 * rows_d : 2 * rows_d + small],
        gains_all[2 * rows_d + small : 2 * rows_d + 2 * small],
        columns(width, D // S),
        gains_all[rows_d : 2 * rows_d],
        both_all[0],
        both_all[1],
        grad_down,
    )


def solution(mesh):
    row, vector, matrix = P("shard", "seq", None), P("shard"), P("shard", None)
    return jax.shard_map(
        per_device,
        mesh=mesh,
        in_specs=(
            row,
            matrix,
            vector,
            matrix,
            matrix,
            matrix,
            vector,
            vector,
            matrix,
            vector,
            matrix,
            matrix,
            matrix,
            row,
        ),
        out_specs=(
            row,
            row,
            vector,
            matrix,
            matrix,
            matrix,
            vector,
            vector,
            matrix,
            vector,
            matrix,
            matrix,
            matrix,
        ),
        check_vma=False,
    )
```

```python
import functools
import math

import jax
import jax.numpy as jnp
from jax import lax
from jax.experimental import pallas as pl
from jax.experimental.pallas import tpu as pltpu
from jax.sharding import PartitionSpec as P

QUERY_HEADS = 16
KEY_VALUE_HEADS = 8
HEAD_SIZE = 64
GROUP = QUERY_HEADS // KEY_VALUE_HEADS
LANES = 128
GAIN_ROWS = 16
SCALE = HEAD_SIZE ** (-0.5)
SCALE2 = SCALE * math.log2(math.e)


eps_norm = 1e-05
rope_base = 1000000.0

bf16 = jnp.bfloat16
f32 = jnp.float32
shape = jax.ShapeDtypeStruct


def dot(left, right):
    return jnp.dot(left, right, preferred_element_type=f32)


def times_t(left, right):
    return lax.dot_general(left, right, (((1,), (1,)), ((), ())), preferred_element_type=f32)


def t_times(left, right):
    return lax.dot_general(left, right, (((0,), (0,)), ((), ())), preferred_element_type=f32)


def inverse_root(value_tokens):
    return lax.rsqrt(jnp.mean(value_tokens * value_tokens, axis=-1, keepdims=True) + eps_norm)


def norm_back(grad_scaled, value_tokens, root):
    return root * (
        grad_scaled
        - value_tokens
        * (root * root)
        * jnp.mean(grad_scaled * value_tokens, axis=-1, keepdims=True)
    )


def rope_tables(places):
    half = HEAD_SIZE // 2
    lane = jnp.arange(LANES, dtype=jnp.int32) % HEAD_SIZE
    inverse = jnp.exp((lane % half).astype(f32) * (-2.0 * math.log(rope_base) / HEAD_SIZE))
    angle = places.astype(f32)[:, None] * inverse[None, :]
    sine = jnp.sin(angle)
    return (jnp.cos(angle), jnp.where(lane < half, -sine, sine))


def inside_of(starts, places):
    before = starts[None, :] <= places[:, None]
    return places - jnp.max(jnp.where(before, starts[None, :], 0), axis=1)


def ring_grid(N):
    Z = min(N, 4)
    return Z, N // Z


def ring_order(N):
    Z, X = ring_grid(N)
    order = [z * X for z in range(Z)]
    for row in range(Z):
        line = [(Z - 1 - row) * X + x for x in range(1, X)]
        order += line if row % 2 == 0 else line[::-1]
    return order


def ring_place(at, N):
    Z, X = ring_grid(N)
    if X == 1:
        return at
    if X == 2:
        return jnp.where(at < Z, at * 2, (2 * Z - 1 - at) * 2 + 1)
    row, column = lax.div(at - Z, X - 1), lax.rem(at - Z, X - 1)
    x = jnp.where(lax.rem(row, 2) == 0, 1 + column, X - 1 - column)
    return jnp.where(at < Z, at * X, (Z - 1 - row) * X + x)


def ring_position(s, N):
    Z, X = ring_grid(N)
    z, x = lax.div(s, X), lax.rem(s, X)
    if X == 1:
        return z
    if X == 2:
        return jnp.where(x == 0, z, 2 * Z - 1 - z)
    row = Z - 1 - z
    turn = jnp.where(lax.rem(row, 2) == 0, x - 1, X - 1 - x)
    return jnp.where(x == 0, z, Z + row * (X - 1) + turn)


def ring_owner(k, N):
    at = ring_position(lax.axis_index("shard"), N) + k % N
    return ring_place(jnp.where(at >= N, at - N, at), N)


def ring_slot(s, N):
    at = ring_position(jnp.int32(s), N) - ring_position(lax.axis_index("shard"), N)
    return jnp.where(at < 0, at + N, at)


def arrived(N, rows):
    half = rows // 32 * 16
    pieces = [(0, 0, rows)]
    for k in range(1, N // 2):
        pieces += [(N - k, 0, rows), (k, 0, rows)]
    return pieces + [(N // 2, 0, half), (N // 2, half, rows - half)]


def call(kernel, spaces, inputs, outputs, out_spaces, scratch, flops, name):
    places = {
        "s": pl.BlockSpec(memory_space=pltpu.SMEM),
        "v": pl.BlockSpec(memory_space=pltpu.VMEM),
        "a": pl.BlockSpec(memory_space=pl.ANY),
    }
    size = sum(math.prod(x.shape) * x.dtype.itemsize for x in list(inputs) + list(outputs))
    return list(pl.pallas_call(
        kernel,
        out_shape=list(outputs),
        in_specs=[places[c] for c in spaces],
        out_specs=[places[c] for c in out_spaces],
        scratch_shapes=scratch,
        compiler_params=pltpu.CompilerParams(vmem_limit_bytes=56 * 2**20),
        cost_estimate=pl.CostEstimate(flops=1, bytes_accessed=1, transcendentals=0),
        name=name,
    )(*inputs))


def aligned(start, unit):
    return pl.multiple_of(start, unit)


def column_block(ref, index, width):
    if width % LANES == 0:
        return ref[:, pl.ds(aligned(index * width, LANES), width)]
    tile = ref[:, pl.ds(aligned(lax.div(index * width, LANES) * LANES, LANES), LANES)].astype(f32)
    moved = pltpu.roll(tile, LANES - lax.rem(index * width, LANES), 1)
    return moved[:, :width].astype(bf16)


def pack_kernel(qd, kd, od, wq, wk, wv, wo, pre, post, qgain, kgain, out, rows):
    Q = lax.axis_index("seq")
    d = wq.shape[0]
    at = 0
    for ref, width in ((wq, qd), (wk, kd), (wv, kd), (wo, od)):
        out[:d, at : at + width] = column_block(ref, Q, width)
        at += width
    rows[...] = jnp.zeros_like(rows)
    for i, ref in enumerate((pre, post, qgain, kgain)):
        rows[i : i + 1, : ref.shape[1]] = ref[...].astype(f32)
    out[d:, :LANES] = rows[...].astype(bf16)
    out[d:, LANES:] = jnp.zeros((GAIN_ROWS, at - LANES), bf16)


def columns_kernel(S, N, piece, gate, up, out):
    Q = lax.axis_index("seq")
    for q in range(S):

        @pl.when(Q == q)
        def _():
            for base, ref in ((0, gate), (N * piece, up)):
                for s in range(N):
                    out[:, base + s * piece : base + (s + 1) * piece] = ref[
                        :, (s * S + q) * piece : (s * S + q + 1) * piece
                    ]


def assemble_kernel(N, d, width, qd, od, *refs):
    pieces = arrived(N, d + GAIN_ROWS)
    chunks, (w, outs, gains) = refs[: len(pieces)], refs[len(pieces) :]
    Q = lax.axis_index("seq")
    gains[...] = jnp.zeros_like(gains)
    lane = lax.broadcasted_iota(jnp.int32, (GAIN_ROWS, LANES), 1)
    for ref, (k, first, rows) in zip(chunks, pieces):
        s = ring_owner(k, N)
        count = min(d - first, rows)
        to = s * d + first
        w[pl.ds(aligned(to, 16), count)] = ref[:count, :width]
        r = jnp.bitwise_xor(lax.div(to, qd), Q)
        outs[r, pl.ds(aligned(lax.rem(to, qd), 16), count)] = ref[:count, width : width + od]
        if first + rows > d:
            tile = ref[count:, :LANES].astype(f32)
            for row, many in ((0, d), (1, d), (2, HEAD_SIZE // N), (3, HEAD_SIZE // N)):
                at = s * many
                moved = pltpu.roll(jnp.where(lane < many, tile, 0.0), lax.rem(at, LANES), 1)
                where = pl.ds(aligned(lax.div(at, LANES) * LANES, LANES), LANES)
                gains[row : row + 1, where] += moved[row : row + 1]
    for row in (2, 3):
        x = gains[row : row + 1, :LANES]
        gains[row : row + 1, :LANES] = x + pltpu.roll(x, HEAD_SIZE, 1)


def group_ones():
    across = lax.broadcasted_iota(jnp.int32, (LANES, LANES), 0) // HEAD_SIZE
    down = lax.broadcasted_iota(jnp.int32, (LANES, LANES), 1) // HEAD_SIZE
    return jnp.where(across == down, 1.0 / HEAD_SIZE, 0.0).astype(bf16)


def split_dot(x, ones):
    high = x.astype(bf16)
    return dot(high, ones) + dot((x - high.astype(f32)).astype(bf16), ones)


def turned(x, low_half):
    half = HEAD_SIZE // 2
    return jnp.where(low_half, pltpu.roll(x, LANES - half, 1), pltpu.roll(x, half, 1))


def begins(starts, places):
    begin = jnp.zeros_like(places)
    for start in starts:
        begin = jnp.maximum(begin, jnp.where(places >= start, start, 0))
    return begin


def spread(x, half, low):
    moved = pltpu.roll(x, HEAD_SIZE, 1)
    return jnp.where(low, moved, x) if half else jnp.where(low, x, moved)


def head_tile(ref, at, low):
    first = at // LANES * LANES
    return spread(ref[:, first : first + LANES], at % LANES // HEAD_SIZE, low)


def forward_kernel(S, qd, kd, starts_ref, *refs):
    xs = refs[:S]
    (w_ref, gains_ref, cos_ref, sin_ref) = refs[S : S + 4]
    (nin_ref, proj_ref, rot_ref, att_ref, stat_ref, wide_ref, both_ref) = refs[S + 4 :]
    T = xs[0].shape[0]
    L = S * T
    heads = kd // HEAD_SIZE
    Q = lax.axis_index("seq")
    starts = [starts_ref[i] for i in range(starts_ref.shape[0])]
    ones = group_ones()
    lane = lax.broadcasted_iota(jnp.int32, (T, LANES), 1)
    low = lane < HEAD_SIZE
    low_half = lane % HEAD_SIZE < HEAD_SIZE // 2
    for r in range(S):
        rows = slice(r * T, (r + 1) * T)
        at = pl.ds(aligned(jnp.bitwise_xor(Q, r) * T, T), T)
        x = xs[r][...].astype(f32)
        nin = (x * inverse_root(x) * gains_ref[0:1]).astype(bf16)
        nin_ref[rows] = nin
        proj = dot(nin, w_ref[...])
        cos, sin = cos_ref[rows], sin_ref[rows]
        for first in range(0, qd + 2 * kd, LANES):
            cols = slice(first, first + LANES)
            tile = proj[:, cols]
            if first < qd + kd:
                proj_ref[at, cols] = tile
                gain = gains_ref[2:3, :LANES] if first < qd else gains_ref[3:4, :LANES]
                y = tile * lax.rsqrt(split_dot(tile * tile, ones) + eps_norm) * gain
                y = y * cos + turned(y, low_half) * sin
                if first + LANES > qd + kd:
                    y = jnp.where(low, y, tile)
                tile = y
            rot_ref[at, cols] = tile.astype(bf16)
    low_all = lax.broadcasted_iota(jnp.int32, (L, LANES), 1) < HEAD_SIZE
    for n in range(heads):
        wide_ref[...] = head_tile(rot_ref, qd + n * HEAD_SIZE, low_all)
        both_ref[:, :LANES] = head_tile(rot_ref, qd + kd + n * HEAD_SIZE, low_all)
        both_ref[:, LANES:] = jnp.ones((L, LANES), bf16)
        cols = slice(n * LANES, (n + 1) * LANES)
        for i in range(S):
            count = (i + 1) * T
            q = rot_ref[i * T : count, cols]
            zero = jnp.zeros_like(q)
            q2 = jnp.concatenate([jnp.where(low, q, zero), jnp.where(low, zero, q)], axis=0)
            s = times_t(q2, wide_ref[:count])
            qpos = i * T + lax.broadcasted_iota(jnp.int32, (T, 1), 0)
            qpos = jnp.concatenate([qpos, qpos], axis=0)
            kpos = lax.broadcasted_iota(jnp.int32, (2 * T, count), 1)
            ok = (kpos >= begins(starts, qpos)) & (kpos <= qpos)
            e = jnp.where(ok, jnp.exp2(s * SCALE2), 0.0).astype(bf16)
            o = dot(e, both_ref[:count])
            total = o[:, LANES:]
            out = o[:, :LANES] / total
            att_ref[pl.ds(aligned(jnp.bitwise_xor(Q, i) * T, T), T), cols] = jnp.where(
                low, out[:T], out[T:]
            ).astype(bf16)
            logs = jnp.log2(total)
            for a in range(GROUP):
                stat_ref[n * GROUP + a : n * GROUP + a + 1, i * T : count] = (
                    logs[a * T : (a + 1) * T].T[:1]
                )


def out_kernel(S, blocks, whole, att_ref, *refs):
    weights, outs = refs[:S], refs[S:]
    T = outs[0].shape[0]
    od = weights[0].shape[1]
    Q = lax.axis_index("seq")
    for j, r in enumerate(blocks):
        a = att_ref[r * T : (r + 1) * T]
        for c in range(S):
            cols = pl.ds(aligned(jnp.bitwise_xor(Q, c) * od, LANES), od)
            outs[j][:, cols] = dot(a, weights[c][...]).astype(outs[j].dtype)
    if whole:
        for c in range(S):
            cols = pl.ds(aligned(jnp.bitwise_xor(Q, c) * od, LANES), od)
            outs[-1][:, cols] = weights[c][...]


def backward_kernel(S, qd, kd, starts_ref, *refs):
    gbs = refs[:S]
    (wo_ref, rot_ref, proj_ref, att_ref, stat_ref, gains_ref, cos_ref, sin_ref) = refs[S : S + 8]
    (grad_ref, sums_ref, do_ref, delta_ref, k_ref, kt_ref, v_ref, dk_ref, dv_ref) = refs[S + 8 :]
    T = gbs[0].shape[0]
    L = S * T
    heads = kd // HEAD_SIZE
    Q = lax.axis_index("seq")
    starts = [starts_ref[i] for i in range(starts_ref.shape[0])]
    ones = group_ones()
    lane = lax.broadcasted_iota(jnp.int32, (T, LANES), 1)
    low = lane < HEAD_SIZE
    low_half = lane % HEAD_SIZE < HEAD_SIZE // 2
    picks = (
        lax.broadcasted_iota(jnp.int32, (8, LANES), 0)
        == lax.broadcasted_iota(jnp.int32, (8, LANES), 1) // HEAD_SIZE
    ).astype(bf16)
    sums_ref[...] = jnp.zeros_like(sums_ref)
    for r in range(S):
        rows = slice(r * T, (r + 1) * T)
        at = pl.ds(aligned(jnp.bitwise_xor(Q, r) * T, T), T)
        grads = times_t(gbs[r][...], wo_ref[...]).astype(bf16)
        do_ref[at] = grads
        for n in range(heads):
            cols = slice(n * LANES, (n + 1) * LANES)
            x = grads[:, cols].astype(f32) * att_ref[rows, cols].astype(f32)
            high = x.astype(bf16)
            rest = (x - high.astype(f32)).astype(bf16)
            delta_ref[n * 8 : n * 8 + 8, at] = times_t(picks, high) + times_t(picks, rest)

    def finish(g, rows, at, cols, gain):
        g = g * cos_ref[rows] - turned(g, low_half) * sin_ref[rows]
        tile = proj_ref[at, cols]
        inverse = lax.rsqrt(split_dot(tile * tile, ones) + eps_norm)
        unit = tile * inverse
        f = g * gain
        return g * unit, inverse * (f - unit * split_dot(f * unit, ones))

    low_all = lax.broadcasted_iota(jnp.int32, (L, LANES), 1) < HEAD_SIZE
    row_low = lax.broadcasted_iota(jnp.int32, (LANES, T), 0) < HEAD_SIZE
    for n in range(heads):
        k = head_tile(rot_ref, qd + n * HEAD_SIZE, low_all)
        k_ref[...] = k
        kt_ref[...] = k.T
        v_ref[...] = head_tile(rot_ref, qd + kd + n * HEAD_SIZE, low_all)
        dk_ref[n] = jnp.zeros((L, LANES), f32)
        dv_ref[n] = jnp.zeros((L, LANES), f32)
        cols = slice(n * LANES, (n + 1) * LANES)
        for i in range(S):
            count = (i + 1) * T
            here = slice(i * T, count)
            q = rot_ref[here, cols]
            do = do_ref[here, cols]
            zero = jnp.zeros_like(q)
            q2 = jnp.concatenate([jnp.where(low, q, zero), jnp.where(low, zero, q)], axis=0)
            do2 = jnp.concatenate([jnp.where(low, do, zero), jnp.where(low, zero, do)], axis=0)
            logs = jnp.concatenate(
                [stat_ref[n * GROUP + a : n * GROUP + a + 1, here] for a in range(GROUP)], axis=1
            )
            delta = jnp.concatenate(
                [delta_ref[n * 8 + a : n * 8 + a + 1, here] for a in range(GROUP)], axis=1
            )
            s = times_t(k_ref[:count], q2)
            dp = times_t(v_ref[:count], do2)
            qpos = i * T + lax.broadcasted_iota(jnp.int32, (1, T), 1)
            qpos = jnp.concatenate([qpos, qpos], axis=1)
            kpos = lax.broadcasted_iota(jnp.int32, (count, 2 * T), 0)
            ok = (kpos >= begins(starts, qpos)) & (kpos <= qpos)
            p = jnp.where(ok, jnp.exp2(s * SCALE2 - logs), 0.0)
            ds = (p * (dp - delta)).astype(bf16)
            dv_ref[n, :count] += dot(p.astype(bf16), do2)
            dk_ref[n, :count] += dot(ds, q2)
            dqt = dot(kt_ref[:, :count], ds)
            dq = jnp.where(row_low, dqt[:, :T], dqt[:, T:]).T * SCALE
            rows = pl.ds(aligned(jnp.bitwise_xor(Q, i) * T, T), T)
            total, grad = finish(dq, rows, here, cols, gains_ref[2:3, :LANES])
            sums_ref[0:1] += jnp.sum(total, axis=0, keepdims=True)
            grad_ref[rows, cols] = grad.astype(bf16)

    def folded(ref, n, rows):
        x = ref[n, rows]
        return x + pltpu.roll(x, HEAD_SIZE, 1)

    for first in range(qd, qd + 2 * kd, LANES):
        cols = slice(first, first + LANES)
        for i in range(S):
            here = slice(i * T, (i + 1) * T)
            sides = []
            for part in (first, first + HEAD_SIZE):
                is_key = part < qd + kd
                n = (part - qd if is_key else part - qd - kd) // HEAD_SIZE
                sides.append(folded(dk_ref if is_key else dv_ref, n, here))
            g = jnp.where(low, sides[0], sides[1])
            rows = pl.ds(aligned(jnp.bitwise_xor(Q, i) * T, T), T)
            if first < qd + kd:
                total, grad = finish(g * SCALE, rows, here, cols, gains_ref[3:4, :LANES])
                if first + LANES > qd + kd:
                    total = jnp.where(low, total, 0.0)
                    grad = jnp.where(low, grad, g)
                sums_ref[1:2] += jnp.sum(total, axis=0, keepdims=True)
                g = grad
            grad_ref[rows, cols] = g.astype(bf16)


def input_grad_kernel(blocks, grad_ref, w_ref, *refs):
    many = len(blocks)
    xs, outs, total = refs[:many], refs[many : 2 * many], refs[2 * many]
    T = xs[0].shape[0]
    total[...] = jnp.zeros_like(total)
    for j, r in enumerate(blocks):
        g = times_t(grad_ref[r * T : (r + 1) * T], w_ref[...])
        outs[j][...] = g.astype(outs[j].dtype)
        x = xs[j][...].astype(f32)
        total[0:1] += jnp.sum(g * (x * inverse_root(x)), axis=0, keepdims=True)


def out_grad_kernel(S, att_ref, *refs):
    gbs, (out, total) = refs[:S], refs[S:]
    T = gbs[0].shape[0]
    od = out.shape[2]
    Q = lax.axis_index("seq")
    acc = t_times(att_ref[:T], gbs[0][...])
    for r in range(1, S):
        acc += t_times(att_ref[r * T : (r + 1) * T], gbs[r][...])
    total[...] = acc
    for r in range(S):
        cols = pl.ds(aligned(jnp.bitwise_xor(Q, r) * od, LANES), od)
        out[r] = total[:, cols].astype(bf16)


def pack_grad_kernel(S, N, nin_ref, grad_ref, sums_ref, pre_refs, post_ref, *refs):
    parts, (out, full, rows) = refs[:S], refs[S:]
    D = nin_ref.shape[1]
    d = D // N
    width = grad_ref.shape[1]
    qd, od = parts[0].shape
    small = HEAD_SIZE // N
    Q = lax.axis_index("seq")
    for r in range(S):
        full[pl.ds(aligned(jnp.bitwise_xor(Q, r) * qd, qd), qd)] = parts[r][...]
    term = t_times(nin_ref[...], grad_ref[...]).astype(bf16)
    pre = pre_refs[0:1] + pre_refs[8:9]
    sums = sums_ref[...] + pltpu.roll(sums_ref[...], HEAD_SIZE, 1)
    rows[...] = jnp.zeros_like(rows)
    for s in range(N):
        k = ring_slot(s, N)
        at = slice(s * d, (s + 1) * d)
        out[k, :d, :width] = term[at]
        out[k, :d, width:] = full[at]
        rows[0:1, :d] = pre[:, at]
        rows[1:2, :d] = post_ref[:, at]
        rows[2:4, :small] = sums[0:2, s * small : (s + 1) * small]
        out[k, d:, :LANES] = rows[...].astype(bf16)
        out[k, d:, LANES:] = jnp.zeros((GAIN_ROWS, width + od - LANES), bf16)


def feed_kernel(N, many, *refs):
    mids, cots = refs[:many], refs[many : 2 * many]
    refs = refs[2 * many :]
    w, sems = refs[-2:]
    D = mids[0].shape[1]
    d = D // N
    pieces = arrived(N, d)
    chunks, refs = refs[: len(pieces)], refs[len(pieces) :]
    down, hidden, both, outs = refs[0], refs[1], refs[2], refs[3 : 3 + many]
    T = mids[0].shape[0]
    FQ = down.shape[0]
    copies = []
    for i, (ref, (k, first, rows)) in enumerate(zip(chunks, pieces)):
        at = aligned(ring_owner(k, N) * d + first, 16)
        copies.append(pltpu.make_async_copy(ref, w.at[pl.ds(at, rows)], sems.at[i]))
        copies[-1].start()
    for c in copies:
        c.wait()
    step = FQ // 3
    for j in range(many):
        rows = slice(j * T, (j + 1) * T)
        x = mids[j][...]
        c = cots[j][...]
        for first in range(0, FQ, step):
            cols = slice(first, first + step)
            gate = dot(x, w[:, cols])
            upper = dot(x, w[:, FQ + first : FQ + first + step])
            grad = times_t(c, down[cols])
            sigmoid = 1.0 / (1.0 + jnp.exp(-gate))
            swish = gate * sigmoid
            hidden[rows, cols] = (swish * upper).astype(bf16)
            both[rows, cols] = (
                grad * upper * (sigmoid * (1.0 + gate * (1.0 - sigmoid)))
            ).astype(bf16)
            both[rows, FQ + first : FQ + first + step] = (grad * swish).astype(bf16)
        outs[j][...] = times_t(both[rows], w[...]).astype(outs[j].dtype)


def both_grad_kernel(S, N, slots, *refs):
    mids, (near, far, out), scratch = refs[:S], refs[S : S + 3], refs[S + 3 :]
    T, D = mids[0].shape
    d = D // N
    half = S // 2 * T
    width = near.shape[1]
    left = scratch[0]
    for r in range(S):
        rows = slice(r * T, (r + 1) * T)
        x = None if d % LANES == 0 else mids[r][...].astype(f32)
        for j, k in enumerate(slots):
            s = ring_owner(k, N)
            if x is None:
                part = mids[r][:, pl.ds(aligned(s * d, LANES), d)]
            else:
                moved = pltpu.roll(x, jnp.where(s == 0, 0, D - s * d), 1)
                part = moved[:, :d].astype(bf16)
            left[rows, j * d : (j + 1) * d] = part
    step = width // 3
    for first in range(0, width, step):
        cols = slice(first, first + step)
        g = t_times(left[:half], near[:, cols]) + t_times(left[half:], far[:, cols])
        for j in range(len(slots)):
            out[j, :, cols] = g[j * d : (j + 1) * d].astype(bf16)


def load_blocks(blocks, held, sems):
    Q = lax.axis_index("seq")
    copies = []
    for r, ref in enumerate(blocks):
        copies.append(
            pltpu.make_async_copy(ref, held.at[jnp.bitwise_xor(Q, r)], sems.at[r])
        )
        copies[-1].start()
    for c in copies:
        c.wait()


def both_out_kernel(S, N, *refs):
    blocks, (gate, up, held, sems) = refs[:S], refs[S:]
    load_blocks(blocks, held, sems)
    piece = gate.shape[1] // N // S
    for q in range(S):
        for base, out in ((0, gate), (N * piece, up)):
            for s in range(N):
                out[:, (s * S + q) * piece : (s * S + q + 1) * piece] = held[
                    q, :, base + s * piece : base + (s + 1) * piece
                ].astype(f32)


def down_out_kernel(S, *refs):
    blocks, (out, held, sems) = refs[:S], refs[S:]
    load_blocks(blocks, held, sems)
    piece = held.shape[1]
    for q in range(S):
        out[q * piece : (q + 1) * piece] = held[q].astype(f32)


def pack_out_kernel(S, N, qd, kd, *refs):
    blocks, refs = refs[:S], refs[S:]
    outs, (pre, post, qgain, kgain, held, sems) = refs[:4], refs[4:]
    load_blocks(blocks, held, sems)
    d = outs[0].shape[0]
    od = outs[3].shape[1] // S
    at = 0
    for out, width in zip(outs, (qd, kd, kd, od)):
        for q in range(S):
            out[:, q * width : (q + 1) * width] = held[q, :d, at : at + width].astype(f32)
        at += width
    rows = held[0, d:, :LANES].astype(f32)
    for q in range(1, S):
        rows += held[q, d:, :LANES].astype(f32)
    for i, ref in enumerate((pre, post, qgain, kgain)):
        ref[...] = rows[i : i + 1, : ref.shape[1]]


def per_device(
    tokens,
    doc_starts,
    pre_gain,
    query_weight,
    key_matrix,
    value_matrix,
    query_gain,
    key_gain,
    out_weight,
    post_gain,
    gate_weight,
    up_weight,
    down_weight,
    cotangent,
):
    S = lax.axis_size("seq")
    N = lax.axis_size("shard")
    Q = lax.axis_index("seq")
    T, D = tokens.shape[1:]
    L = S * T
    d = D // N
    od = D // S
    qd = QUERY_HEADS * HEAD_SIZE // S
    kd = KEY_VALUE_HEADS * HEAD_SIZE // S
    width = qd + 2 * kd
    heads = kd // HEAD_SIZE
    FF = gate_weight.shape[1]
    piece = FF // N // S
    FQ = FF // S
    near, far = list(range(S // 2)), list(range(S // 2, S))
    dma = pltpu.SemaphoreType.DMA


    def swap(x, step):
        return lax.ppermute(x, "seq", [(i, i ^ step) for i in range(S)])

    def gather_seq(x):
        blocks = {0: x}
        step = S // 2
        while step:
            for r in list(blocks):
                blocks[r + step] = swap(blocks[r], step)
            step //= 2
        return [blocks[r] for r in range(S)]

    def scatter_seq(blocks):
        def reduce(low, size):
            if size == 2:
                return blocks[low] + swap(blocks[low + 1], 1).astype(f32)
            half = size // 2
            moved = swap(reduce(low + half, half).astype(bf16), half)
            return reduce(low, half) + moved.astype(f32)

        return reduce(0, S)

    def block_shapes(blocks):
        return [shape((T, D), bf16 if r % 2 else f32) for r in blocks]

    order = ring_order(N)

    def hop(x, way):
        return lax.ppermute(x, "shard", [(order[i], order[(i + way) % N]) for i in range(N)])

    def ring_gather(x):
        half = x.shape[0] // 32 * 16
        up = down = x
        chunks = [x]
        for k in range(1, N // 2):
            up, down = lax.optimization_barrier((hop(up, 1), hop(down, -1)))
            chunks += [up, down]
        return chunks + [hop(up[:half], 1), hop(down[half:], -1)]

    def ring_scatter(x):
        half = x[0].shape[0] // 32 * 16
        mid = x[N // 2]
        up, down = lax.optimization_barrier((hop(mid[:half], 1), hop(mid[half:], -1)))
        for k in range(N // 2 - 1, 0, -1):
            ahead, behind = x[k].astype(f32), x[N - k].astype(f32)
            if k == N // 2 - 1:
                ahead = jnp.concatenate([ahead[:half] + up.astype(f32), ahead[half:]], axis=0)
                behind = jnp.concatenate([behind[:half], behind[half:] + down.astype(f32)], axis=0)
            else:
                ahead, behind = ahead + up.astype(f32), behind + down.astype(f32)
            up, down = lax.optimization_barrier(
                (hop(ahead.astype(bf16), 1), hop(behind.astype(bf16), -1))
            )
        return (x[0].astype(f32) + up.astype(f32) + down.astype(f32)).astype(bf16)

    (pack,) = call(
        functools.partial(pack_kernel, qd, kd, od),
        "v" * 8,
        (
            query_weight,
            key_matrix,
            value_matrix,
            out_weight,
            pre_gain[None],
            post_gain[None],
            query_gain[None],
            key_gain[None],
        ),
        [shape((d + GAIN_ROWS, width + od), bf16)],
        "v",
        [pltpu.VMEM((GAIN_ROWS, LANES), f32)],
        0,
        "pack",
    )
    pack_chunks = ring_gather(pack)
    local = tokens[0]
    xs = gather_seq(local)

    starts = doc_starts[0]
    blocks_at = jnp.arange(S, dtype=jnp.int32) ^ Q
    places = (blocks_at[:, None] * T + jnp.arange(T, dtype=jnp.int32)[None, :]).reshape(L)
    cosine, sine = rope_tables(inside_of(starts, places))

    (both_columns,) = call(
        functools.partial(columns_kernel, S, N, piece),
        "vv",
        (gate_weight, up_weight),
        [shape((d, 2 * FQ), bf16)],
        "v",
        [],
        0,
        "columns",
    )
    own_rows = lax.dynamic_slice(
        down_weight, (Q * piece, 0), (piece, D), allow_negative_indices=False
    )
    cot = cotangent[0]
    both_columns, own_rows, cot_first, _ = lax.optimization_barrier(
        (both_columns, own_rows, cot, pack_chunks[-3])
    )
    both_chunks = ring_gather(both_columns)
    full_down = lax.all_gather(own_rows, "shard", axis=0, tiled=True)
    cots = gather_seq(cot_first)

    w_qkv, out_parts, gains = call(
        functools.partial(assemble_kernel, N, d, width, qd, od),
        "v" * len(pack_chunks),
        pack_chunks,
        [shape((D, width), bf16), shape((S, qd, od), bf16), shape((8, D), f32)],
        "vvv",
        [],
        0,
        "assemble",
    )
    out_blocks = [out_parts[0]] + [swap(out_parts[r], r) for r in range(1, S)]

    normed_in, proj, rotated, attended, stats = call(
        functools.partial(forward_kernel, S, qd, kd),
        "s" + "v" * (S + 4),
        (starts, *xs, w_qkv, gains, cosine, sine),
        [
            shape((L, D), bf16),
            shape((L, -(-(qd + kd) // LANES) * LANES), f32),
            shape((L, width), bf16),
            shape((L, qd), bf16),
            shape((max(8, qd // HEAD_SIZE), L), f32),
        ],
        "v" * 5,
        [pltpu.VMEM((L, LANES), bf16), pltpu.VMEM((L, 2 * LANES), bf16)],
        2 * L * D * width + 2 * L * L * qd,
        "attend",
    )

    def project(blocks, whole):
        return call(
            functools.partial(out_kernel, S, blocks, whole),
            "v" * (S + 1),
            (attended, *out_blocks),
            block_shapes(blocks) + ([shape((qd, D), bf16)] if whole else []),
            "v" * (len(blocks) + whole),
            [],
            2 * len(blocks) * T * qd * D,
            "project",
        )

    far_blocks = project(far, False)
    *near_blocks, full_out = project(near, True)
    middle = local.astype(f32) + scatter_seq(near_blocks + far_blocks)

    full_post = gains[1]
    root_mid = inverse_root(middle)
    scaled_mid = middle * root_mid
    mids = gather_seq((scaled_mid * full_post).astype(bf16))

    def feed(blocks):
        return call(
            functools.partial(feed_kernel, N, len(blocks)),
            "v" * (2 * len(blocks)) + "a" * len(both_chunks) + "v",
            (*[mids[r] for r in blocks], *[cots[r] for r in blocks], *both_chunks, full_down),
            [shape((len(blocks) * T, FQ), bf16), shape((len(blocks) * T, 2 * FQ), bf16)]
            + block_shapes(blocks),
            "v" * (2 + len(blocks)),
            [pltpu.VMEM((D, 2 * FQ), bf16), dma((len(both_chunks),))],
            10 * len(blocks) * T * D * FQ,
            "feed",
        )

    hidden_far, both_far, *grads_far = feed(far)
    hidden_near, both_near, *grads_near = feed(near)
    grad_nmid = scatter_seq(grads_near + grads_far)
    all_cot = jnp.concatenate(cots, axis=0)
    term_down = t_times(jnp.concatenate([hidden_near, hidden_far], axis=0), all_cot)
    shard_down = lax.psum_scatter(
        term_down.astype(bf16), "shard", scatter_dimension=0, tiled=True
    )
    term_both = {}

    def both_grads(slots):
        (terms,) = call(
            functools.partial(both_grad_kernel, S, N, slots),
            "v" * (S + 2),
            (*mids, both_near, both_far),
            [shape((len(slots), d, 2 * FQ), bf16)],
            "v",
            [pltpu.VMEM((L, len(slots) * d), bf16)],
            4 * L * len(slots) * d * FQ,
            "both_grad",
        )
        for j, k in enumerate(slots):
            term_both[k] = terms[j]

    middle_slots = [N // 2, N // 2 - 1, N // 2 + 1]
    both_grads(middle_slots)
    both_grads([k for k in range(N) if k not in middle_slots])
    shard_both = ring_scatter(term_both)
    output_blocks = []
    for hidden, blocks in ((hidden_near, near), (hidden_far, far)):
        product = dot(hidden, full_down)
        for j, r in enumerate(blocks):
            block = product[j * T : (j + 1) * T]
            output_blocks.append(block.astype(bf16) if r % 2 else block)
    output = middle + scatter_seq(output_blocks)
    term_post = jnp.sum(grad_nmid * scaled_mid, axis=0)
    grad_middle = cot.astype(f32) + norm_back(grad_nmid * full_post, middle, root_mid)

    gbs = gather_seq(grad_middle.astype(bf16))
    grad_proj, sums = call(
        functools.partial(backward_kernel, S, qd, kd),
        "s" + "v" * (S + 8),
        (starts, *gbs, full_out, rotated, proj, attended, stats, gains, cosine, sine),
        [shape((L, width), bf16), shape((8, LANES), f32)],
        "vv",
        [
            pltpu.VMEM((L, qd), bf16),
            pltpu.VMEM((8 * heads, L), f32),
            pltpu.VMEM((L, LANES), bf16),
            pltpu.VMEM((LANES, L), bf16),
            pltpu.VMEM((L, LANES), bf16),
            pltpu.VMEM((heads, L, LANES), f32),
            pltpu.VMEM((heads, L, LANES), f32),
        ],
        2 * L * D * qd + 5 * L * L * qd,
        "attend_back",
    )

    def input_grads(blocks):
        return call(
            functools.partial(input_grad_kernel, blocks),
            "v" * (2 + len(blocks)),
            (grad_proj, w_qkv, *[xs[r] for r in blocks]),
            block_shapes(blocks) + [shape((8, D), f32)],
            "v" * (len(blocks) + 1),
            [],
            2 * len(blocks) * T * D * width,
            "input_grad",
        )

    *nins_far, pre_far = input_grads(far)
    *nins_near, pre_near = input_grads(near)
    grad_nin = scatter_seq(nins_near + nins_far)
    wide = local.astype(f32)
    grad_tokens = grad_middle + norm_back(grad_nin * gains[0], wide, inverse_root(wide))

    (out_terms,) = call(
        functools.partial(out_grad_kernel, S),
        "v" * (S + 1),
        (attended, *gbs),
        [shape((S, qd, od), bf16)],
        "v",
        [pltpu.VMEM((qd, D), f32)],
        2 * L * qd * D,
        "out_grad",
    )
    out_terms = [out_terms[0]] + [swap(out_terms[r], r) for r in range(1, S)]
    (pack_terms,) = call(
        functools.partial(pack_grad_kernel, S, N),
        "v" * (5 + S),
        (
            normed_in,
            grad_proj,
            sums,
            jnp.concatenate([pre_near, pre_far], axis=0),
            term_post[None],
            *out_terms,
        ),
        [shape((N, d + GAIN_ROWS, width + od), bf16)],
        "v",
        [pltpu.VMEM((D, od), bf16), pltpu.VMEM((GAIN_ROWS, LANES), f32)],
        2 * L * D * width,
        "pack_grad",
    )
    shard_pack = ring_scatter(pack_terms)

    gate_grad, up_grad = call(
        functools.partial(both_out_kernel, S, N),
        "a" * S,
        gather_seq(shard_both),
        [shape((d, FF), f32), shape((d, FF), f32)],
        "vv",
        [pltpu.VMEM((S, d, 2 * FQ), bf16), dma((S,))],
        0,
        "both_out",
    )
    (down_grad,) = call(
        functools.partial(down_out_kernel, S),
        "a" * S,
        gather_seq(shard_down),
        [shape((S * piece, D), f32)],
        "v",
        [pltpu.VMEM((S, piece, D), bf16), dma((S,))],
        0,
        "down_out",
    )
    small = HEAD_SIZE // N
    q_grad, k_grad, v_grad, o_grad, pre_grad, post_grad, qgain_grad, kgain_grad = call(
        functools.partial(pack_out_kernel, S, N, qd, kd),
        "a" * S,
        gather_seq(shard_pack),
        [
            shape((d, S * qd), f32),
            shape((d, S * kd), f32),
            shape((d, S * kd), f32),
            shape((d, D), f32),
            shape((1, d), f32),
            shape((1, d), f32),
            shape((1, small), f32),
            shape((1, small), f32),
        ],
        "v" * 8,
        [pltpu.VMEM((S, d + GAIN_ROWS, width + od), bf16), dma((S,))],
        0,
        "pack_out",
    )
    return (
        output.astype(bf16)[None],
        grad_tokens[None],
        pre_grad[0],
        q_grad,
        k_grad,
        v_grad,
        qgain_grad[0],
        kgain_grad[0],
        o_grad,
        post_grad[0],
        gate_grad,
        up_grad,
        down_grad,
    )


def solution(mesh):
    row, vector, matrix = P("shard", "seq", None), P("shard"), P("shard", None)
    return jax.shard_map(
        per_device,
        mesh=mesh,
        in_specs=(
            row,
            matrix,
            vector,
            matrix,
            matrix,
            matrix,
            vector,
            vector,
            matrix,
            vector,
            matrix,
            matrix,
            matrix,
            row,
        ),
        out_specs=(
            row,
            row,
            vector,
            matrix,
            matrix,
            matrix,
            vector,
            vector,
            matrix,
            vector,
            matrix,
            matrix,
            matrix,
        ),
        check_vma=False,
    )
```

```python
import functools
import math

import jax
import jax.numpy as jnp
from jax import lax
from jax.experimental import pallas as pl
from jax.experimental.pallas import tpu as pltpu
from jax.sharding import PartitionSpec as P

QUERY_HEADS = 16
KEY_VALUE_HEADS = 8
HEAD_SIZE = 64
GROUP = QUERY_HEADS // KEY_VALUE_HEADS
LANES = 128
GAIN_ROWS = 16
SCALE = HEAD_SIZE ** (-0.5)
SCALE2 = SCALE * math.log2(math.e)


eps_norm = 1e-05
rope_base = 1000000.0

bf16 = jnp.bfloat16
f32 = jnp.float32
shape = jax.ShapeDtypeStruct


def dot(left, right):
    return jnp.dot(left, right, preferred_element_type=f32)


def times_t(left, right):
    return lax.dot_general(left, right, (((1,), (1,)), ((), ())), preferred_element_type=f32)


def t_times(left, right):
    return lax.dot_general(left, right, (((0,), (0,)), ((), ())), preferred_element_type=f32)


def inverse_root(value_tokens):
    return lax.rsqrt(jnp.mean(value_tokens * value_tokens, axis=-1, keepdims=True) + eps_norm)


def norm_back(grad_scaled, value_tokens, root):
    return root * (
        grad_scaled
        - value_tokens
        * (root * root)
        * jnp.mean(grad_scaled * value_tokens, axis=-1, keepdims=True)
    )


def rope_tables(places):
    half = HEAD_SIZE // 2
    lane = jnp.arange(LANES, dtype=jnp.int32) % HEAD_SIZE
    inverse = jnp.exp((lane % half).astype(f32) * (-2.0 * math.log(rope_base) / HEAD_SIZE))
    angle = places.astype(f32)[:, None] * inverse[None, :]
    sine = jnp.sin(angle)
    return (jnp.cos(angle), jnp.where(lane < half, -sine, sine))


def inside_of(starts, places):
    before = starts[None, :] <= places[:, None]
    return places - jnp.max(jnp.where(before, starts[None, :], 0), axis=1)


def ring_grid(N):
    Z = min(N, 4)
    return Z, N // Z


def ring_order(N):
    Z, X = ring_grid(N)
    order = [z * X for z in range(Z)]
    for row in range(Z):
        line = [(Z - 1 - row) * X + x for x in range(1, X)]
        order += line if row % 2 == 0 else line[::-1]
    return order


def ring_place(at, N):
    Z, X = ring_grid(N)
    if X == 1:
        return at
    if X == 2:
        return jnp.where(at < Z, at * 2, (2 * Z - 1 - at) * 2 + 1)
    row, column = lax.div(at - Z, X - 1), lax.rem(at - Z, X - 1)
    x = jnp.where(lax.rem(row, 2) == 0, 1 + column, X - 1 - column)
    return jnp.where(at < Z, at * X, (Z - 1 - row) * X + x)


def ring_position(s, N):
    Z, X = ring_grid(N)
    z, x = lax.div(s, X), lax.rem(s, X)
    if X == 1:
        return z
    if X == 2:
        return jnp.where(x == 0, z, 2 * Z - 1 - z)
    row = Z - 1 - z
    turn = jnp.where(lax.rem(row, 2) == 0, x - 1, X - 1 - x)
    return jnp.where(x == 0, z, Z + row * (X - 1) + turn)


def ring_owner(k, N):
    at = ring_position(lax.axis_index("shard"), N) + k % N
    return ring_place(jnp.where(at >= N, at - N, at), N)


def ring_slot(s, N):
    at = ring_position(jnp.int32(s), N) - ring_position(lax.axis_index("shard"), N)
    return jnp.where(at < 0, at + N, at)


def arrived(N, rows):
    half = rows // 32 * 16
    pieces = [(0, 0, rows)]
    for k in range(1, N // 2):
        pieces += [(N - k, 0, rows), (k, 0, rows)]
    return pieces + [(N // 2, 0, half), (N // 2, half, rows - half)]


def call(kernel, spaces, inputs, outputs, out_spaces, scratch, name):
    places = {
        "s": pl.BlockSpec(memory_space=pltpu.SMEM),
        "v": pl.BlockSpec(memory_space=pltpu.VMEM),
        "a": pl.BlockSpec(memory_space=pl.ANY),
    }
    return list(pl.pallas_call(
        kernel,
        out_shape=list(outputs),
        in_specs=[places[c] for c in spaces],
        out_specs=[places[c] for c in out_spaces],
        scratch_shapes=scratch,
        compiler_params=pltpu.CompilerParams(vmem_limit_bytes=56 * 2**20),
        cost_estimate=pl.CostEstimate(
            flops=1, bytes_accessed=1, transcendentals=0
        ),
        name=name,
    )(*inputs))


def aligned(start, unit):
    return pl.multiple_of(start, unit)


def column_block(ref, index, width):
    if width % LANES == 0:
        return ref[:, pl.ds(aligned(index * width, LANES), width)]
    tile = ref[:, pl.ds(aligned(lax.div(index * width, LANES) * LANES, LANES), LANES)].astype(f32)
    moved = pltpu.roll(tile, LANES - lax.rem(index * width, LANES), 1)
    return moved[:, :width].astype(bf16)


def pack_kernel(qd, kd, od, wq, wk, wv, wo, pre, post, qgain, kgain, out, rows):
    Q = lax.axis_index("seq")
    d = wq.shape[0]
    at = 0
    for ref, width in ((wq, qd), (wk, kd), (wv, kd), (wo, od)):
        out[:d, at : at + width] = column_block(ref, Q, width)
        at += width
    rows[...] = jnp.zeros_like(rows)
    for i, ref in enumerate((pre, post, qgain, kgain)):
        rows[i : i + 1, : ref.shape[1]] = ref[...].astype(f32)
    out[d:, :LANES] = rows[...].astype(bf16)
    out[d:, LANES:] = jnp.zeros((GAIN_ROWS, at - LANES), bf16)


def fold_rows(piece, D, width):
    extra = 64
    fits = piece == 2 * extra + extra // 4 and width == 2 * D + D // 4
    return extra if fits else 0


def folds(extra, D):
    parts = [(0, 0, 0, 0, extra, D), (0, D, extra, 0, extra, D)]
    for c in range(4):
        parts.append((c * extra // 4, 2 * D, 2 * extra, c * D // 4, extra // 4, D // 4))
    return parts


def columns_kernel(S, N, piece, extra, gate, up, down, out):
    Q = lax.axis_index("seq")
    d = gate.shape[0]
    for q in range(S):

        @pl.when(Q == q)
        def _():
            for base, ref in ((0, gate), (N * piece, up)):
                for s in range(N):
                    out[:d, base + s * piece : base + (s + 1) * piece] = ref[
                        :, (s * S + q) * piece : (s * S + q + 1) * piece
                    ]

    if extra:
        for row, col, at, first, rows, cols in folds(extra, down.shape[1]):
            out[d + row : d + row + rows, col : col + cols] = down[
                pl.ds(aligned(Q * piece + at, 16), rows), first : first + cols
            ]


def assemble_kernel(N, d, width, qd, od, *refs):
    pieces = arrived(N, d + GAIN_ROWS)
    chunks, (w, outs, gains) = refs[: len(pieces)], refs[len(pieces) :]
    Q = lax.axis_index("seq")
    gains[...] = jnp.zeros_like(gains)
    lane = lax.broadcasted_iota(jnp.int32, (GAIN_ROWS, LANES), 1)
    for ref, (k, first, rows) in zip(chunks, pieces):
        s = ring_owner(k, N)
        count = min(d - first, rows)
        to = s * d + first
        w[pl.ds(aligned(to, 16), count)] = ref[:count, :width]
        r = jnp.bitwise_xor(lax.div(to, qd), Q)
        outs[r, pl.ds(aligned(lax.rem(to, qd), 16), count)] = ref[:count, width : width + od]
        if first + rows > d:
            tile = ref[count:, :LANES].astype(f32)
            for row, many in ((0, d), (1, d), (2, HEAD_SIZE // N), (3, HEAD_SIZE // N)):
                at = s * many
                moved = pltpu.roll(jnp.where(lane < many, tile, 0.0), lax.rem(at, LANES), 1)
                where = pl.ds(aligned(lax.div(at, LANES) * LANES, LANES), LANES)
                gains[row : row + 1, where] += moved[row : row + 1]
    for row in (2, 3):
        x = gains[row : row + 1, :LANES]
        gains[row : row + 1, :LANES] = x + pltpu.roll(x, HEAD_SIZE, 1)


def group_ones():
    across = lax.broadcasted_iota(jnp.int32, (LANES, LANES), 0) // HEAD_SIZE
    down = lax.broadcasted_iota(jnp.int32, (LANES, LANES), 1) // HEAD_SIZE
    return jnp.where(across == down, 1.0 / HEAD_SIZE, 0.0).astype(bf16)


def split_dot(x, ones):
    high = x.astype(bf16)
    return dot(high, ones) + dot((x - high.astype(f32)).astype(bf16), ones)


def turned(x, low_half):
    half = HEAD_SIZE // 2
    return jnp.where(low_half, pltpu.roll(x, LANES - half, 1), pltpu.roll(x, half, 1))


def begins(starts, places):
    begin = jnp.zeros_like(places)
    for start in starts:
        begin = jnp.maximum(begin, jnp.where(places >= start, start, 0))
    return begin


def spread(x, half, low):
    moved = pltpu.roll(x, HEAD_SIZE, 1)
    return jnp.where(low, moved, x) if half else jnp.where(low, x, moved)


def head_tile(ref, at, low):
    first = at // LANES * LANES
    return spread(ref[:, first : first + LANES], at % LANES // HEAD_SIZE, low)


def forward_kernel(S, qd, kd, starts_ref, *refs):
    xs = refs[:S]
    (w_ref, gains_ref, cos_ref, sin_ref) = refs[S : S + 4]
    (nin_ref, proj_ref, rot_ref, att_ref, stat_ref, wide_ref, both_ref) = refs[S + 4 :]
    T = xs[0].shape[0]
    L = S * T
    heads = kd // HEAD_SIZE
    Q = lax.axis_index("seq")
    starts = [starts_ref[i] for i in range(starts_ref.shape[0])]
    ones = group_ones()
    lane = lax.broadcasted_iota(jnp.int32, (T, LANES), 1)
    low = lane < HEAD_SIZE
    low_half = lane % HEAD_SIZE < HEAD_SIZE // 2
    for r in range(S):
        rows = slice(r * T, (r + 1) * T)
        at = pl.ds(aligned(jnp.bitwise_xor(Q, r) * T, T), T)
        x = xs[r][...].astype(f32)
        nin = (x * inverse_root(x) * gains_ref[0:1]).astype(bf16)
        nin_ref[rows] = nin
        proj = dot(nin, w_ref[...])
        cos, sin = cos_ref[rows], sin_ref[rows]
        for first in range(0, qd + 2 * kd, LANES):
            cols = slice(first, first + LANES)
            tile = proj[:, cols]
            if first < qd + kd:
                proj_ref[at, cols] = tile
                gain = gains_ref[2:3, :LANES] if first < qd else gains_ref[3:4, :LANES]
                y = tile * lax.rsqrt(split_dot(tile * tile, ones) + eps_norm) * gain
                y = y * cos + turned(y, low_half) * sin
                if first + LANES > qd + kd:
                    y = jnp.where(low, y, tile)
                tile = y
            rot_ref[at, cols] = tile.astype(bf16)
    low_all = lax.broadcasted_iota(jnp.int32, (L, LANES), 1) < HEAD_SIZE
    for n in range(heads):
        wide_ref[...] = head_tile(rot_ref, qd + n * HEAD_SIZE, low_all)
        both_ref[:, :LANES] = head_tile(rot_ref, qd + kd + n * HEAD_SIZE, low_all)
        both_ref[:, LANES:] = jnp.ones((L, LANES), bf16)
        cols = slice(n * LANES, (n + 1) * LANES)
        for i in range(S):
            count = (i + 1) * T
            q = rot_ref[i * T : count, cols]
            zero = jnp.zeros_like(q)
            q2 = jnp.concatenate([jnp.where(low, q, zero), jnp.where(low, zero, q)], axis=0)
            s = times_t(q2, wide_ref[:count])
            qpos = i * T + lax.broadcasted_iota(jnp.int32, (T, 1), 0)
            qpos = jnp.concatenate([qpos, qpos], axis=0)
            kpos = lax.broadcasted_iota(jnp.int32, (2 * T, count), 1)
            ok = (kpos >= begins(starts, qpos)) & (kpos <= qpos)
            e = jnp.where(ok, jnp.exp2(s * SCALE2), 0.0).astype(bf16)
            o = dot(e, both_ref[:count])
            total = o[:, LANES:]
            out = o[:, :LANES] / total
            att_ref[pl.ds(aligned(jnp.bitwise_xor(Q, i) * T, T), T), cols] = jnp.where(
                low, out[:T], out[T:]
            ).astype(bf16)
            logs = jnp.log2(total)
            for a in range(GROUP):
                stat_ref[n * GROUP + a : n * GROUP + a + 1, i * T : count] = (
                    logs[a * T : (a + 1) * T].T[:1]
                )


def out_kernel(S, blocks, whole, att_ref, *refs):
    weights, outs = refs[:S], refs[S:]
    T = outs[0].shape[0]
    od = weights[0].shape[1]
    Q = lax.axis_index("seq")
    for j, r in enumerate(blocks):
        a = att_ref[r * T : (r + 1) * T]
        for c in range(S):
            cols = pl.ds(aligned(jnp.bitwise_xor(Q, c) * od, LANES), od)
            outs[j][:, cols] = dot(a, weights[c][...]).astype(outs[j].dtype)
    if whole:
        for c in range(S):
            cols = pl.ds(aligned(jnp.bitwise_xor(Q, c) * od, LANES), od)
            outs[-1][:, cols] = weights[c][...]


def backward_kernel(S, qd, kd, starts_ref, *refs):
    gbs = refs[:S]
    (wo_ref, rot_ref, proj_ref, att_ref, stat_ref, gains_ref, cos_ref, sin_ref) = refs[S : S + 8]
    (grad_ref, sums_ref, do_ref, delta_ref, k_ref, kt_ref, v_ref, dk_ref, dv_ref) = refs[S + 8 :]
    T = gbs[0].shape[0]
    L = S * T
    heads = kd // HEAD_SIZE
    Q = lax.axis_index("seq")
    starts = [starts_ref[i] for i in range(starts_ref.shape[0])]
    ones = group_ones()
    lane = lax.broadcasted_iota(jnp.int32, (T, LANES), 1)
    low = lane < HEAD_SIZE
    low_half = lane % HEAD_SIZE < HEAD_SIZE // 2
    picks = (
        lax.broadcasted_iota(jnp.int32, (8, LANES), 0)
        == lax.broadcasted_iota(jnp.int32, (8, LANES), 1) // HEAD_SIZE
    ).astype(bf16)
    sums_ref[...] = jnp.zeros_like(sums_ref)
    for r in range(S):
        rows = slice(r * T, (r + 1) * T)
        at = pl.ds(aligned(jnp.bitwise_xor(Q, r) * T, T), T)
        grads = times_t(gbs[r][...], wo_ref[...]).astype(bf16)
        do_ref[at] = grads
        for n in range(heads):
            cols = slice(n * LANES, (n + 1) * LANES)
            x = grads[:, cols].astype(f32) * att_ref[rows, cols].astype(f32)
            high = x.astype(bf16)
            rest = (x - high.astype(f32)).astype(bf16)
            delta_ref[n * 8 : n * 8 + 8, at] = times_t(picks, high) + times_t(picks, rest)

    def finish(g, rows, at, cols, gain):
        g = g * cos_ref[rows] - turned(g, low_half) * sin_ref[rows]
        tile = proj_ref[at, cols]
        inverse = lax.rsqrt(split_dot(tile * tile, ones) + eps_norm)
        unit = tile * inverse
        f = g * gain
        return g * unit, inverse * (f - unit * split_dot(f * unit, ones))

    low_all = lax.broadcasted_iota(jnp.int32, (L, LANES), 1) < HEAD_SIZE
    row_low = lax.broadcasted_iota(jnp.int32, (LANES, T), 0) < HEAD_SIZE
    for n in range(heads):
        k = head_tile(rot_ref, qd + n * HEAD_SIZE, low_all)
        k_ref[...] = k
        kt_ref[...] = k.T
        v_ref[...] = head_tile(rot_ref, qd + kd + n * HEAD_SIZE, low_all)
        dk_ref[n] = jnp.zeros((L, LANES), f32)
        dv_ref[n] = jnp.zeros((L, LANES), f32)
        cols = slice(n * LANES, (n + 1) * LANES)
        for i in range(S):
            count = (i + 1) * T
            here = slice(i * T, count)
            q = rot_ref[here, cols]
            do = do_ref[here, cols]
            zero = jnp.zeros_like(q)
            q2 = jnp.concatenate([jnp.where(low, q, zero), jnp.where(low, zero, q)], axis=0)
            do2 = jnp.concatenate([jnp.where(low, do, zero), jnp.where(low, zero, do)], axis=0)
            logs = jnp.concatenate(
                [stat_ref[n * GROUP + a : n * GROUP + a + 1, here] for a in range(GROUP)], axis=1
            )
            delta = jnp.concatenate(
                [delta_ref[n * 8 + a : n * 8 + a + 1, here] for a in range(GROUP)], axis=1
            )
            s = times_t(k_ref[:count], q2)
            dp = times_t(v_ref[:count], do2)
            qpos = i * T + lax.broadcasted_iota(jnp.int32, (1, T), 1)
            qpos = jnp.concatenate([qpos, qpos], axis=1)
            kpos = lax.broadcasted_iota(jnp.int32, (count, 2 * T), 0)
            ok = (kpos >= begins(starts, qpos)) & (kpos <= qpos)
            p = jnp.where(ok, jnp.exp2(s * SCALE2 - logs), 0.0)
            ds = (p * (dp - delta)).astype(bf16)
            dv_ref[n, :count] += dot(p.astype(bf16), do2)
            dk_ref[n, :count] += dot(ds, q2)
            dqt = dot(kt_ref[:, :count], ds)
            dq = jnp.where(row_low, dqt[:, :T], dqt[:, T:]).T * SCALE
            rows = pl.ds(aligned(jnp.bitwise_xor(Q, i) * T, T), T)
            total, grad = finish(dq, rows, here, cols, gains_ref[2:3, :LANES])
            sums_ref[0:1] += jnp.sum(total, axis=0, keepdims=True)
            grad_ref[rows, cols] = grad.astype(bf16)

    def folded(ref, n, rows):
        x = ref[n, rows]
        return x + pltpu.roll(x, HEAD_SIZE, 1)

    for first in range(qd, qd + 2 * kd, LANES):
        cols = slice(first, first + LANES)
        for i in range(S):
            here = slice(i * T, (i + 1) * T)
            sides = []
            for part in (first, first + HEAD_SIZE):
                is_key = part < qd + kd
                n = (part - qd if is_key else part - qd - kd) // HEAD_SIZE
                sides.append(folded(dk_ref if is_key else dv_ref, n, here))
            g = jnp.where(low, sides[0], sides[1])
            rows = pl.ds(aligned(jnp.bitwise_xor(Q, i) * T, T), T)
            if first < qd + kd:
                total, grad = finish(g * SCALE, rows, here, cols, gains_ref[3:4, :LANES])
                if first + LANES > qd + kd:
                    total = jnp.where(low, total, 0.0)
                    grad = jnp.where(low, grad, g)
                sums_ref[1:2] += jnp.sum(total, axis=0, keepdims=True)
                g = grad
            grad_ref[rows, cols] = g.astype(bf16)


def input_grad_kernel(blocks, grad_ref, w_ref, *refs):
    many = len(blocks)
    xs, outs, total = refs[:many], refs[many : 2 * many], refs[2 * many]
    T = xs[0].shape[0]
    total[...] = jnp.zeros_like(total)
    for j, r in enumerate(blocks):
        g = times_t(grad_ref[r * T : (r + 1) * T], w_ref[...])
        outs[j][...] = g.astype(outs[j].dtype)
        x = xs[j][...].astype(f32)
        total[0:1] += jnp.sum(g * (x * inverse_root(x)), axis=0, keepdims=True)


def out_grad_kernel(S, att_ref, *refs):
    gbs, outs, total = refs[:S], refs[S : 2 * S], refs[2 * S]
    T = gbs[0].shape[0]
    od = outs[0].shape[1]
    Q = lax.axis_index("seq")
    acc = t_times(att_ref[:T], gbs[0][...])
    for r in range(1, S):
        acc += t_times(att_ref[r * T : (r + 1) * T], gbs[r][...])
    total[...] = acc
    for r in range(S):
        cols = pl.ds(aligned(jnp.bitwise_xor(Q, r) * od, LANES), od)
        outs[r][...] = total[:, cols].astype(bf16)


def pack_grad_kernel(S, N, nin_ref, grad_ref, sums_ref, pre_near, pre_far, post_ref, *refs):
    parts, (out, full, rows) = refs[:S], refs[S:]
    D = nin_ref.shape[1]
    d = D // N
    width = grad_ref.shape[1]
    qd, od = parts[0].shape
    small = HEAD_SIZE // N
    Q = lax.axis_index("seq")
    for r in range(S):
        full[pl.ds(aligned(jnp.bitwise_xor(Q, r) * qd, qd), qd)] = parts[r][...]
    term = t_times(nin_ref[...], grad_ref[...]).astype(bf16)
    pre = pre_near[0:1] + pre_far[0:1]
    sums = sums_ref[...] + pltpu.roll(sums_ref[...], HEAD_SIZE, 1)
    rows[...] = jnp.zeros_like(rows)
    for s in range(N):
        k = ring_slot(s, N)
        at = slice(s * d, (s + 1) * d)
        out[k, :d, :width] = term[at]
        out[k, :d, width:] = full[at]
        rows[0:1, :d] = pre[:, at]
        rows[1:2, :d] = post_ref[:, at]
        rows[2:4, :small] = sums[0:2, s * small : (s + 1) * small]
        out[k, d:, :LANES] = rows[...].astype(bf16)
        out[k, d:, LANES:] = jnp.zeros((GAIN_ROWS, width + od - LANES), bf16)


def load_chunks(N, pieces, extra, chunks, w, down, sems):
    d = w.shape[0] // N
    piece = down.shape[0] // N
    copies = []

    def copy(source, target):
        copies.append(pltpu.make_async_copy(source, target, sems.at[len(copies)]))
        copies[-1].start()

    for ref, (k, first, rows) in zip(chunks, pieces):
        s = ring_owner(k, N)
        count = min(d - first, rows)
        copy(ref.at[:count], w.at[pl.ds(aligned(s * d + first, 16), count)])
        if extra and first + rows > d:
            for row, col, at, left, many, cols in folds(extra, down.shape[1]):
                copy(
                    ref.at[count + row : count + row + many, col : col + cols],
                    down.at[pl.ds(aligned(s * piece + at, 16), many), left : left + cols],
                )
    for c in copies:
        c.wait()


def feed_kernel(N, many, pieces, extra, *refs):
    mids, cots, refs = refs[:many], refs[many : 2 * many], refs[2 * many :]
    if pieces:
        chunks, refs = refs[: len(pieces)], refs[len(pieces) :]
        if not extra:
            down, refs = refs[0], refs[1:]
            hidden, both, *outs, w, sems = refs
        else:
            hidden, both, *outs, w, down, sems = refs
        load_chunks(N, pieces, extra, chunks, w, down, sems)
    else:
        w, down, hidden, both, *outs = refs
    T = mids[0].shape[0]
    FQ = down.shape[0]
    step = FQ // 3
    for j in range(many):
        rows = slice(j * T, (j + 1) * T)
        x = mids[j][...]
        c = cots[j][...]
        for first in range(0, FQ, step):
            cols = slice(first, first + step)
            gate = dot(x, w[:, cols])
            upper = dot(x, w[:, FQ + first : FQ + first + step])
            grad = times_t(c, down[cols])
            sigmoid = 1.0 / (1.0 + jnp.exp(-gate))
            swish = gate * sigmoid
            hidden[rows, cols] = (swish * upper).astype(bf16)
            both[rows, cols] = (grad * sigmoid * upper * (1.0 + gate - swish)).astype(bf16)
            both[rows, FQ + first : FQ + first + step] = (grad * swish).astype(bf16)
        outs[j][...] = times_t(both[rows], w[...]).astype(outs[j].dtype)


def both_grad_kernel(S, N, slots, extra, *refs):
    mids, near, far, folded = refs[:S], refs[S], refs[S + 1], refs[S + 2]
    outs, left = refs[S + 3 : -1], refs[-1]
    T, D = mids[0].shape
    d = D // N
    half = S // 2 * T
    width = near.shape[1]
    for r in range(S):
        rows = slice(r * T, (r + 1) * T)
        x = None if d % LANES == 0 else mids[r][...].astype(f32)
        for j, k in enumerate(slots):
            s = ring_owner(k, N)
            if x is None:
                part = mids[r][:, pl.ds(aligned(s * d, LANES), d)]
            else:
                moved = pltpu.roll(x, jnp.where(s == 0, 0, D - s * d), 1)
                part = moved[:, :d].astype(bf16)
            left[rows, j * d : (j + 1) * d] = part
    step = width // 3
    for first in range(0, width, step):
        cols = slice(first, first + step)
        g = t_times(left[:half], near[:, cols]) + t_times(left[half:], far[:, cols])
        held = list(outs)
        for j, k in enumerate(slots):
            at = j * d
            while at < (j + 1) * d:
                out = held.pop(0)
                count = min(out.shape[0], (j + 1) * d - at)
                out[:count, cols] = g[at : at + count].astype(bf16)
                at += count
            if extra:
                out[count:, cols] = folded[k, :, cols]


def down_grad_kernel(S, N, extra, near, far, *refs):
    cots, (out, cot) = refs[:S], refs[S:]
    T = cots[0].shape[0]
    half = S // 2 * T
    for r in range(S):
        cot[r * T : (r + 1) * T] = cots[r][...]
    D = cot.shape[1]
    piece = near.shape[1] // N
    step = D // 2
    for first in range(0, D, step):
        cols = slice(first, first + step)
        g = t_times(near[...], cot[:half, cols]) + t_times(far[...], cot[half:, cols])
        for s in range(N):
            part = g[s * piece : (s + 1) * piece].astype(bf16)
            if not extra:
                out[s, :, cols] = part
                continue
            k = ring_slot(s, N)
            for row, col, at, left, rows, many in folds(extra, D):
                low, high = max(left, first), min(left + many, first + step)
                if low < high:
                    out[k, row : row + rows, col + low - left : col + high - left] = part[
                        at : at + rows, low - first : high - first
                    ]


def load_blocks(blocks, held, sems):
    Q = lax.axis_index("seq")
    copies = []
    for r, ref in enumerate(blocks):
        copies.append(
            pltpu.make_async_copy(ref, held.at[jnp.bitwise_xor(Q, r)], sems.at[r])
        )
        copies[-1].start()
    for c in copies:
        c.wait()


def both_out_kernel(S, N, extra, *refs):
    blocks, (gate, up, *down, held, sems) = refs[:S], refs[S:]
    load_blocks(blocks, held, sems)
    d = gate.shape[0]
    piece = gate.shape[1] // N // S
    for q in range(S):
        for base, out in ((0, gate), (N * piece, up)):
            for s in range(N):
                out[:, (s * S + q) * piece : (s * S + q + 1) * piece] = held[
                    q, :d, base + s * piece : base + (s + 1) * piece
                ].astype(f32)
        if extra:
            for row, col, at, left, rows, cols in folds(extra, down[0].shape[1]):
                down[0][q * piece + at : q * piece + at + rows, left : left + cols] = held[
                    q, d + row : d + row + rows, col : col + cols
                ].astype(f32)


def down_out_kernel(S, *refs):
    blocks, (out, held, sems) = refs[:S], refs[S:]
    load_blocks(blocks, held, sems)
    piece = held.shape[1]
    for q in range(S):
        out[q * piece : (q + 1) * piece] = held[q].astype(f32)


def pack_out_kernel(S, N, qd, kd, *refs):
    blocks, refs = refs[:S], refs[S:]
    outs, (pre, post, qgain, kgain, held, sems) = refs[:4], refs[4:]
    load_blocks(blocks, held, sems)
    d = outs[0].shape[0]
    od = outs[3].shape[1] // S
    at = 0
    for out, width in zip(outs, (qd, kd, kd, od)):
        for q in range(S):
            out[:, q * width : (q + 1) * width] = held[q, :d, at : at + width].astype(f32)
        at += width
    rows = held[0, d:, :LANES].astype(f32)
    for q in range(1, S):
        rows += held[q, d:, :LANES].astype(f32)
    for i, ref in enumerate((pre, post, qgain, kgain)):
        ref[...] = rows[i : i + 1, : ref.shape[1]]


def per_device(
    tokens,
    doc_starts,
    pre_gain,
    query_weight,
    key_matrix,
    value_matrix,
    query_gain,
    key_gain,
    out_weight,
    post_gain,
    gate_weight,
    up_weight,
    down_weight,
    cotangent,
):
    S = lax.axis_size("seq")
    N = lax.axis_size("shard")
    Q = lax.axis_index("seq")
    T, D = tokens.shape[1:]
    L = S * T
    d = D // N
    od = D // S
    qd = QUERY_HEADS * HEAD_SIZE // S
    kd = KEY_VALUE_HEADS * HEAD_SIZE // S
    width = qd + 2 * kd
    heads = kd // HEAD_SIZE
    FF = gate_weight.shape[1]
    piece = FF // N // S
    FQ = FF // S
    extra = fold_rows(piece, D, 2 * FQ)
    near, far = list(range(S // 2)), list(range(S // 2, S))
    dma = pltpu.SemaphoreType.DMA


    def swap(x, step):
        return lax.ppermute(x, "seq", [(i, i ^ step) for i in range(S)])

    def gather_seq(x):
        blocks = {0: x}
        step = S // 2
        while step:
            for r in list(blocks):
                blocks[r + step] = swap(blocks[r], step)
            step //= 2
        return [blocks[r] for r in range(S)]

    def block_shapes(blocks):
        return [shape((T, D), bf16 if r % 2 else f32) for r in blocks]

    order = ring_order(N)

    def hop(x, way):
        return lax.ppermute(x, "shard", [(order[i], order[(i + way) % N]) for i in range(N)])

    def after(x, *others):
        return lax.optimization_barrier((x, *others))[0]

    def pair(up, down):
        return lax.optimization_barrier((hop(up, 1), hop(down, -1)))


    def quarters(step):
        many = N // 2

        def quarter(i, *others):
            at = None
            for k in range(i * many // 4, (i + 1) * many // 4):
                at = step(k + 1, others)
            return at

        return quarter

    def gather_ring(x):
        half = x.shape[0] // 32 * 16
        chunks = [x]

        def step(k, others):
            up, down = chunks[-2:] if k > 1 else (x, x)
            if k == N // 2:
                up, down = up[:half], down[half:]
            up, down, *_ = lax.optimization_barrier((up, down, *others))
            chunks.extend(pair(up, down))
            return chunks[-1]

        return chunks, quarters(step)

    def scatter_ring(x, halves):
        half = halves[0].shape[0]
        moved = [*halves]
        sent = [*halves]

        def step(k, others):
            up, down = moved
            at = N // 2 + 1 - k
            if k > 1:
                ahead, behind = x[at].astype(f32), x[N - at].astype(f32)
                if k == 2:
                    ahead = jnp.concatenate([ahead[:half] + up.astype(f32), ahead[half:]], axis=0)
                    behind = jnp.concatenate(
                        [behind[:half], behind[half:] + down.astype(f32)], axis=0
                    )
                else:
                    ahead, behind = ahead + up.astype(f32), behind + down.astype(f32)
                up, down = ahead.astype(bf16), behind.astype(bf16)
            sent[:] = up, down
            up, down, *_ = lax.optimization_barrier((up, down, *others))
            moved[:] = pair(up, down)
            return moved[0]

        def total():
            return (x[0].astype(f32) + moved[0].astype(f32) + moved[1].astype(f32)).astype(bf16)

        return total, quarters(step), sent

    def partial_sum(blocks, low, size):
        if size == 2:
            return blocks[low] + swap(blocks[low + 1], 1).astype(f32)
        half = size // 2
        moved = swap(partial_sum(blocks, low + half, half).astype(bf16), half)
        return partial_sum(blocks, low, half) + moved.astype(f32)

    def far_part(blocks):
        return partial_sum([None] * len(near) + blocks, S // 2, S // 2).astype(bf16)

    (pack,) = call(
        functools.partial(pack_kernel, qd, kd, od),
        "v" * 8,
        (
            query_weight,
            key_matrix,
            value_matrix,
            out_weight,
            pre_gain[None],
            post_gain[None],
            query_gain[None],
            key_gain[None],
        ),
        [shape((d + GAIN_ROWS, width + od), bf16)],
        "v",
        [pltpu.VMEM((GAIN_ROWS, LANES), f32)],
        "pack",
    )
    pack_chunks, pack_ring = gather_ring(pack)
    pack_1 = pack_ring(0)
    local = tokens[0]
    xs = gather_seq(local)
    (both_columns,) = call(
        functools.partial(columns_kernel, S, N, piece, extra),
        "vvv",
        (after(gate_weight, pack), up_weight, down_weight),
        [shape((d + extra, 2 * FQ), bf16)],
        "v",
        [],
        "columns",
    )
    pack_2 = pack_ring(1, both_columns)
    starts = doc_starts[0]
    blocks_at = jnp.arange(S, dtype=jnp.int32) ^ Q
    places = (blocks_at[:, None] * T + jnp.arange(T, dtype=jnp.int32)[None, :]).reshape(L)
    cosine, sine = rope_tables(inside_of(after(starts, pack_1), places))
    cot = cotangent[0]
    cots = gather_seq(after(cot, pack_2))
    both_chunks, both_ring = gather_ring(both_columns)
    pack_ring(2, cosine, sine)
    pack_ring(3)
    both_1 = both_ring(0, pack_chunks[-1])
    both_pieces = arrived(N, d + extra)
    downs = []
    if not extra:
        own_rows = lax.dynamic_slice(
            down_weight, (Q * piece, 0), (piece, D), allow_negative_indices=False
        )
        downs = [lax.all_gather(own_rows, "shard", axis=0, tiled=True)]

    w_qkv, out_parts, gains = call(
        functools.partial(assemble_kernel, N, d, width, qd, od),
        "v" * len(pack_chunks),
        pack_chunks,
        [shape((D, width), bf16), shape((S, qd, od), bf16), shape((8, D), f32)],
        "vvv",
        [],
        "assemble",
    )
    out_blocks = [out_parts[0]] + [swap(out_parts[r], r) for r in range(1, S)]

    normed_in, proj, rotated, attended, stats = call(
        functools.partial(forward_kernel, S, qd, kd),
        "s" + "v" * (S + 4),
        (starts, *xs, after(w_qkv, cots[S // 2], both_1), gains, cosine, sine),
        [
            shape((L, D), bf16),
            shape((L, -(-(qd + kd) // LANES) * LANES), f32),
            shape((L, width), bf16),
            shape((L, qd), bf16),
            shape((max(8, qd // HEAD_SIZE), L), f32),
        ],
        "v" * 5,
        [pltpu.VMEM((L, LANES), bf16), pltpu.VMEM((L, 2 * LANES), bf16)],
        "attend",
    )

    both_2 = both_ring(1)

    def project(blocks, whole):
        return call(
            functools.partial(out_kernel, S, blocks, whole),
            "v" * (S + 1),
            (attended, *out_blocks),
            block_shapes(blocks) + ([shape((qd, D), bf16)] if whole else []),
            "v" * (len(blocks) + whole),
            [],
            "project",
        )

    far_blocks = project(far, False)
    *near_blocks, full_out = project(near, True)
    far_sum = after(far_part(far_blocks), both_2)
    both_ring(2)
    middle = (
        local.astype(f32)
        + partial_sum(near_blocks, 0, S // 2)
        + swap(far_sum, S // 2).astype(f32)
    )

    full_post = gains[1]
    root_mid = inverse_root(middle)
    scaled_mid = middle * root_mid
    normed_mid = (scaled_mid * full_post).astype(bf16)
    both_ring(3, normed_mid)
    mids = gather_seq(normed_mid)
    def feed(blocks, first, weights, pieces):
        rows = len(blocks) * T
        made = []
        if pieces:
            made = [shape((D, 2 * FQ), bf16)] + [shape((FQ, D), bf16)] * (extra > 0)
        return call(
            functools.partial(feed_kernel, N, len(blocks), pieces, extra),
            "v" * (2 * len(blocks))
            + ("a" * len(pieces) + "v" * (len(weights) - len(pieces)) if pieces else "vv"),
            (first, *[mids[r] for r in blocks[1:]], *[cots[r] for r in blocks], *weights),
            [shape((rows, FQ), bf16), shape((rows, 2 * FQ), bf16)] + block_shapes(blocks) + made,
            "v" * (2 + len(blocks) + len(made)),
            [dma((len(pieces) + 6 * N,))] if pieces else [],
            "feed",
        )

    hidden_far, both_far, *grads_far = feed(
        far, mids[far[0]], both_chunks + downs, both_pieces
    )
    if extra:
        downs = [grads_far.pop()]
    full_both = grads_far.pop()
    far_sum = far_part(grads_far)
    hidden_near, both_near, *grads_near = feed(
        near, after(mids[near[0]], far_sum), [full_both] + downs, []
    )
    far_moved = swap(far_sum, S // 2)
    term_both = {}
    split = (d + extra) // 32 * 16
    (term_down,) = call(
        functools.partial(down_grad_kernel, S, N, extra),
        "v" * (S + 2),
        (hidden_near, hidden_far, *cots),
        [shape((N, extra, 2 * FQ) if extra else (N, piece, D), bf16)],
        "v",
        [pltpu.VMEM((L, D), bf16)],
        "down_grad",
    )

    def both_grads(slots, side):
        rows = []
        for k in slots:
            rows += [split, d + extra - split] if k == N // 2 else [d + extra]
        terms = call(
            functools.partial(both_grad_kernel, S, N, slots, extra),
            "v" * (S + 3),
            (*mids, side, both_far, term_down),
            [shape((many, 2 * FQ), bf16) for many in rows],
            "v" * len(rows),
            [pltpu.VMEM((L, len(slots) * d), bf16)],
            "both_grad",
        )
        if slots[0] == N // 2:
            term_both[N // 2] = terms[:2]
            terms, slots = terms[2:], slots[1:]
        term_both.update(zip(slots, terms))
        return terms[0]

    middle_slots = [N // 2, N // 2 - 1, N // 2 + 1]
    grads_near[0] = after(grads_near[0], term_down)
    grad_nmid = partial_sum(grads_near, 0, S // 2) + far_moved.astype(f32)
    term_post = jnp.sum(grad_nmid * scaled_mid, axis=0)
    grad_middle = cot.astype(f32) + norm_back(grad_nmid * full_post, middle, root_mid)
    grad_branch = grad_middle.astype(bf16)
    first_terms = both_grads(middle_slots, after(both_near, grad_branch))
    both_total, both_back, both_sent = scatter_ring(term_both, term_both[N // 2])
    both_back(0)
    last_terms = both_grads(
        [k for k in range(N) if k not in middle_slots], after(both_near, first_terms)
    )
    both_back(1, last_terms)
    second = tuple(both_sent)
    output_blocks = []
    for hidden, blocks in ((after(hidden_near, *second), near), (hidden_far, far)):
        product = dot(hidden, downs[0])
        for j, r in enumerate(blocks):
            block = product[j * T : (j + 1) * T]
            output_blocks.append(block.astype(bf16) if r % 2 else block)

    out_sum = far_part(output_blocks[len(near) :])
    out_moved = swap(out_sum, S // 2)

    gbs = gather_seq(grad_branch)
    out_terms = call(
        functools.partial(out_grad_kernel, S),
        "v" * (S + 1),
        (attended, *gbs),
        [shape((qd, od), bf16)] * S,
        "v" * S,
        [pltpu.VMEM((qd, D), f32)],
        "out_grad",
    )
    first_gb = after(gbs[0], *second, out_terms[0], out_sum)
    grad_proj, sums = call(
        functools.partial(backward_kernel, S, qd, kd),
        "s" + "v" * (S + 8),
        (starts, first_gb, *gbs[1:], full_out, rotated, proj, attended, stats, gains, cosine, sine),
        [shape((L, width), bf16), shape((8, LANES), f32)],
        "vv",
        [
            pltpu.VMEM((L, qd), bf16),
            pltpu.VMEM((8 * heads, L), f32),
            pltpu.VMEM((L, LANES), bf16),
            pltpu.VMEM((LANES, L), bf16),
            pltpu.VMEM((L, LANES), bf16),
            pltpu.VMEM((heads, L, LANES), f32),
            pltpu.VMEM((heads, L, LANES), f32),
        ],
        "attend_back",
    )

    both_back(2, grad_proj)
    third = tuple(both_sent)
    back_4 = both_back(3)
    output_blocks[0] = after(output_blocks[0], grad_proj)
    output = middle + partial_sum(output_blocks, 0, S // 2) + out_moved.astype(f32)
    out_terms = [out_terms[0]] + [swap(out_terms[r], r) for r in range(1, S)]
    grad_proj = after(grad_proj, *third, out_moved, *out_terms[1:])

    def input_grads(blocks):
        return call(
            functools.partial(input_grad_kernel, blocks),
            "v" * (2 + len(blocks)),
            (grad_proj, w_qkv, *[xs[r] for r in blocks]),
            block_shapes(blocks) + [shape((8, D), f32)],
            "v" * (len(blocks) + 1),
            [],
            "input_grad",
        )

    *nins_far, pre_far = input_grads(far)
    *nins_near, pre_near = input_grads(near)
    nin_sum = far_part(nins_far)
    nin_moved = swap(nin_sum, S // 2)
    grad_nin = partial_sum(nins_near, 0, S // 2) + nin_moved.astype(f32)
    wide = local.astype(f32)
    grad_tokens = grad_middle + norm_back(grad_nin * gains[0], wide, inverse_root(wide))

    (pack_terms,) = call(
        functools.partial(pack_grad_kernel, S, N),
        "v" * (6 + S),
        (
            after(normed_in, nin_moved),
            grad_proj,
            sums,
            pre_near,
            pre_far,
            term_post[None],
            *out_terms,
        ),
        [shape((N, d + GAIN_ROWS, width + od), bf16)],
        "v",
        [pltpu.VMEM((D, od), bf16), pltpu.VMEM((GAIN_ROWS, LANES), f32)],
        "pack_grad",
    )
    split = (d + GAIN_ROWS) // 32 * 16
    pack_total, pack_back, _ = scatter_ring(
        pack_terms, (pack_terms[N // 2, :split], pack_terms[N // 2, split:])
    )
    pack_back(0, back_4)
    pack_back(1)
    pack_back(2)
    pack_back(3)

    gate_grad, up_grad, *down_grad = call(
        functools.partial(both_out_kernel, S, N, extra),
        "a" * S,
        gather_seq(both_total()),
        [shape((d, FF), f32), shape((d, FF), f32)] + [shape((S * piece, D), f32)] * (extra > 0),
        "vv" + "v" * (extra > 0),
        [pltpu.VMEM((S, d + extra, 2 * FQ), bf16), dma((S,))],
        "both_out",
    )
    if not extra:
        shard_down = lax.psum_scatter(
            term_down.reshape(FQ, D), "shard", scatter_dimension=0, tiled=True
        )
        down_grad = call(
            functools.partial(down_out_kernel, S),
            "a" * S,
            gather_seq(shard_down),
            [shape((S * piece, D), f32)],
            "v",
            [pltpu.VMEM((S, piece, D), bf16), dma((S,))],
            "down_out",
        )
    pack_blocks = gather_seq(pack_total())
    pack_blocks[0] = after(pack_blocks[0], gate_grad)
    small = HEAD_SIZE // N
    q_grad, k_grad, v_grad, o_grad, pre_grad, post_grad, qgain_grad, kgain_grad = call(
        functools.partial(pack_out_kernel, S, N, qd, kd),
        "a" * S,
        pack_blocks,
        [
            shape((d, S * qd), f32),
            shape((d, S * kd), f32),
            shape((d, S * kd), f32),
            shape((d, D), f32),
            shape((1, d), f32),
            shape((1, d), f32),
            shape((1, small), f32),
            shape((1, small), f32),
        ],
        "v" * 8,
        [pltpu.VMEM((S, d + GAIN_ROWS, width + od), bf16), dma((S,))],
        "pack_out",
    )
    return (
        output.astype(bf16)[None],
        grad_tokens[None],
        pre_grad[0],
        q_grad,
        k_grad,
        v_grad,
        qgain_grad[0],
        kgain_grad[0],
        o_grad,
        post_grad[0],
        gate_grad,
        up_grad,
        down_grad[0],
    )


def solution(mesh):
    row, vector, matrix = P("shard", "seq", None), P("shard"), P("shard", None)
    return jax.shard_map(
        per_device,
        mesh=mesh,
        in_specs=(
            row,
            matrix,
            vector,
            matrix,
            matrix,
            matrix,
            vector,
            vector,
            matrix,
            vector,
            matrix,
            matrix,
            matrix,
            row,
        ),
        out_specs=(
            row,
            row,
            vector,
            matrix,
            matrix,
            matrix,
            vector,
            vector,
            matrix,
            vector,
            matrix,
            matrix,
            matrix,
        ),
        check_vma=False,
    )
```

```python
import functools
import math

import jax
import jax.numpy as jnp
from jax import lax
from jax.experimental import pallas as pl
from jax.experimental.pallas import tpu as pltpu
from jax.sharding import PartitionSpec as P

QUERY_HEADS = 16
KEY_VALUE_HEADS = 8
HEAD_SIZE = 64
GROUP = QUERY_HEADS // KEY_VALUE_HEADS
LANES = 128
GAIN_ROWS = 16
SCALE = HEAD_SIZE ** (-0.5)
SCALE2 = SCALE * math.log2(math.e)


eps_norm = 1e-05
rope_base = 1000000.0

bf16 = jnp.bfloat16
f32 = jnp.float32
shape = jax.ShapeDtypeStruct


def dot(left, right):
    return jnp.dot(left, right, preferred_element_type=f32)


def times_t(left, right):
    return lax.dot_general(left, right, (((1,), (1,)), ((), ())), preferred_element_type=f32)


def t_times(left, right):
    return lax.dot_general(left, right, (((0,), (0,)), ((), ())), preferred_element_type=f32)


def inverse_root(value_tokens):
    return lax.rsqrt(jnp.mean(value_tokens * value_tokens, axis=-1, keepdims=True) + eps_norm)


def norm_back(grad_scaled, value_tokens, root):
    return root * (
        grad_scaled
        - value_tokens
        * (root * root)
        * jnp.mean(grad_scaled * value_tokens, axis=-1, keepdims=True)
    )


def rope_tables(places):
    half = HEAD_SIZE // 2
    lane = jnp.arange(LANES, dtype=jnp.int32) % HEAD_SIZE
    inverse = jnp.exp((lane % half).astype(f32) * (-2.0 * math.log(rope_base) / HEAD_SIZE))
    angle = places.astype(f32)[:, None] * inverse[None, :]
    sine = jnp.sin(angle)
    return (jnp.cos(angle), jnp.where(lane < half, -sine, sine))


def inside_of(starts, places):
    before = starts[None, :] <= places[:, None]
    return places - jnp.max(jnp.where(before, starts[None, :], 0), axis=1)


def ring_grid(N):
    Z = min(N, 4)
    return Z, N // Z


def ring_order(N):
    Z, X = ring_grid(N)
    order = [z * X for z in range(Z)]
    for row in range(Z):
        line = [(Z - 1 - row) * X + x for x in range(1, X)]
        order += line if row % 2 == 0 else line[::-1]
    return order


def ring_place(at, N):
    Z, X = ring_grid(N)
    if X == 1:
        return at
    if X == 2:
        return jnp.where(at < Z, at * 2, (2 * Z - 1 - at) * 2 + 1)
    row, column = lax.div(at - Z, X - 1), lax.rem(at - Z, X - 1)
    x = jnp.where(lax.rem(row, 2) == 0, 1 + column, X - 1 - column)
    return jnp.where(at < Z, at * X, (Z - 1 - row) * X + x)


def ring_position(s, N):
    Z, X = ring_grid(N)
    z, x = lax.div(s, X), lax.rem(s, X)
    if X == 1:
        return z
    if X == 2:
        return jnp.where(x == 0, z, 2 * Z - 1 - z)
    row = Z - 1 - z
    turn = jnp.where(lax.rem(row, 2) == 0, x - 1, X - 1 - x)
    return jnp.where(x == 0, z, Z + row * (X - 1) + turn)


def ring_owner(k, N):
    at = ring_position(lax.axis_index("shard"), N) + k % N
    return ring_place(jnp.where(at >= N, at - N, at), N)


def ring_slot(s, N):
    at = ring_position(jnp.int32(s), N) - ring_position(lax.axis_index("shard"), N)
    return jnp.where(at < 0, at + N, at)


def arrived(N, rows):
    half = rows // 32 * 16
    pieces = [(0, 0, rows)]
    for k in range(1, N // 2):
        pieces += [(N - k, 0, rows), (k, 0, rows)]
    return pieces + [(N // 2, 0, half), (N // 2, half, rows - half)]


def call(kernel, spaces, inputs, outputs, out_spaces, scratch, name):
    places = {
        "s": pl.BlockSpec(memory_space=pltpu.SMEM),
        "v": pl.BlockSpec(memory_space=pltpu.VMEM),
        "a": pl.BlockSpec(memory_space=pl.ANY),
    }
    return list(pl.pallas_call(
        kernel,
        out_shape=list(outputs),
        in_specs=[places[c] for c in spaces],
        out_specs=[places[c] for c in out_spaces],
        scratch_shapes=scratch,
        compiler_params=pltpu.CompilerParams(vmem_limit_bytes=56 * 2**20),
        cost_estimate=pl.CostEstimate(
            flops=1, bytes_accessed=1, transcendentals=0
        ),
        name=name,
    )(*inputs))


def aligned(start, unit):
    return pl.multiple_of(start, unit)


def column_block(ref, index, width):
    if width % LANES == 0:
        return ref[:, pl.ds(aligned(index * width, LANES), width)]
    tile = ref[:, pl.ds(aligned(lax.div(index * width, LANES) * LANES, LANES), LANES)].astype(f32)
    moved = pltpu.roll(tile, LANES - lax.rem(index * width, LANES), 1)
    return moved[:, :width].astype(bf16)


def pack_kernel(qd, kd, od, wq, wk, wv, wo, pre, post, qgain, kgain, out, rows):
    Q = lax.axis_index("seq")
    d = wq.shape[0]
    at = 0
    for ref, width in ((wq, qd), (wk, kd), (wv, kd), (wo, od)):
        out[:d, at : at + width] = column_block(ref, Q, width)
        at += width
    rows[...] = jnp.zeros_like(rows)
    for i, ref in enumerate((pre, post, qgain, kgain)):
        rows[i : i + 1, : ref.shape[1]] = ref[...].astype(f32)
    out[d:, :LANES] = rows[...].astype(bf16)
    out[d:, LANES:] = jnp.zeros((GAIN_ROWS, at - LANES), bf16)


def fold_rows(piece, D, width):
    extra = 64
    fits = piece == 2 * extra + extra // 4 and width == 2 * D + D // 4
    return extra if fits else 0


def folds(extra, D):
    parts = [(0, 0, 0, 0, extra, D), (0, D, extra, 0, extra, D)]
    for c in range(4):
        parts.append((c * extra // 4, 2 * D, 2 * extra, c * D // 4, extra // 4, D // 4))
    return parts


def columns_kernel(S, N, piece, extra, gate, up, down, out):
    Q = lax.axis_index("seq")
    d = gate.shape[0]
    for q in range(S):

        @pl.when(Q == q)
        def _():
            for base, ref in ((0, gate), (N * piece, up)):
                for s in range(N):
                    out[:d, base + s * piece : base + (s + 1) * piece] = ref[
                        :, (s * S + q) * piece : (s * S + q + 1) * piece
                    ]

    if extra:
        for row, col, at, first, rows, cols in folds(extra, down.shape[1]):
            out[d + row : d + row + rows, col : col + cols] = down[
                pl.ds(aligned(Q * piece + at, 16), rows), first : first + cols
            ]


def assemble_kernel(N, d, width, qd, od, *refs):
    pieces = arrived(N, d + GAIN_ROWS)
    chunks, (w, outs, gains) = refs[: len(pieces)], refs[len(pieces) :]
    Q = lax.axis_index("seq")
    gains[...] = jnp.zeros_like(gains)
    lane = lax.broadcasted_iota(jnp.int32, (GAIN_ROWS, LANES), 1)
    for ref, (k, first, rows) in zip(chunks, pieces):
        s = ring_owner(k, N)
        count = min(d - first, rows)
        to = s * d + first
        w[pl.ds(aligned(to, 16), count)] = ref[:count, :width]
        r = jnp.bitwise_xor(lax.div(to, qd), Q)
        outs[r, pl.ds(aligned(lax.rem(to, qd), 16), count)] = ref[:count, width : width + od]
        if first + rows > d:
            tile = ref[count:, :LANES].astype(f32)
            for row, many in ((0, d), (1, d), (2, HEAD_SIZE // N), (3, HEAD_SIZE // N)):
                at = s * many
                moved = pltpu.roll(jnp.where(lane < many, tile, 0.0), lax.rem(at, LANES), 1)
                where = pl.ds(aligned(lax.div(at, LANES) * LANES, LANES), LANES)
                gains[row : row + 1, where] += moved[row : row + 1]
    for row in (2, 3):
        x = gains[row : row + 1, :LANES]
        gains[row : row + 1, :LANES] = x + pltpu.roll(x, HEAD_SIZE, 1)


def group_ones():
    across = lax.broadcasted_iota(jnp.int32, (LANES, LANES), 0) // HEAD_SIZE
    down = lax.broadcasted_iota(jnp.int32, (LANES, LANES), 1) // HEAD_SIZE
    return jnp.where(across == down, 1.0 / HEAD_SIZE, 0.0).astype(bf16)


def split_dot(x, ones):
    high = x.astype(bf16)
    return dot(high, ones) + dot((x - high.astype(f32)).astype(bf16), ones)


def turned(x, low_half):
    half = HEAD_SIZE // 2
    return jnp.where(low_half, pltpu.roll(x, LANES - half, 1), pltpu.roll(x, half, 1))


def begins(starts, places):
    begin = jnp.zeros_like(places)
    for start in starts:
        begin = jnp.maximum(begin, jnp.where(places >= start, start, 0))
    return begin


def spread(x, half, low):
    moved = pltpu.roll(x, HEAD_SIZE, 1)
    return jnp.where(low, moved, x) if half else jnp.where(low, x, moved)


def head_tile(ref, at, low):
    first = at // LANES * LANES
    return spread(ref[:, first : first + LANES], at % LANES // HEAD_SIZE, low)


def forward_kernel(S, qd, kd, starts_ref, *refs):
    xs = refs[:S]
    (w_ref, gains_ref, cos_ref, sin_ref) = refs[S : S + 4]
    (nin_ref, proj_ref, rot_ref, att_ref, stat_ref, wide_ref, both_ref) = refs[S + 4 :]
    T = xs[0].shape[0]
    L = S * T
    heads = kd // HEAD_SIZE
    Q = lax.axis_index("seq")
    starts = [starts_ref[i] for i in range(starts_ref.shape[0])]
    ones = group_ones()
    lane = lax.broadcasted_iota(jnp.int32, (T, LANES), 1)
    low = lane < HEAD_SIZE
    low_half = lane % HEAD_SIZE < HEAD_SIZE // 2
    for r in range(S):
        rows = slice(r * T, (r + 1) * T)
        at = pl.ds(aligned(jnp.bitwise_xor(Q, r) * T, T), T)
        x = xs[r][...].astype(f32)
        nin = (x * inverse_root(x) * gains_ref[0:1]).astype(bf16)
        nin_ref[rows] = nin
        proj = dot(nin, w_ref[...])
        cos, sin = cos_ref[rows], sin_ref[rows]
        for first in range(0, qd + 2 * kd, LANES):
            cols = slice(first, first + LANES)
            tile = proj[:, cols]
            if first < qd + kd:
                proj_ref[at, cols] = tile
                gain = gains_ref[2:3, :LANES] if first < qd else gains_ref[3:4, :LANES]
                y = tile * lax.rsqrt(split_dot(tile * tile, ones) + eps_norm) * gain
                y = y * cos + turned(y, low_half) * sin
                if first + LANES > qd + kd:
                    y = jnp.where(low, y, tile)
                tile = y
            rot_ref[at, cols] = tile.astype(bf16)
    low_all = lax.broadcasted_iota(jnp.int32, (L, LANES), 1) < HEAD_SIZE
    for n in range(heads):
        wide_ref[...] = head_tile(rot_ref, qd + n * HEAD_SIZE, low_all)
        both_ref[:, :LANES] = head_tile(rot_ref, qd + kd + n * HEAD_SIZE, low_all)
        both_ref[:, LANES:] = jnp.ones((L, LANES), bf16)
        cols = slice(n * LANES, (n + 1) * LANES)
        for i in range(S):
            count = (i + 1) * T
            q = rot_ref[i * T : count, cols]
            zero = jnp.zeros_like(q)
            q2 = jnp.concatenate([jnp.where(low, q, zero), jnp.where(low, zero, q)], axis=0)
            s = times_t(q2, wide_ref[:count])
            qpos = i * T + lax.broadcasted_iota(jnp.int32, (T, 1), 0)
            qpos = jnp.concatenate([qpos, qpos], axis=0)
            kpos = lax.broadcasted_iota(jnp.int32, (2 * T, count), 1)
            ok = (kpos >= begins(starts, qpos)) & (kpos <= qpos)
            e = jnp.where(ok, jnp.exp2(s * SCALE2), 0.0).astype(bf16)
            o = dot(e, both_ref[:count])
            total = o[:, LANES:]
            out = o[:, :LANES] / total
            att_ref[pl.ds(aligned(jnp.bitwise_xor(Q, i) * T, T), T), cols] = jnp.where(
                low, out[:T], out[T:]
            ).astype(bf16)
            logs = jnp.log2(total)
            for a in range(GROUP):
                stat_ref[n * GROUP + a : n * GROUP + a + 1, i * T : count] = (
                    logs[a * T : (a + 1) * T].T[:1]
                )


def out_kernel(S, blocks, whole, att_ref, *refs):
    weights, outs = refs[:S], refs[S:]
    T = outs[0].shape[0]
    od = weights[0].shape[1]
    Q = lax.axis_index("seq")
    for j, r in enumerate(blocks):
        a = att_ref[r * T : (r + 1) * T]
        for c in range(S):
            cols = pl.ds(aligned(jnp.bitwise_xor(Q, c) * od, LANES), od)
            outs[j][:, cols] = dot(a, weights[c][...]).astype(outs[j].dtype)
    if whole:
        for c in range(S):
            cols = pl.ds(aligned(jnp.bitwise_xor(Q, c) * od, LANES), od)
            outs[-1][:, cols] = weights[c][...]


def backward_kernel(S, qd, kd, starts_ref, *refs):
    gbs = refs[:S]
    (wo_ref, rot_ref, proj_ref, att_ref, stat_ref, gains_ref, cos_ref, sin_ref) = refs[S : S + 8]
    (grad_ref, sums_ref, do_ref, delta_ref, k_ref, kt_ref, v_ref, dk_ref, dv_ref) = refs[S + 8 :]
    T = gbs[0].shape[0]
    L = S * T
    heads = kd // HEAD_SIZE
    Q = lax.axis_index("seq")
    starts = [starts_ref[i] for i in range(starts_ref.shape[0])]
    ones = group_ones()
    lane = lax.broadcasted_iota(jnp.int32, (T, LANES), 1)
    low = lane < HEAD_SIZE
    low_half = lane % HEAD_SIZE < HEAD_SIZE // 2
    picks = (
        lax.broadcasted_iota(jnp.int32, (8, LANES), 0)
        == lax.broadcasted_iota(jnp.int32, (8, LANES), 1) // HEAD_SIZE
    ).astype(bf16)
    sums_ref[...] = jnp.zeros_like(sums_ref)
    for r in range(S):
        rows = slice(r * T, (r + 1) * T)
        at = pl.ds(aligned(jnp.bitwise_xor(Q, r) * T, T), T)
        grads = times_t(gbs[r][...], wo_ref[...]).astype(bf16)
        do_ref[at] = grads
        for n in range(heads):
            cols = slice(n * LANES, (n + 1) * LANES)
            x = grads[:, cols].astype(f32) * att_ref[rows, cols].astype(f32)
            high = x.astype(bf16)
            rest = (x - high.astype(f32)).astype(bf16)
            delta_ref[n * 8 : n * 8 + 8, at] = times_t(picks, high) + times_t(picks, rest)

    def finish(g, rows, at, cols, gain):
        g = g * cos_ref[rows] - turned(g, low_half) * sin_ref[rows]
        tile = proj_ref[at, cols]
        inverse = lax.rsqrt(split_dot(tile * tile, ones) + eps_norm)
        unit = tile * inverse
        f = g * gain
        return g * unit, inverse * (f - unit * split_dot(f * unit, ones))

    low_all = lax.broadcasted_iota(jnp.int32, (L, LANES), 1) < HEAD_SIZE
    row_low = lax.broadcasted_iota(jnp.int32, (LANES, T), 0) < HEAD_SIZE
    for n in range(heads):
        k = head_tile(rot_ref, qd + n * HEAD_SIZE, low_all)
        k_ref[...] = k
        kt_ref[...] = k.T
        v_ref[...] = head_tile(rot_ref, qd + kd + n * HEAD_SIZE, low_all)
        dk_ref[n] = jnp.zeros((L, LANES), f32)
        dv_ref[n] = jnp.zeros((L, LANES), f32)
        cols = slice(n * LANES, (n + 1) * LANES)
        for i in range(S):
            count = (i + 1) * T
            here = slice(i * T, count)
            q = rot_ref[here, cols]
            do = do_ref[here, cols]
            zero = jnp.zeros_like(q)
            q2 = jnp.concatenate([jnp.where(low, q, zero), jnp.where(low, zero, q)], axis=0)
            do2 = jnp.concatenate([jnp.where(low, do, zero), jnp.where(low, zero, do)], axis=0)
            logs = jnp.concatenate(
                [stat_ref[n * GROUP + a : n * GROUP + a + 1, here] for a in range(GROUP)], axis=1
            )
            delta = jnp.concatenate(
                [delta_ref[n * 8 + a : n * 8 + a + 1, here] for a in range(GROUP)], axis=1
            )
            s = times_t(k_ref[:count], q2)
            dp = times_t(v_ref[:count], do2)
            qpos = i * T + lax.broadcasted_iota(jnp.int32, (1, T), 1)
            qpos = jnp.concatenate([qpos, qpos], axis=1)
            kpos = lax.broadcasted_iota(jnp.int32, (count, 2 * T), 0)
            ok = (kpos >= begins(starts, qpos)) & (kpos <= qpos)
            p = jnp.where(ok, jnp.exp2(s * SCALE2 - logs), 0.0)
            ds = (p * (dp - delta)).astype(bf16)
            dv_ref[n, :count] += dot(p.astype(bf16), do2)
            dk_ref[n, :count] += dot(ds, q2)
            dqt = dot(kt_ref[:, :count], ds)
            dq = jnp.where(row_low, dqt[:, :T], dqt[:, T:]).T * SCALE
            rows = pl.ds(aligned(jnp.bitwise_xor(Q, i) * T, T), T)
            total, grad = finish(dq, rows, here, cols, gains_ref[2:3, :LANES])
            sums_ref[0:1] += jnp.sum(total, axis=0, keepdims=True)
            grad_ref[rows, cols] = grad.astype(bf16)

    def folded(ref, n, rows):
        x = ref[n, rows]
        return x + pltpu.roll(x, HEAD_SIZE, 1)

    for first in range(qd, qd + 2 * kd, LANES):
        cols = slice(first, first + LANES)
        for i in range(S):
            here = slice(i * T, (i + 1) * T)
            sides = []
            for part in (first, first + HEAD_SIZE):
                is_key = part < qd + kd
                n = (part - qd if is_key else part - qd - kd) // HEAD_SIZE
                sides.append(folded(dk_ref if is_key else dv_ref, n, here))
            g = jnp.where(low, sides[0], sides[1])
            rows = pl.ds(aligned(jnp.bitwise_xor(Q, i) * T, T), T)
            if first < qd + kd:
                total, grad = finish(g * SCALE, rows, here, cols, gains_ref[3:4, :LANES])
                if first + LANES > qd + kd:
                    total = jnp.where(low, total, 0.0)
                    grad = jnp.where(low, grad, g)
                sums_ref[1:2] += jnp.sum(total, axis=0, keepdims=True)
                g = grad
            grad_ref[rows, cols] = g.astype(bf16)


def input_grad_kernel(blocks, grad_ref, w_ref, *refs):
    many = len(blocks)
    xs, outs, total = refs[:many], refs[many : 2 * many], refs[2 * many]
    T = xs[0].shape[0]
    total[...] = jnp.zeros_like(total)
    for j, r in enumerate(blocks):
        g = times_t(grad_ref[r * T : (r + 1) * T], w_ref[...])
        outs[j][...] = g.astype(outs[j].dtype)
        x = xs[j][...].astype(f32)
        total[0:1] += jnp.sum(g * (x * inverse_root(x)), axis=0, keepdims=True)


def out_grad_kernel(S, att_ref, *refs):
    gbs, outs, total = refs[:S], refs[S : 2 * S], refs[2 * S]
    T = gbs[0].shape[0]
    od = outs[0].shape[1]
    Q = lax.axis_index("seq")
    acc = t_times(att_ref[:T], gbs[0][...])
    for r in range(1, S):
        acc += t_times(att_ref[r * T : (r + 1) * T], gbs[r][...])
    total[...] = acc
    for r in range(S):
        cols = pl.ds(aligned(jnp.bitwise_xor(Q, r) * od, LANES), od)
        outs[r][...] = total[:, cols].astype(bf16)


def pack_grad_kernel(S, N, nin_ref, grad_ref, sums_ref, pre_near, pre_far, post_ref, *refs):
    parts, (out, full, rows) = refs[:S], refs[S:]
    D = nin_ref.shape[1]
    d = D // N
    width = grad_ref.shape[1]
    qd, od = parts[0].shape
    small = HEAD_SIZE // N
    Q = lax.axis_index("seq")
    for r in range(S):
        full[pl.ds(aligned(jnp.bitwise_xor(Q, r) * qd, qd), qd)] = parts[r][...]
    term = t_times(nin_ref[...], grad_ref[...]).astype(bf16)
    pre = pre_near[0:1] + pre_far[0:1]
    sums = sums_ref[...] + pltpu.roll(sums_ref[...], HEAD_SIZE, 1)
    rows[...] = jnp.zeros_like(rows)
    for s in range(N):
        k = ring_slot(s, N)
        at = slice(s * d, (s + 1) * d)
        out[k, :d, :width] = term[at]
        out[k, :d, width:] = full[at]
        rows[0:1, :d] = pre[:, at]
        rows[1:2, :d] = post_ref[:, at]
        rows[2:4, :small] = sums[0:2, s * small : (s + 1) * small]
        out[k, d:, :LANES] = rows[...].astype(bf16)
        out[k, d:, LANES:] = jnp.zeros((GAIN_ROWS, width + od - LANES), bf16)


def load_chunks(N, pieces, extra, chunks, w, down, sems):
    d = w.shape[0] // N
    piece = down.shape[0] // N
    copies = []

    def copy(source, target):
        copies.append(pltpu.make_async_copy(source, target, sems.at[len(copies)]))
        copies[-1].start()

    for ref, (k, first, rows) in zip(chunks, pieces):
        s = ring_owner(k, N)
        count = min(d - first, rows)
        copy(ref.at[:count], w.at[pl.ds(aligned(s * d + first, 16), count)])
        if extra and first + rows > d:
            for row, col, at, left, many, cols in folds(extra, down.shape[1]):
                copy(
                    ref.at[count + row : count + row + many, col : col + cols],
                    down.at[pl.ds(aligned(s * piece + at, 16), many), left : left + cols],
                )
    for c in copies:
        c.wait()


def feed_kernel(N, many, pieces, extra, *refs):
    mids, cots, refs = refs[:many], refs[many : 2 * many], refs[2 * many :]
    if pieces:
        chunks, refs = refs[: len(pieces)], refs[len(pieces) :]
        if not extra:
            down, refs = refs[0], refs[1:]
            hidden, both, *outs, w, sems = refs
        else:
            hidden, both, *outs, w, down, sems = refs
        load_chunks(N, pieces, extra, chunks, w, down, sems)
    else:
        w, down, hidden, both, *outs = refs
    T = mids[0].shape[0]
    FQ = down.shape[0]
    step = FQ // 3
    for j in range(many):
        rows = slice(j * T, (j + 1) * T)
        x = mids[j][...]
        c = cots[j][...]
        for first in range(0, FQ, step):
            cols = slice(first, first + step)
            gate = dot(x, w[:, cols])
            upper = dot(x, w[:, FQ + first : FQ + first + step])
            grad = times_t(c, down[cols])
            sigmoid = 1.0 / (1.0 + jnp.exp(-gate))
            swish = gate * sigmoid
            hidden[rows, cols] = (swish * upper).astype(bf16)
            both[rows, cols] = (grad * sigmoid * upper * (1.0 + gate - swish)).astype(bf16)
            both[rows, FQ + first : FQ + first + step] = (grad * swish).astype(bf16)
        outs[j][...] = times_t(both[rows], w[...]).astype(outs[j].dtype)


def both_grad_kernel(S, N, slots, extra, *refs):
    mids, near, far, folded = refs[:S], refs[S], refs[S + 1], refs[S + 2]
    outs, left = refs[S + 3 : -1], refs[-1]
    T, D = mids[0].shape
    d = D // N
    half = S // 2 * T
    width = near.shape[1]
    for r in range(S):
        rows = slice(r * T, (r + 1) * T)
        x = None if d % LANES == 0 else mids[r][...].astype(f32)
        for j, k in enumerate(slots):
            s = ring_owner(k, N)
            if x is None:
                part = mids[r][:, pl.ds(aligned(s * d, LANES), d)]
            else:
                moved = pltpu.roll(x, jnp.where(s == 0, 0, D - s * d), 1)
                part = moved[:, :d].astype(bf16)
            left[rows, j * d : (j + 1) * d] = part
    step = width // 3
    for first in range(0, width, step):
        cols = slice(first, first + step)
        g = t_times(left[:half], near[:, cols]) + t_times(left[half:], far[:, cols])
        held = list(outs)
        for j, k in enumerate(slots):
            at = j * d
            while at < (j + 1) * d:
                out = held.pop(0)
                count = min(out.shape[0], (j + 1) * d - at)
                out[:count, cols] = g[at : at + count].astype(bf16)
                at += count
            if extra:
                out[count:, cols] = folded[k, :, cols]


def down_grad_kernel(S, N, extra, near, far, *refs):
    cots, (out, cot) = refs[:S], refs[S:]
    T = cots[0].shape[0]
    half = S // 2 * T
    for r in range(S):
        cot[r * T : (r + 1) * T] = cots[r][...]
    D = cot.shape[1]
    piece = near.shape[1] // N
    step = D // 2
    for first in range(0, D, step):
        cols = slice(first, first + step)
        g = t_times(near[...], cot[:half, cols]) + t_times(far[...], cot[half:, cols])
        for s in range(N):
            part = g[s * piece : (s + 1) * piece].astype(bf16)
            if not extra:
                out[s, :, cols] = part
                continue
            k = ring_slot(s, N)
            for row, col, at, left, rows, many in folds(extra, D):
                low, high = max(left, first), min(left + many, first + step)
                if low < high:
                    out[k, row : row + rows, col + low - left : col + high - left] = part[
                        at : at + rows, low - first : high - first
                    ]


def load_blocks(blocks, held, sems):
    Q = lax.axis_index("seq")
    copies = []
    for r, ref in enumerate(blocks):
        copies.append(
            pltpu.make_async_copy(ref, held.at[jnp.bitwise_xor(Q, r)], sems.at[r])
        )
        copies[-1].start()
    for c in copies:
        c.wait()


def both_out_kernel(S, N, extra, *refs):
    blocks, (gate, up, *down, held, sems) = refs[:S], refs[S:]
    load_blocks(blocks, held, sems)
    d = gate.shape[0]
    piece = gate.shape[1] // N // S
    for q in range(S):
        for base, out in ((0, gate), (N * piece, up)):
            for s in range(N):
                out[:, (s * S + q) * piece : (s * S + q + 1) * piece] = held[
                    q, :d, base + s * piece : base + (s + 1) * piece
                ].astype(f32)
        if extra:
            for row, col, at, left, rows, cols in folds(extra, down[0].shape[1]):
                down[0][q * piece + at : q * piece + at + rows, left : left + cols] = held[
                    q, d + row : d + row + rows, col : col + cols
                ].astype(f32)


def down_out_kernel(S, *refs):
    blocks, (out, held, sems) = refs[:S], refs[S:]
    load_blocks(blocks, held, sems)
    piece = held.shape[1]
    for q in range(S):
        out[q * piece : (q + 1) * piece] = held[q].astype(f32)


def pack_out_kernel(S, N, qd, kd, *refs):
    blocks, refs = refs[:S], refs[S:]
    outs, (pre, post, qgain, kgain, held, sems) = refs[:4], refs[4:]
    load_blocks(blocks, held, sems)
    d = outs[0].shape[0]
    od = outs[3].shape[1] // S
    at = 0
    for out, width in zip(outs, (qd, kd, kd, od)):
        for q in range(S):
            out[:, q * width : (q + 1) * width] = held[q, :d, at : at + width].astype(f32)
        at += width
    rows = held[0, d:, :LANES].astype(f32)
    for q in range(1, S):
        rows += held[q, d:, :LANES].astype(f32)
    for i, ref in enumerate((pre, post, qgain, kgain)):
        ref[...] = rows[i : i + 1, : ref.shape[1]]


def per_device(
    tokens,
    doc_starts,
    pre_gain,
    query_weight,
    key_matrix,
    value_matrix,
    query_gain,
    key_gain,
    out_weight,
    post_gain,
    gate_weight,
    up_weight,
    down_weight,
    cotangent,
):
    S = lax.axis_size("seq")
    N = lax.axis_size("shard")
    Q = lax.axis_index("seq")
    T, D = tokens.shape[1:]
    L = S * T
    d = D // N
    od = D // S
    qd = QUERY_HEADS * HEAD_SIZE // S
    kd = KEY_VALUE_HEADS * HEAD_SIZE // S
    width = qd + 2 * kd
    heads = kd // HEAD_SIZE
    FF = gate_weight.shape[1]
    piece = FF // N // S
    FQ = FF // S
    extra = fold_rows(piece, D, 2 * FQ)
    near, far = list(range(S // 2)), list(range(S // 2, S))
    dma = pltpu.SemaphoreType.DMA


    def swap(x, step):
        return lax.ppermute(x, "seq", [(i, i ^ step) for i in range(S)])

    def gather_seq(x):
        blocks = {0: x}
        step = S // 2
        while step:
            for r in list(blocks):
                blocks[r + step] = swap(blocks[r], step)
            step //= 2
        return [blocks[r] for r in range(S)]

    def block_shapes(blocks):
        return [shape((T, D), bf16 if r % 2 else f32) for r in blocks]

    order = ring_order(N)

    def hop(x, way):
        return lax.ppermute(x, "shard", [(order[i], order[(i + way) % N]) for i in range(N)])

    def after(x, *others):
        return lax.optimization_barrier((x, *others))[0]

    def pair(up, down):
        return lax.optimization_barrier((hop(up, 1), hop(down, -1)))


    def quarters(step):
        many = N // 2

        def quarter(i, *others):
            at = None
            for k in range(i * many // 4, (i + 1) * many // 4):
                at = step(k + 1, others)
            return at

        return quarter

    def gather_ring(x):
        half = x.shape[0] // 32 * 16
        chunks = [x]

        def step(k, others):
            up, down = chunks[-2:] if k > 1 else (x, x)
            if k == N // 2:
                up, down = up[:half], down[half:]
            up, down, *_ = lax.optimization_barrier((up, down, *others))
            chunks.extend(pair(up, down))
            return chunks[-1]

        return chunks, quarters(step)

    def scatter_ring(x, halves):
        half = halves[0].shape[0]
        moved = [*halves]
        sent = [*halves]

        def step(k, others):
            up, down = moved
            at = N // 2 + 1 - k
            if k > 1:
                ahead, behind = x[at].astype(f32), x[N - at].astype(f32)
                if k == 2:
                    ahead = jnp.concatenate([ahead[:half] + up.astype(f32), ahead[half:]], axis=0)
                    behind = jnp.concatenate(
                        [behind[:half], behind[half:] + down.astype(f32)], axis=0
                    )
                else:
                    ahead, behind = ahead + up.astype(f32), behind + down.astype(f32)
                up, down = ahead.astype(bf16), behind.astype(bf16)
            sent[:] = up, down
            up, down, *_ = lax.optimization_barrier((up, down, *others))
            moved[:] = pair(up, down)
            return moved[0]

        def total():
            return (x[0].astype(f32) + moved[0].astype(f32) + moved[1].astype(f32)).astype(bf16)

        return total, quarters(step), sent

    def partial_sum(blocks, low, size):
        if size == 2:
            return blocks[low] + swap(blocks[low + 1], 1).astype(f32)
        half = size // 2
        moved = swap(partial_sum(blocks, low + half, half).astype(bf16), half)
        return partial_sum(blocks, low, half) + moved.astype(f32)

    def far_part(blocks):
        return partial_sum([None] * len(near) + blocks, S // 2, S // 2).astype(bf16)

    (pack,) = call(
        functools.partial(pack_kernel, qd, kd, od),
        "v" * 8,
        (
            query_weight,
            key_matrix,
            value_matrix,
            out_weight,
            pre_gain[None],
            post_gain[None],
            query_gain[None],
            key_gain[None],
        ),
        [shape((d + GAIN_ROWS, width + od), bf16)],
        "v",
        [pltpu.VMEM((GAIN_ROWS, LANES), f32)],
        "pack",
    )
    pack_chunks, pack_ring = gather_ring(pack)
    pack_1 = pack_ring(0)
    local = tokens[0]
    xs = gather_seq(local)
    (both_columns,) = call(
        functools.partial(columns_kernel, S, N, piece, extra),
        "vvv",
        (after(gate_weight, pack), up_weight, down_weight),
        [shape((d + extra, 2 * FQ), bf16)],
        "v",
        [],
        "columns",
    )
    pack_2 = pack_ring(1, both_columns)
    starts = doc_starts[0]
    blocks_at = jnp.arange(S, dtype=jnp.int32) ^ Q
    places = (blocks_at[:, None] * T + jnp.arange(T, dtype=jnp.int32)[None, :]).reshape(L)
    cosine, sine = rope_tables(inside_of(after(starts, pack_1), places))
    cot = cotangent[0]
    cots = gather_seq(after(cot, pack_2))
    both_chunks, both_ring = gather_ring(both_columns)
    pack_ring(2, cosine, sine)
    pack_ring(3)
    both_1 = both_ring(0, pack_chunks[-1])
    both_pieces = arrived(N, d + extra)
    downs = []
    if not extra:
        own_rows = lax.dynamic_slice(
            down_weight, (Q * piece, 0), (piece, D), allow_negative_indices=False
        )
        downs = [lax.all_gather(own_rows, "shard", axis=0, tiled=True)]

    w_qkv, out_parts, gains = call(
        functools.partial(assemble_kernel, N, d, width, qd, od),
        "v" * len(pack_chunks),
        pack_chunks,
        [shape((D, width), bf16), shape((S, qd, od), bf16), shape((8, D), f32)],
        "vvv",
        [],
        "assemble",
    )
    out_blocks = [out_parts[0]] + [swap(out_parts[r], r) for r in range(1, S)]

    normed_in, proj, rotated, attended, stats = call(
        functools.partial(forward_kernel, S, qd, kd),
        "s" + "v" * (S + 4),
        (starts, *xs, after(w_qkv, cots[S // 2]), gains, cosine, sine),
        [
            shape((L, D), bf16),
            shape((L, -(-(qd + kd) // LANES) * LANES), f32),
            shape((L, width), bf16),
            shape((L, qd), bf16),
            shape((max(8, qd // HEAD_SIZE), L), f32),
        ],
        "v" * 5,
        [pltpu.VMEM((L, LANES), bf16), pltpu.VMEM((L, 2 * LANES), bf16)],
        "attend",
    )

    both_2 = both_ring(1)

    def project(blocks, whole):
        return call(
            functools.partial(out_kernel, S, blocks, whole),
            "v" * (S + 1),
            (attended, *out_blocks),
            block_shapes(blocks) + ([shape((qd, D), bf16)] if whole else []),
            "v" * (len(blocks) + whole),
            [],
            "project",
        )

    far_blocks = project(far, False)
    *near_blocks, full_out = project(near, True)
    far_sum = far_part(far_blocks)
    near_blocks[0] = after(near_blocks[0], both_2)
    both_ring(2)
    middle = (
        local.astype(f32)
        + partial_sum(near_blocks, 0, S // 2)
        + swap(far_sum, S // 2).astype(f32)
    )

    full_post = gains[1]
    root_mid = inverse_root(middle)
    scaled_mid = middle * root_mid
    normed_mid = (scaled_mid * full_post).astype(bf16)
    both_ring(3, normed_mid)
    mids = gather_seq(normed_mid)
    def feed(blocks, first, weights, pieces):
        rows = len(blocks) * T
        made = []
        if pieces:
            made = [shape((D, 2 * FQ), bf16)] + [shape((FQ, D), bf16)] * (extra > 0)
        return call(
            functools.partial(feed_kernel, N, len(blocks), pieces, extra),
            "v" * (2 * len(blocks))
            + ("a" * len(pieces) + "v" * (len(weights) - len(pieces)) if pieces else "vv"),
            (first, *[mids[r] for r in blocks[1:]], *[cots[r] for r in blocks], *weights),
            [shape((rows, FQ), bf16), shape((rows, 2 * FQ), bf16)] + block_shapes(blocks) + made,
            "v" * (2 + len(blocks) + len(made)),
            [dma((len(pieces) + 6 * N,))] if pieces else [],
            "feed",
        )

    hidden_far, both_far, *grads_far = feed(
        far, mids[far[0]], both_chunks + downs, both_pieces
    )
    if extra:
        downs = [grads_far.pop()]
    full_both = grads_far.pop()
    far_sum = far_part(grads_far)
    hidden_near, both_near, *grads_near = feed(
        near, after(mids[near[0]], far_sum), [full_both] + downs, []
    )
    far_moved = swap(far_sum, S // 2)
    term_both = {}
    split = (d + extra) // 32 * 16
    (term_down,) = call(
        functools.partial(down_grad_kernel, S, N, extra),
        "v" * (S + 2),
        (hidden_near, hidden_far, *cots),
        [shape((N, extra, 2 * FQ) if extra else (N, piece, D), bf16)],
        "v",
        [pltpu.VMEM((L, D), bf16)],
        "down_grad",
    )

    def both_grads(slots, side):
        rows = []
        for k in slots:
            rows += [split, d + extra - split] if k == N // 2 else [d + extra]
        terms = call(
            functools.partial(both_grad_kernel, S, N, slots, extra),
            "v" * (S + 3),
            (*mids, side, both_far, term_down),
            [shape((many, 2 * FQ), bf16) for many in rows],
            "v" * len(rows),
            [pltpu.VMEM((L, len(slots) * d), bf16)],
            "both_grad",
        )
        if slots[0] == N // 2:
            term_both[N // 2] = terms[:2]
            terms, slots = terms[2:], slots[1:]
        term_both.update(zip(slots, terms))
        return terms[0]

    middle_slots = [N // 2, N // 2 - 1, N // 2 + 1]
    grads_near[0] = after(grads_near[0], term_down)
    grad_nmid = partial_sum(grads_near, 0, S // 2) + far_moved.astype(f32)
    term_post = jnp.sum(grad_nmid * scaled_mid, axis=0)
    grad_middle = cot.astype(f32) + norm_back(grad_nmid * full_post, middle, root_mid)
    grad_branch = grad_middle.astype(bf16)
    first_terms = both_grads(middle_slots, after(both_near, grad_branch))
    both_total, both_back, both_sent = scatter_ring(term_both, term_both[N // 2])
    both_back(0)
    last_terms = both_grads(
        [k for k in range(N) if k not in middle_slots], after(both_near, first_terms)
    )
    both_back(1, last_terms)
    second = tuple(both_sent)
    output_blocks = []
    for hidden, blocks in ((after(hidden_near, *second), near), (hidden_far, far)):
        product = dot(hidden, downs[0])
        for j, r in enumerate(blocks):
            block = product[j * T : (j + 1) * T]
            output_blocks.append(block.astype(bf16) if r % 2 else block)

    out_sum = far_part(output_blocks[len(near) :])
    out_moved = swap(out_sum, S // 2)

    gbs = gather_seq(grad_branch)
    out_terms = call(
        functools.partial(out_grad_kernel, S),
        "v" * (S + 1),
        (attended, *gbs),
        [shape((qd, od), bf16)] * S,
        "v" * S,
        [pltpu.VMEM((qd, D), f32)],
        "out_grad",
    )
    first_gb = after(gbs[0], *second, out_terms[0], out_sum)
    grad_proj, sums = call(
        functools.partial(backward_kernel, S, qd, kd),
        "s" + "v" * (S + 8),
        (starts, first_gb, *gbs[1:], full_out, rotated, proj, attended, stats, gains, cosine, sine),
        [shape((L, width), bf16), shape((8, LANES), f32)],
        "vv",
        [
            pltpu.VMEM((L, qd), bf16),
            pltpu.VMEM((8 * heads, L), f32),
            pltpu.VMEM((L, LANES), bf16),
            pltpu.VMEM((LANES, L), bf16),
            pltpu.VMEM((L, LANES), bf16),
            pltpu.VMEM((heads, L, LANES), f32),
            pltpu.VMEM((heads, L, LANES), f32),
        ],
        "attend_back",
    )

    both_back(2, grad_proj)
    third = tuple(both_sent)
    back_4 = both_back(3)
    output_blocks[0] = after(output_blocks[0], grad_proj)
    output = middle + partial_sum(output_blocks, 0, S // 2) + out_moved.astype(f32)
    out_terms = [out_terms[0]] + [swap(out_terms[r], r) for r in range(1, S)]
    grad_proj = after(grad_proj, *third, out_moved, *out_terms[1:])

    def input_grads(blocks):
        return call(
            functools.partial(input_grad_kernel, blocks),
            "v" * (2 + len(blocks)),
            (grad_proj, w_qkv, *[xs[r] for r in blocks]),
            block_shapes(blocks) + [shape((8, D), f32)],
            "v" * (len(blocks) + 1),
            [],
            "input_grad",
        )

    *nins_far, pre_far = input_grads(far)
    *nins_near, pre_near = input_grads(near)
    nin_sum = far_part(nins_far)
    nin_moved = swap(nin_sum, S // 2)
    grad_nin = partial_sum(nins_near, 0, S // 2) + nin_moved.astype(f32)
    wide = local.astype(f32)
    grad_tokens = grad_middle + norm_back(grad_nin * gains[0], wide, inverse_root(wide))

    (pack_terms,) = call(
        functools.partial(pack_grad_kernel, S, N),
        "v" * (6 + S),
        (
            after(normed_in, nin_moved),
            grad_proj,
            sums,
            pre_near,
            pre_far,
            term_post[None],
            *out_terms,
        ),
        [shape((N, d + GAIN_ROWS, width + od), bf16)],
        "v",
        [pltpu.VMEM((D, od), bf16), pltpu.VMEM((GAIN_ROWS, LANES), f32)],
        "pack_grad",
    )
    split = (d + GAIN_ROWS) // 32 * 16
    pack_total, pack_back, _ = scatter_ring(
        pack_terms, (pack_terms[N // 2, :split], pack_terms[N // 2, split:])
    )
    pack_back(0, back_4)
    pack_back(1)
    pack_back(2)
    pack_back(3)

    gate_grad, up_grad, *down_grad = call(
        functools.partial(both_out_kernel, S, N, extra),
        "a" * S,
        gather_seq(both_total()),
        [shape((d, FF), f32), shape((d, FF), f32)] + [shape((S * piece, D), f32)] * (extra > 0),
        "vv" + "v" * (extra > 0),
        [pltpu.VMEM((S, d + extra, 2 * FQ), bf16), dma((S,))],
        "both_out",
    )
    if not extra:
        shard_down = lax.psum_scatter(
            term_down.reshape(FQ, D), "shard", scatter_dimension=0, tiled=True
        )
        down_grad = call(
            functools.partial(down_out_kernel, S),
            "a" * S,
            gather_seq(shard_down),
            [shape((S * piece, D), f32)],
            "v",
            [pltpu.VMEM((S, piece, D), bf16), dma((S,))],
            "down_out",
        )
    pack_blocks = gather_seq(pack_total())
    for r in range(1, S // 2):
        pack_blocks[S // 2 + r] = swap(after(pack_blocks[S // 2], gate_grad), r)
    small = HEAD_SIZE // N
    q_grad, k_grad, v_grad, o_grad, pre_grad, post_grad, qgain_grad, kgain_grad = call(
        functools.partial(pack_out_kernel, S, N, qd, kd),
        "a" * S,
        pack_blocks,
        [
            shape((d, S * qd), f32),
            shape((d, S * kd), f32),
            shape((d, S * kd), f32),
            shape((d, D), f32),
            shape((1, d), f32),
            shape((1, d), f32),
            shape((1, small), f32),
            shape((1, small), f32),
        ],
        "v" * 8,
        [pltpu.VMEM((S, d + GAIN_ROWS, width + od), bf16), dma((S,))],
        "pack_out",
    )
    return (
        output.astype(bf16)[None],
        grad_tokens[None],
        pre_grad[0],
        q_grad,
        k_grad,
        v_grad,
        qgain_grad[0],
        kgain_grad[0],
        o_grad,
        post_grad[0],
        gate_grad,
        up_grad,
        down_grad[0],
    )


def solution(mesh):
    row, vector, matrix = P("shard", "seq", None), P("shard"), P("shard", None)
    return jax.shard_map(
        per_device,
        mesh=mesh,
        in_specs=(
            row,
            matrix,
            vector,
            matrix,
            matrix,
            matrix,
            vector,
            vector,
            matrix,
            vector,
            matrix,
            matrix,
            matrix,
            row,
        ),
        out_specs=(
            row,
            row,
            vector,
            matrix,
            matrix,
            matrix,
            vector,
            vector,
            matrix,
            vector,
            matrix,
            matrix,
            matrix,
        ),
        check_vma=False,
    )
```

```python
import functools
import math

import jax
import jax.numpy as jnp
from jax import lax
from jax.experimental import pallas as pl
from jax.experimental.pallas import tpu as pltpu
from jax.sharding import PartitionSpec as P

QUERY_HEADS = 16
KEY_VALUE_HEADS = 8
HEAD_SIZE = 64
GROUP = QUERY_HEADS // KEY_VALUE_HEADS
LANES = 128
GAIN_ROWS = 16
SCALE = HEAD_SIZE ** (-0.5)
SCALE2 = SCALE * math.log2(math.e)


eps_norm = 1e-05
rope_base = 1000000.0

bf16 = jnp.bfloat16
f32 = jnp.float32
shape = jax.ShapeDtypeStruct


def dot(left, right):
    return jnp.dot(left, right, preferred_element_type=f32)


def times_t(left, right):
    return lax.dot_general(left, right, (((1,), (1,)), ((), ())), preferred_element_type=f32)


def t_times(left, right):
    return lax.dot_general(left, right, (((0,), (0,)), ((), ())), preferred_element_type=f32)


def inverse_root(value_tokens):
    return lax.rsqrt(jnp.mean(value_tokens * value_tokens, axis=-1, keepdims=True) + eps_norm)


def norm_back(grad_scaled, value_tokens, root):
    return root * (
        grad_scaled
        - value_tokens
        * (root * root)
        * jnp.mean(grad_scaled * value_tokens, axis=-1, keepdims=True)
    )


def rope_tables(places):
    half = HEAD_SIZE // 2
    lane = jnp.arange(LANES, dtype=jnp.int32) % HEAD_SIZE
    inverse = jnp.exp((lane % half).astype(f32) * (-2.0 * math.log(rope_base) / HEAD_SIZE))
    angle = places.astype(f32)[:, None] * inverse[None, :]
    sine = jnp.sin(angle)
    return (jnp.cos(angle), jnp.where(lane < half, -sine, sine))


def inside_of(starts, places):
    before = starts[None, :] <= places[:, None]
    return places - jnp.max(jnp.where(before, starts[None, :], 0), axis=1)


def ring_grid(N):
    Z = min(N, 4)
    return Z, N // Z


def ring_order(N):
    Z, X = ring_grid(N)
    order = [z * X for z in range(Z)]
    for row in range(Z):
        line = [(Z - 1 - row) * X + x for x in range(1, X)]
        order += line if row % 2 == 0 else line[::-1]
    return order


def ring_place(at, N):
    Z, X = ring_grid(N)
    if X == 1:
        return at
    if X == 2:
        return jnp.where(at < Z, at * 2, (2 * Z - 1 - at) * 2 + 1)
    row, column = lax.div(at - Z, X - 1), lax.rem(at - Z, X - 1)
    x = jnp.where(lax.rem(row, 2) == 0, 1 + column, X - 1 - column)
    return jnp.where(at < Z, at * X, (Z - 1 - row) * X + x)


def ring_position(s, N):
    Z, X = ring_grid(N)
    z, x = lax.div(s, X), lax.rem(s, X)
    if X == 1:
        return z
    if X == 2:
        return jnp.where(x == 0, z, 2 * Z - 1 - z)
    row = Z - 1 - z
    turn = jnp.where(lax.rem(row, 2) == 0, x - 1, X - 1 - x)
    return jnp.where(x == 0, z, Z + row * (X - 1) + turn)


def ring_owner(k, N):
    at = ring_position(lax.axis_index("shard"), N) + k % N
    return ring_place(jnp.where(at >= N, at - N, at), N)


def ring_slot(s, N):
    at = ring_position(jnp.int32(s), N) - ring_position(lax.axis_index("shard"), N)
    return jnp.where(at < 0, at + N, at)


def arrived(N, rows):
    half = rows // 32 * 16
    pieces = [(0, 0, rows)]
    for k in range(1, N // 2):
        pieces += [(N - k, 0, rows), (k, 0, rows)]
    return pieces + [(N // 2, 0, half), (N // 2, half, rows - half)]


def call(kernel, spaces, inputs, outputs, out_spaces, scratch, name):
    places = {
        "s": pl.BlockSpec(memory_space=pltpu.SMEM),
        "v": pl.BlockSpec(memory_space=pltpu.VMEM),
        "a": pl.BlockSpec(memory_space=pl.ANY),
    }
    return list(pl.pallas_call(
        kernel,
        out_shape=list(outputs),
        in_specs=[places[c] for c in spaces],
        out_specs=[places[c] for c in out_spaces],
        scratch_shapes=scratch,
        compiler_params=pltpu.CompilerParams(vmem_limit_bytes=56 * 2**20),
        cost_estimate=pl.CostEstimate(
            flops=1, bytes_accessed=1, transcendentals=0
        ),
        name=name,
    )(*inputs))


def aligned(start, unit):
    return pl.multiple_of(start, unit)


def column_block(ref, index, width):
    if width % LANES == 0:
        return ref[:, pl.ds(aligned(index * width, LANES), width)]
    tile = ref[:, pl.ds(aligned(lax.div(index * width, LANES) * LANES, LANES), LANES)].astype(f32)
    moved = pltpu.roll(tile, LANES - lax.rem(index * width, LANES), 1)
    return moved[:, :width].astype(bf16)


def pack_kernel(qd, kd, od, wq, wk, wv, wo, pre, post, qgain, kgain, out, rows):
    Q = lax.axis_index("seq")
    d = wq.shape[0]
    at = 0
    for ref, width in ((wq, qd), (wk, kd), (wv, kd), (wo, od)):
        out[:d, at : at + width] = column_block(ref, Q, width)
        at += width
    rows[...] = jnp.zeros_like(rows)
    for i, ref in enumerate((pre, post, qgain, kgain)):
        rows[i : i + 1, : ref.shape[1]] = ref[...].astype(f32)
    out[d:, :LANES] = rows[...].astype(bf16)
    out[d:, LANES:] = jnp.zeros((GAIN_ROWS, at - LANES), bf16)


def fold_rows(piece, D, width):
    extra = 64
    fits = piece == 2 * extra + extra // 4 and width == 2 * D + D // 4
    return extra if fits else 0


def folds(extra, D):
    parts = [(0, 0, 0, 0, extra, D), (0, D, extra, 0, extra, D)]
    for c in range(4):
        parts.append((c * extra // 4, 2 * D, 2 * extra, c * D // 4, extra // 4, D // 4))
    return parts


def columns_kernel(S, N, piece, extra, gate, up, down, out):
    Q = lax.axis_index("seq")
    d = gate.shape[0]
    for q in range(S):

        @pl.when(Q == q)
        def _():
            for base, ref in ((0, gate), (N * piece, up)):
                for s in range(N):
                    out[:d, base + s * piece : base + (s + 1) * piece] = ref[
                        :, (s * S + q) * piece : (s * S + q + 1) * piece
                    ]

    if extra:
        for row, col, at, first, rows, cols in folds(extra, down.shape[1]):
            out[d + row : d + row + rows, col : col + cols] = down[
                pl.ds(aligned(Q * piece + at, 16), rows), first : first + cols
            ]


def assemble_kernel(N, d, width, qd, od, *refs):
    pieces = arrived(N, d + GAIN_ROWS)
    chunks, (w, outs, gains) = refs[: len(pieces)], refs[len(pieces) :]
    Q = lax.axis_index("seq")
    gains[...] = jnp.zeros_like(gains)
    lane = lax.broadcasted_iota(jnp.int32, (GAIN_ROWS, LANES), 1)
    for ref, (k, first, rows) in zip(chunks, pieces):
        s = ring_owner(k, N)
        count = min(d - first, rows)
        to = s * d + first
        w[pl.ds(aligned(to, 16), count)] = ref[:count, :width]
        r = jnp.bitwise_xor(lax.div(to, qd), Q)
        outs[r, pl.ds(aligned(lax.rem(to, qd), 16), count)] = ref[:count, width : width + od]
        if first + rows > d:
            tile = ref[count:, :LANES].astype(f32)
            for row, many in ((0, d), (1, d), (2, HEAD_SIZE // N), (3, HEAD_SIZE // N)):
                at = s * many
                moved = pltpu.roll(jnp.where(lane < many, tile, 0.0), lax.rem(at, LANES), 1)
                where = pl.ds(aligned(lax.div(at, LANES) * LANES, LANES), LANES)
                gains[row : row + 1, where] += moved[row : row + 1]
    for row in (2, 3):
        x = gains[row : row + 1, :LANES]
        gains[row : row + 1, :LANES] = x + pltpu.roll(x, HEAD_SIZE, 1)


def group_ones():
    across = lax.broadcasted_iota(jnp.int32, (LANES, LANES), 0) // HEAD_SIZE
    down = lax.broadcasted_iota(jnp.int32, (LANES, LANES), 1) // HEAD_SIZE
    return jnp.where(across == down, 1.0 / HEAD_SIZE, 0.0).astype(bf16)


def split_dot(x, ones):
    high = x.astype(bf16)
    return dot(high, ones) + dot((x - high.astype(f32)).astype(bf16), ones)


def turned(x, low_half):
    half = HEAD_SIZE // 2
    return jnp.where(low_half, pltpu.roll(x, LANES - half, 1), pltpu.roll(x, half, 1))


def begins(starts, places):
    begin = jnp.zeros_like(places)
    for start in starts:
        begin = jnp.maximum(begin, jnp.where(places >= start, start, 0))
    return begin


def masked_exp2(x, begin, qpos, before, axis):
    parts = []
    for first, last in ((0, before), (before, x.shape[axis])):
        if first == last:
            continue
        part = lax.slice_in_dim(x, first, last, axis=axis)
        kpos = first + lax.broadcasted_iota(jnp.int32, part.shape, axis)
        ok = kpos >= begin
        if first == before:
            ok = ok & (kpos <= qpos)
        parts.append(jnp.where(ok, jnp.exp2(part), 0.0))
    return jnp.concatenate(parts, axis=axis) if len(parts) > 1 else parts[0]


def spread(x, half, low):
    moved = pltpu.roll(x, HEAD_SIZE, 1)
    return jnp.where(low, moved, x) if half else jnp.where(low, x, moved)


def head_tile(ref, at, low):
    first = at // LANES * LANES
    return spread(ref[:, first : first + LANES], at % LANES // HEAD_SIZE, low)


def forward_kernel(S, qd, kd, starts_ref, *refs):
    xs = refs[:S]
    (w_ref, gains_ref, cos_ref, sin_ref) = refs[S : S + 4]
    (nin_ref, proj_ref, rot_ref, att_ref, stat_ref, wide_ref, both_ref) = refs[S + 4 :]
    T = xs[0].shape[0]
    L = S * T
    heads = kd // HEAD_SIZE
    Q = lax.axis_index("seq")
    starts = [starts_ref[i] for i in range(starts_ref.shape[0])]
    ones = group_ones()
    lane = lax.broadcasted_iota(jnp.int32, (T, LANES), 1)
    low = lane < HEAD_SIZE
    low_half = lane % HEAD_SIZE < HEAD_SIZE // 2
    for r in range(S):
        rows = slice(r * T, (r + 1) * T)
        at = pl.ds(aligned(jnp.bitwise_xor(Q, r) * T, T), T)
        x = xs[r][...].astype(f32)
        nin = (x * inverse_root(x) * gains_ref[0:1]).astype(bf16)
        nin_ref[rows] = nin
        proj = dot(nin, w_ref[...])
        cos, sin = cos_ref[rows], sin_ref[rows]
        for first in range(0, qd + 2 * kd, LANES):
            cols = slice(first, first + LANES)
            tile = proj[:, cols]
            if first < qd + kd:
                proj_ref[at, cols] = tile
                gain = gains_ref[2:3, :LANES] if first < qd else gains_ref[3:4, :LANES]
                y = tile * lax.rsqrt(split_dot(tile * tile, ones) + eps_norm) * gain
                y = y * cos + turned(y, low_half) * sin
                if first + LANES > qd + kd:
                    y = jnp.where(low, y, tile)
                tile = y
            rot_ref[at, cols] = tile.astype(bf16)
    low_all = lax.broadcasted_iota(jnp.int32, (L, LANES), 1) < HEAD_SIZE
    for n in range(heads):
        wide_ref[...] = head_tile(rot_ref, qd + n * HEAD_SIZE, low_all)
        both_ref[:, :LANES] = head_tile(rot_ref, qd + kd + n * HEAD_SIZE, low_all)
        both_ref[:, LANES:] = jnp.ones((L, LANES), bf16)
        cols = slice(n * LANES, (n + 1) * LANES)
        for i in range(S):
            count = (i + 1) * T
            q = rot_ref[i * T : count, cols]
            zero = jnp.zeros_like(q)
            q2 = jnp.concatenate([jnp.where(low, q, zero), jnp.where(low, zero, q)], axis=0)
            s = times_t(q2, wide_ref[:count])
            qpos = i * T + lax.broadcasted_iota(jnp.int32, (T, 1), 0)
            qpos = jnp.concatenate([qpos, qpos], axis=0)
            e = masked_exp2(s * SCALE2, begins(starts, qpos), qpos, i * T, 1).astype(bf16)
            o = dot(e, both_ref[:count])
            total = o[:, LANES:]
            out = o[:, :LANES] / total
            att_ref[pl.ds(aligned(jnp.bitwise_xor(Q, i) * T, T), T), cols] = jnp.where(
                low, out[:T], out[T:]
            ).astype(bf16)
            logs = jnp.log2(total)
            for a in range(GROUP):
                stat_ref[n * GROUP + a : n * GROUP + a + 1, i * T : count] = (
                    logs[a * T : (a + 1) * T].T[:1]
                )


def out_kernel(S, blocks, whole, att_ref, *refs):
    weights, outs = refs[:S], refs[S:]
    T = outs[0].shape[0]
    od = weights[0].shape[1]
    Q = lax.axis_index("seq")
    for j, r in enumerate(blocks):
        a = att_ref[r * T : (r + 1) * T]
        for c in range(S):
            cols = pl.ds(aligned(jnp.bitwise_xor(Q, c) * od, LANES), od)
            outs[j][:, cols] = dot(a, weights[c][...]).astype(outs[j].dtype)
    if whole:
        for c in range(S):
            cols = pl.ds(aligned(jnp.bitwise_xor(Q, c) * od, LANES), od)
            outs[-1][:, cols] = weights[c][...]


def backward_kernel(S, qd, kd, starts_ref, *refs):
    gbs = refs[:S]
    (wo_ref, rot_ref, proj_ref, att_ref, stat_ref, gains_ref, cos_ref, sin_ref) = refs[S : S + 8]
    (grad_ref, sums_ref, do_ref, delta_ref, k_ref, kt_ref, v_ref, dk_ref, dv_ref) = refs[S + 8 :]
    T = gbs[0].shape[0]
    L = S * T
    heads = kd // HEAD_SIZE
    Q = lax.axis_index("seq")
    starts = [starts_ref[i] for i in range(starts_ref.shape[0])]
    ones = group_ones()
    lane = lax.broadcasted_iota(jnp.int32, (T, LANES), 1)
    low = lane < HEAD_SIZE
    low_half = lane % HEAD_SIZE < HEAD_SIZE // 2
    picks = (
        lax.broadcasted_iota(jnp.int32, (8, LANES), 0)
        == lax.broadcasted_iota(jnp.int32, (8, LANES), 1) // HEAD_SIZE
    ).astype(bf16)
    sums_ref[...] = jnp.zeros_like(sums_ref)
    for r in range(S):
        rows = slice(r * T, (r + 1) * T)
        at = pl.ds(aligned(jnp.bitwise_xor(Q, r) * T, T), T)
        grads = times_t(gbs[r][...], wo_ref[...]).astype(bf16)
        do_ref[at] = grads
        for n in range(heads):
            cols = slice(n * LANES, (n + 1) * LANES)
            x = grads[:, cols].astype(f32) * att_ref[rows, cols].astype(f32)
            high = x.astype(bf16)
            rest = (x - high.astype(f32)).astype(bf16)
            delta_ref[n * 8 : n * 8 + 8, at] = times_t(picks, high) + times_t(picks, rest)

    def finish(g, rows, at, cols, gain):
        g = g * cos_ref[rows] - turned(g, low_half) * sin_ref[rows]
        tile = proj_ref[at, cols]
        inverse = lax.rsqrt(split_dot(tile * tile, ones) + eps_norm)
        unit = tile * inverse
        f = g * gain
        return g * unit, inverse * (f - unit * split_dot(f * unit, ones))

    low_all = lax.broadcasted_iota(jnp.int32, (L, LANES), 1) < HEAD_SIZE
    row_low = lax.broadcasted_iota(jnp.int32, (LANES, T), 0) < HEAD_SIZE
    for n in range(heads):
        k = head_tile(rot_ref, qd + n * HEAD_SIZE, low_all)
        k_ref[...] = k
        kt_ref[...] = k.T
        v_ref[...] = head_tile(rot_ref, qd + kd + n * HEAD_SIZE, low_all)
        dk_ref[n] = jnp.zeros((L, LANES), f32)
        dv_ref[n] = jnp.zeros((L, LANES), f32)
        cols = slice(n * LANES, (n + 1) * LANES)
        for i in range(S):
            count = (i + 1) * T
            here = slice(i * T, count)
            q = rot_ref[here, cols]
            do = do_ref[here, cols]
            zero = jnp.zeros_like(q)
            q2 = jnp.concatenate([jnp.where(low, q, zero), jnp.where(low, zero, q)], axis=0)
            do2 = jnp.concatenate([jnp.where(low, do, zero), jnp.where(low, zero, do)], axis=0)
            logs = jnp.concatenate(
                [stat_ref[n * GROUP + a : n * GROUP + a + 1, here] for a in range(GROUP)], axis=1
            )
            delta = jnp.concatenate(
                [delta_ref[n * 8 + a : n * 8 + a + 1, here] for a in range(GROUP)], axis=1
            )
            s = times_t(k_ref[:count], q2)
            dp = times_t(v_ref[:count], do2)
            qpos = i * T + lax.broadcasted_iota(jnp.int32, (1, T), 1)
            qpos = jnp.concatenate([qpos, qpos], axis=1)
            p = masked_exp2(s * SCALE2 - logs, begins(starts, qpos), qpos, i * T, 0)
            ds = (p * (dp - delta)).astype(bf16)
            dv_ref[n, :count] += dot(p.astype(bf16), do2)
            dk_ref[n, :count] += dot(ds, q2)
            dqt = dot(kt_ref[:, :count], ds)
            dq = jnp.where(row_low, dqt[:, :T], dqt[:, T:]).T * SCALE
            rows = pl.ds(aligned(jnp.bitwise_xor(Q, i) * T, T), T)
            total, grad = finish(dq, rows, here, cols, gains_ref[2:3, :LANES])
            sums_ref[0:1] += jnp.sum(total, axis=0, keepdims=True)
            grad_ref[rows, cols] = grad.astype(bf16)

    def folded(ref, n, rows):
        x = ref[n, rows]
        return x + pltpu.roll(x, HEAD_SIZE, 1)

    for first in range(qd, qd + 2 * kd, LANES):
        cols = slice(first, first + LANES)
        for i in range(S):
            here = slice(i * T, (i + 1) * T)
            sides = []
            for part in (first, first + HEAD_SIZE):
                is_key = part < qd + kd
                n = (part - qd if is_key else part - qd - kd) // HEAD_SIZE
                sides.append(folded(dk_ref if is_key else dv_ref, n, here))
            g = jnp.where(low, sides[0], sides[1])
            rows = pl.ds(aligned(jnp.bitwise_xor(Q, i) * T, T), T)
            if first < qd + kd:
                total, grad = finish(g * SCALE, rows, here, cols, gains_ref[3:4, :LANES])
                if first + LANES > qd + kd:
                    total = jnp.where(low, total, 0.0)
                    grad = jnp.where(low, grad, g)
                sums_ref[1:2] += jnp.sum(total, axis=0, keepdims=True)
                g = grad
            grad_ref[rows, cols] = g.astype(bf16)


def input_grad_kernel(blocks, grad_ref, w_ref, *refs):
    many = len(blocks)
    xs, outs, total = refs[:many], refs[many : 2 * many], refs[2 * many]
    T = xs[0].shape[0]
    total[...] = jnp.zeros_like(total)
    for j, r in enumerate(blocks):
        g = times_t(grad_ref[r * T : (r + 1) * T], w_ref[...])
        outs[j][...] = g.astype(outs[j].dtype)
        x = xs[j][...].astype(f32)
        total[0:1] += jnp.sum(g * (x * inverse_root(x)), axis=0, keepdims=True)


def out_grad_kernel(S, att_ref, *refs):
    gbs, outs, total = refs[:S], refs[S : 2 * S], refs[2 * S]
    T = gbs[0].shape[0]
    od = outs[0].shape[1]
    Q = lax.axis_index("seq")
    acc = t_times(att_ref[:T], gbs[0][...])
    for r in range(1, S):
        acc += t_times(att_ref[r * T : (r + 1) * T], gbs[r][...])
    total[...] = acc
    for r in range(S):
        cols = pl.ds(aligned(jnp.bitwise_xor(Q, r) * od, LANES), od)
        outs[r][...] = total[:, cols].astype(bf16)


def pack_grad_kernel(S, N, nin_ref, grad_ref, sums_ref, pre_near, pre_far, post_ref, *refs):
    parts, (out, full, rows) = refs[:S], refs[S:]
    D = nin_ref.shape[1]
    d = D // N
    width = grad_ref.shape[1]
    qd, od = parts[0].shape
    small = HEAD_SIZE // N
    Q = lax.axis_index("seq")
    for r in range(S):
        full[pl.ds(aligned(jnp.bitwise_xor(Q, r) * qd, qd), qd)] = parts[r][...]
    term = t_times(nin_ref[...], grad_ref[...]).astype(bf16)
    pre = pre_near[0:1] + pre_far[0:1]
    sums = sums_ref[...] + pltpu.roll(sums_ref[...], HEAD_SIZE, 1)
    rows[...] = jnp.zeros_like(rows)
    for s in range(N):
        k = ring_slot(s, N)
        at = slice(s * d, (s + 1) * d)
        out[k, :d, :width] = term[at]
        out[k, :d, width:] = full[at]
        rows[0:1, :d] = pre[:, at]
        rows[1:2, :d] = post_ref[:, at]
        rows[2:4, :small] = sums[0:2, s * small : (s + 1) * small]
        out[k, d:, :LANES] = rows[...].astype(bf16)
        out[k, d:, LANES:] = jnp.zeros((GAIN_ROWS, width + od - LANES), bf16)


def load_chunks(N, pieces, extra, chunks, w, down, sems):
    d = w.shape[0] // N
    piece = down.shape[0] // N
    copies = []

    def copy(source, target):
        copies.append(pltpu.make_async_copy(source, target, sems.at[len(copies)]))
        copies[-1].start()

    for ref, (k, first, rows) in zip(chunks, pieces):
        s = ring_owner(k, N)
        count = min(d - first, rows)
        copy(ref.at[:count], w.at[pl.ds(aligned(s * d + first, 16), count)])
        if extra and first + rows > d:
            for row, col, at, left, many, cols in folds(extra, down.shape[1]):
                copy(
                    ref.at[count + row : count + row + many, col : col + cols],
                    down.at[pl.ds(aligned(s * piece + at, 16), many), left : left + cols],
                )
    for c in copies:
        c.wait()


def feed_kernel(N, many, pieces, extra, *refs):
    mids, cots, refs = refs[:many], refs[many : 2 * many], refs[2 * many :]
    if pieces:
        chunks, refs = refs[: len(pieces)], refs[len(pieces) :]
        if not extra:
            down, refs = refs[0], refs[1:]
            hidden, both, *outs, w, sems = refs
        else:
            hidden, both, *outs, w, down, sems = refs
        load_chunks(N, pieces, extra, chunks, w, down, sems)
    else:
        w, down, hidden, both, *outs = refs
    T = mids[0].shape[0]
    FQ = down.shape[0]
    step = FQ // 3
    for j in range(many):
        rows = slice(j * T, (j + 1) * T)
        x = mids[j][...]
        c = cots[j][...]
        for first in range(0, FQ, step):
            cols = slice(first, first + step)
            gate = dot(x, w[:, cols])
            upper = dot(x, w[:, FQ + first : FQ + first + step])
            grad = times_t(c, down[cols])
            sigmoid = 1.0 / (1.0 + jnp.exp(-gate))
            swish = gate * sigmoid
            hidden[rows, cols] = (swish * upper).astype(bf16)
            both[rows, cols] = (grad * sigmoid * upper * (1.0 + gate - swish)).astype(bf16)
            both[rows, FQ + first : FQ + first + step] = (grad * swish).astype(bf16)
        outs[j][...] = times_t(both[rows], w[...]).astype(outs[j].dtype)


def both_grad_kernel(S, N, slots, extra, *refs):
    mids, near, far, folded = refs[:S], refs[S], refs[S + 1], refs[S + 2]
    outs, left = refs[S + 3 : -1], refs[-1]
    T, D = mids[0].shape
    d = D // N
    half = S // 2 * T
    width = near.shape[1]
    for r in range(S):
        rows = slice(r * T, (r + 1) * T)
        x = None if d % LANES == 0 else mids[r][...].astype(f32)
        for j, k in enumerate(slots):
            s = ring_owner(k, N)
            if x is None:
                part = mids[r][:, pl.ds(aligned(s * d, LANES), d)]
            else:
                moved = pltpu.roll(x, jnp.where(s == 0, 0, D - s * d), 1)
                part = moved[:, :d].astype(bf16)
            left[rows, j * d : (j + 1) * d] = part
    step = width // 3
    for first in range(0, width, step):
        cols = slice(first, first + step)
        g = t_times(left[:half], near[:, cols]) + t_times(left[half:], far[:, cols])
        held = list(outs)
        for j, k in enumerate(slots):
            at = j * d
            while at < (j + 1) * d:
                out = held.pop(0)
                count = min(out.shape[0], (j + 1) * d - at)
                out[:count, cols] = g[at : at + count].astype(bf16)
                at += count
            if extra:
                out[count:, cols] = folded[k, :, cols]


def down_grad_kernel(S, N, extra, near, far, *refs):
    cots, (out, cot) = refs[:S], refs[S:]
    T = cots[0].shape[0]
    half = S // 2 * T
    for r in range(S):
        cot[r * T : (r + 1) * T] = cots[r][...]
    D = cot.shape[1]
    piece = near.shape[1] // N
    step = D // 2
    for first in range(0, D, step):
        cols = slice(first, first + step)
        g = t_times(near[...], cot[:half, cols]) + t_times(far[...], cot[half:, cols])
        for s in range(N):
            part = g[s * piece : (s + 1) * piece].astype(bf16)
            if not extra:
                out[s, :, cols] = part
                continue
            k = ring_slot(s, N)
            for row, col, at, left, rows, many in folds(extra, D):
                low, high = max(left, first), min(left + many, first + step)
                if low < high:
                    out[k, row : row + rows, col + low - left : col + high - left] = part[
                        at : at + rows, low - first : high - first
                    ]


def load_blocks(blocks, held, sems):
    Q = lax.axis_index("seq")
    copies = []
    for r, ref in enumerate(blocks):
        copies.append(
            pltpu.make_async_copy(ref, held.at[jnp.bitwise_xor(Q, r)], sems.at[r])
        )
        copies[-1].start()
    for c in copies:
        c.wait()


def both_out_kernel(S, N, extra, *refs):
    blocks, (gate, up, *down, held, sems) = refs[:S], refs[S:]
    load_blocks(blocks, held, sems)
    d = gate.shape[0]
    piece = gate.shape[1] // N // S
    for q in range(S):
        for base, out in ((0, gate), (N * piece, up)):
            for s in range(N):
                out[:, (s * S + q) * piece : (s * S + q + 1) * piece] = held[
                    q, :d, base + s * piece : base + (s + 1) * piece
                ].astype(f32)
        if extra:
            for row, col, at, left, rows, cols in folds(extra, down[0].shape[1]):
                down[0][q * piece + at : q * piece + at + rows, left : left + cols] = held[
                    q, d + row : d + row + rows, col : col + cols
                ].astype(f32)


def down_out_kernel(S, *refs):
    blocks, (out, held, sems) = refs[:S], refs[S:]
    load_blocks(blocks, held, sems)
    piece = held.shape[1]
    for q in range(S):
        out[q * piece : (q + 1) * piece] = held[q].astype(f32)


def pack_out_kernel(S, N, qd, kd, *refs):
    blocks, refs = refs[:S], refs[S:]
    outs, (pre, post, qgain, kgain, held, sems) = refs[:4], refs[4:]
    load_blocks(blocks, held, sems)
    d = outs[0].shape[0]
    od = outs[3].shape[1] // S
    at = 0
    for out, width in zip(outs, (qd, kd, kd, od)):
        for q in range(S):
            out[:, q * width : (q + 1) * width] = held[q, :d, at : at + width].astype(f32)
        at += width
    rows = held[0, d:, :LANES].astype(f32)
    for q in range(1, S):
        rows += held[q, d:, :LANES].astype(f32)
    for i, ref in enumerate((pre, post, qgain, kgain)):
        ref[...] = rows[i : i + 1, : ref.shape[1]]


def per_device(
    tokens,
    doc_starts,
    pre_gain,
    query_weight,
    key_matrix,
    value_matrix,
    query_gain,
    key_gain,
    out_weight,
    post_gain,
    gate_weight,
    up_weight,
    down_weight,
    cotangent,
):
    S = lax.axis_size("seq")
    N = lax.axis_size("shard")
    Q = lax.axis_index("seq")
    T, D = tokens.shape[1:]
    L = S * T
    d = D // N
    od = D // S
    qd = QUERY_HEADS * HEAD_SIZE // S
    kd = KEY_VALUE_HEADS * HEAD_SIZE // S
    width = qd + 2 * kd
    heads = kd // HEAD_SIZE
    FF = gate_weight.shape[1]
    piece = FF // N // S
    FQ = FF // S
    extra = fold_rows(piece, D, 2 * FQ)
    near, far = list(range(S // 2)), list(range(S // 2, S))
    dma = pltpu.SemaphoreType.DMA


    def swap(x, step):
        return lax.ppermute(x, "seq", [(i, i ^ step) for i in range(S)])

    def gather_seq(x):
        blocks = {0: x}
        step = S // 2
        while step:
            for r in list(blocks):
                blocks[r + step] = swap(blocks[r], step)
            step //= 2
        return [blocks[r] for r in range(S)]

    def block_shapes(blocks):
        return [shape((T, D), bf16 if r % 2 else f32) for r in blocks]

    order = ring_order(N)

    def hop(x, way):
        return lax.ppermute(x, "shard", [(order[i], order[(i + way) % N]) for i in range(N)])

    def after(x, *others):
        return lax.optimization_barrier((x, *others))[0]

    def pair(up, down):
        return lax.optimization_barrier((hop(up, 1), hop(down, -1)))


    def quarters(step):
        many = N // 2

        def quarter(i, *others):
            at = None
            for k in range(i * many // 4, (i + 1) * many // 4):
                at = step(k + 1, others)
            return at

        return quarter

    def gather_ring(x):
        half = x.shape[0] // 32 * 16
        chunks = [x]

        def step(k, others):
            up, down = chunks[-2:] if k > 1 else (x, x)
            if k == N // 2:
                up, down = up[:half], down[half:]
            up, down, *_ = lax.optimization_barrier((up, down, *others))
            chunks.extend(pair(up, down))
            return chunks[-1]

        return chunks, quarters(step)

    def scatter_ring(x, halves):
        half = halves[0].shape[0]
        moved = [*halves]
        sent = [*halves]

        def step(k, others):
            up, down = moved
            at = N // 2 + 1 - k
            if k > 1:
                ahead, behind = x[at].astype(f32), x[N - at].astype(f32)
                if k == 2:
                    ahead = jnp.concatenate([ahead[:half] + up.astype(f32), ahead[half:]], axis=0)
                    behind = jnp.concatenate(
                        [behind[:half], behind[half:] + down.astype(f32)], axis=0
                    )
                else:
                    ahead, behind = ahead + up.astype(f32), behind + down.astype(f32)
                up, down = ahead.astype(bf16), behind.astype(bf16)
            sent[:] = up, down
            up, down, *_ = lax.optimization_barrier((up, down, *others))
            moved[:] = pair(up, down)
            return moved[0]

        def total():
            return (x[0].astype(f32) + moved[0].astype(f32) + moved[1].astype(f32)).astype(bf16)

        return total, quarters(step), sent

    def partial_sum(blocks, low, size):
        if size == 2:
            return blocks[low] + swap(blocks[low + 1], 1).astype(f32)
        half = size // 2
        moved = swap(partial_sum(blocks, low + half, half).astype(bf16), half)
        return partial_sum(blocks, low, half) + moved.astype(f32)

    def far_part(blocks):
        return partial_sum([None] * len(near) + blocks, S // 2, S // 2).astype(bf16)

    (pack,) = call(
        functools.partial(pack_kernel, qd, kd, od),
        "v" * 8,
        (
            query_weight,
            key_matrix,
            value_matrix,
            out_weight,
            pre_gain[None],
            post_gain[None],
            query_gain[None],
            key_gain[None],
        ),
        [shape((d + GAIN_ROWS, width + od), bf16)],
        "v",
        [pltpu.VMEM((GAIN_ROWS, LANES), f32)],
        "pack",
    )
    pack_chunks, pack_ring = gather_ring(pack)
    pack_1 = pack_ring(0)
    local = tokens[0]
    xs = gather_seq(local)
    (both_columns,) = call(
        functools.partial(columns_kernel, S, N, piece, extra),
        "vvv",
        (after(gate_weight, pack), up_weight, down_weight),
        [shape((d + extra, 2 * FQ), bf16)],
        "v",
        [],
        "columns",
    )
    pack_2 = pack_ring(1, both_columns)
    starts = doc_starts[0]
    blocks_at = jnp.arange(S, dtype=jnp.int32) ^ Q
    places = (blocks_at[:, None] * T + jnp.arange(T, dtype=jnp.int32)[None, :]).reshape(L)
    cosine, sine = rope_tables(inside_of(after(starts, pack_1), places))
    cot = cotangent[0]
    cots = gather_seq(after(cot, pack_2))
    both_chunks, both_ring = gather_ring(both_columns)
    pack_ring(2, cosine, sine)
    pack_ring(3)
    both_1 = both_ring(0, pack_chunks[-1])
    both_pieces = arrived(N, d + extra)
    downs = []
    if not extra:
        own_rows = lax.dynamic_slice(
            down_weight, (Q * piece, 0), (piece, D), allow_negative_indices=False
        )
        downs = [lax.all_gather(own_rows, "shard", axis=0, tiled=True)]

    w_qkv, out_parts, gains = call(
        functools.partial(assemble_kernel, N, d, width, qd, od),
        "v" * len(pack_chunks),
        pack_chunks,
        [shape((D, width), bf16), shape((S, qd, od), bf16), shape((8, D), f32)],
        "vvv",
        [],
        "assemble",
    )
    out_blocks = [out_parts[0]] + [swap(out_parts[r], r) for r in range(1, S)]

    normed_in, proj, rotated, attended, stats = call(
        functools.partial(forward_kernel, S, qd, kd),
        "s" + "v" * (S + 4),
        (starts, *xs, after(w_qkv, cots[S // 2]), gains, cosine, sine),
        [
            shape((L, D), bf16),
            shape((L, -(-(qd + kd) // LANES) * LANES), f32),
            shape((L, width), bf16),
            shape((L, qd), bf16),
            shape((max(8, qd // HEAD_SIZE), L), f32),
        ],
        "v" * 5,
        [pltpu.VMEM((L, LANES), bf16), pltpu.VMEM((L, 2 * LANES), bf16)],
        "attend",
    )

    both_2 = both_ring(1)

    def project(blocks, whole):
        return call(
            functools.partial(out_kernel, S, blocks, whole),
            "v" * (S + 1),
            (attended, *out_blocks),
            block_shapes(blocks) + ([shape((qd, D), bf16)] if whole else []),
            "v" * (len(blocks) + whole),
            [],
            "project",
        )

    far_blocks = project(far, False)
    *near_blocks, full_out = project(near, True)
    far_sum = far_part(far_blocks)
    near_blocks[0] = after(near_blocks[0], both_2)
    both_ring(2)
    middle = (
        local.astype(f32)
        + partial_sum(near_blocks, 0, S // 2)
        + swap(far_sum, S // 2).astype(f32)
    )

    full_post = gains[1]
    root_mid = inverse_root(middle)
    scaled_mid = middle * root_mid
    normed_mid = (scaled_mid * full_post).astype(bf16)
    both_ring(3, normed_mid)
    mids = gather_seq(normed_mid)
    def feed(blocks, first, weights, pieces):
        rows = len(blocks) * T
        made = []
        if pieces:
            made = [shape((D, 2 * FQ), bf16)] + [shape((FQ, D), bf16)] * (extra > 0)
        return call(
            functools.partial(feed_kernel, N, len(blocks), pieces, extra),
            "v" * (2 * len(blocks))
            + ("a" * len(pieces) + "v" * (len(weights) - len(pieces)) if pieces else "vv"),
            (first, *[mids[r] for r in blocks[1:]], *[cots[r] for r in blocks], *weights),
            [shape((rows, FQ), bf16), shape((rows, 2 * FQ), bf16)] + block_shapes(blocks) + made,
            "v" * (2 + len(blocks) + len(made)),
            [dma((len(pieces) + 6 * N,))] if pieces else [],
            "feed",
        )

    hidden_far, both_far, *grads_far = feed(
        far, mids[far[0]], both_chunks + downs, both_pieces
    )
    if extra:
        downs = [grads_far.pop()]
    full_both = grads_far.pop()
    far_sum = far_part(grads_far)
    hidden_near, both_near, *grads_near = feed(
        near, after(mids[near[0]], far_sum), [full_both] + downs, []
    )
    far_moved = swap(far_sum, S // 2)
    term_both = {}
    split = (d + extra) // 32 * 16
    (term_down,) = call(
        functools.partial(down_grad_kernel, S, N, extra),
        "v" * (S + 2),
        (hidden_near, hidden_far, *cots),
        [shape((N, extra, 2 * FQ) if extra else (N, piece, D), bf16)],
        "v",
        [pltpu.VMEM((L, D), bf16)],
        "down_grad",
    )

    def both_grads(slots, side):
        rows = []
        for k in slots:
            rows += [split, d + extra - split] if k == N // 2 else [d + extra]
        terms = call(
            functools.partial(both_grad_kernel, S, N, slots, extra),
            "v" * (S + 3),
            (*mids, side, both_far, term_down),
            [shape((many, 2 * FQ), bf16) for many in rows],
            "v" * len(rows),
            [pltpu.VMEM((L, len(slots) * d), bf16)],
            "both_grad",
        )
        if slots[0] == N // 2:
            term_both[N // 2] = terms[:2]
            terms, slots = terms[2:], slots[1:]
        term_both.update(zip(slots, terms))
        return terms[0]

    middle_slots = [N // 2, N // 2 - 1, N // 2 + 1]
    grads_near[0] = after(grads_near[0], term_down)
    grad_nmid = partial_sum(grads_near, 0, S // 2) + far_moved.astype(f32)
    term_post = jnp.sum(grad_nmid * scaled_mid, axis=0)
    grad_middle = cot.astype(f32) + norm_back(grad_nmid * full_post, middle, root_mid)
    grad_branch = grad_middle.astype(bf16)
    first_terms = both_grads(middle_slots, after(both_near, grad_branch))
    both_total, both_back, both_sent = scatter_ring(term_both, term_both[N // 2])
    both_back(0)
    last_terms = both_grads(
        [k for k in range(N) if k not in middle_slots], after(both_near, first_terms)
    )
    both_back(1, last_terms)
    second = tuple(both_sent)
    output_blocks = []
    for hidden, blocks in ((after(hidden_near, *second), near), (hidden_far, far)):
        product = dot(hidden, downs[0])
        for j, r in enumerate(blocks):
            block = product[j * T : (j + 1) * T]
            output_blocks.append(block.astype(bf16) if r % 2 else block)

    out_sum = far_part(output_blocks[len(near) :])
    out_moved = swap(out_sum, S // 2)

    gbs = gather_seq(grad_branch)
    out_terms = call(
        functools.partial(out_grad_kernel, S),
        "v" * (S + 1),
        (attended, *gbs),
        [shape((qd, od), bf16)] * S,
        "v" * S,
        [pltpu.VMEM((qd, D), f32)],
        "out_grad",
    )
    first_gb = after(gbs[0], *second, out_terms[0], out_sum)
    grad_proj, sums = call(
        functools.partial(backward_kernel, S, qd, kd),
        "s" + "v" * (S + 8),
        (starts, first_gb, *gbs[1:], full_out, rotated, proj, attended, stats, gains, cosine, sine),
        [shape((L, width), bf16), shape((8, LANES), f32)],
        "vv",
        [
            pltpu.VMEM((L, qd), bf16),
            pltpu.VMEM((8 * heads, L), f32),
            pltpu.VMEM((L, LANES), bf16),
            pltpu.VMEM((LANES, L), bf16),
            pltpu.VMEM((L, LANES), bf16),
            pltpu.VMEM((heads, L, LANES), f32),
            pltpu.VMEM((heads, L, LANES), f32),
        ],
        "attend_back",
    )

    both_back(2, grad_proj)
    third = tuple(both_sent)
    back_4 = both_back(3)
    output_blocks[0] = after(output_blocks[0], grad_proj)
    output = middle + partial_sum(output_blocks, 0, S // 2) + out_moved.astype(f32)
    out_terms = [out_terms[0]] + [swap(out_terms[r], r) for r in range(1, S)]
    grad_proj = after(grad_proj, *third, out_moved, *out_terms[1:])

    def input_grads(blocks):
        return call(
            functools.partial(input_grad_kernel, blocks),
            "v" * (2 + len(blocks)),
            (grad_proj, w_qkv, *[xs[r] for r in blocks]),
            block_shapes(blocks) + [shape((8, D), f32)],
            "v" * (len(blocks) + 1),
            [],
            "input_grad",
        )

    *nins_far, pre_far = input_grads(far)
    *nins_near, pre_near = input_grads(near)
    nin_sum = far_part(nins_far)
    nin_moved = swap(nin_sum, S // 2)
    grad_nin = partial_sum(nins_near, 0, S // 2) + nin_moved.astype(f32)
    wide = local.astype(f32)
    grad_tokens = grad_middle + norm_back(grad_nin * gains[0], wide, inverse_root(wide))

    (pack_terms,) = call(
        functools.partial(pack_grad_kernel, S, N),
        "v" * (6 + S),
        (
            after(normed_in, nin_moved),
            grad_proj,
            sums,
            pre_near,
            pre_far,
            term_post[None],
            *out_terms,
        ),
        [shape((N, d + GAIN_ROWS, width + od), bf16)],
        "v",
        [pltpu.VMEM((D, od), bf16), pltpu.VMEM((GAIN_ROWS, LANES), f32)],
        "pack_grad",
    )
    split = (d + GAIN_ROWS) // 32 * 16
    pack_total, pack_back, _ = scatter_ring(
        pack_terms, (pack_terms[N // 2, :split], pack_terms[N // 2, split:])
    )
    pack_back(0, back_4)
    pack_back(1)
    pack_back(2)
    pack_back(3)

    gate_grad, up_grad, *down_grad = call(
        functools.partial(both_out_kernel, S, N, extra),
        "a" * S,
        gather_seq(both_total()),
        [shape((d, FF), f32), shape((d, FF), f32)] + [shape((S * piece, D), f32)] * (extra > 0),
        "vv" + "v" * (extra > 0),
        [pltpu.VMEM((S, d + extra, 2 * FQ), bf16), dma((S,))],
        "both_out",
    )
    if not extra:
        shard_down = lax.psum_scatter(
            term_down.reshape(FQ, D), "shard", scatter_dimension=0, tiled=True
        )
        down_grad = call(
            functools.partial(down_out_kernel, S),
            "a" * S,
            gather_seq(shard_down),
            [shape((S * piece, D), f32)],
            "v",
            [pltpu.VMEM((S, piece, D), bf16), dma((S,))],
            "down_out",
        )
    pack_blocks = gather_seq(pack_total())
    for r in range(1, S // 2):
        pack_blocks[S // 2 + r] = swap(after(pack_blocks[S // 2], gate_grad), r)
    small = HEAD_SIZE // N
    q_grad, k_grad, v_grad, o_grad, pre_grad, post_grad, qgain_grad, kgain_grad = call(
        functools.partial(pack_out_kernel, S, N, qd, kd),
        "a" * S,
        pack_blocks,
        [
            shape((d, S * qd), f32),
            shape((d, S * kd), f32),
            shape((d, S * kd), f32),
            shape((d, D), f32),
            shape((1, d), f32),
            shape((1, d), f32),
            shape((1, small), f32),
            shape((1, small), f32),
        ],
        "v" * 8,
        [pltpu.VMEM((S, d + GAIN_ROWS, width + od), bf16), dma((S,))],
        "pack_out",
    )
    return (
        output.astype(bf16)[None],
        grad_tokens[None],
        pre_grad[0],
        q_grad,
        k_grad,
        v_grad,
        qgain_grad[0],
        kgain_grad[0],
        o_grad,
        post_grad[0],
        gate_grad,
        up_grad,
        down_grad[0],
    )


def solution(mesh):
    row, vector, matrix = P("shard", "seq", None), P("shard"), P("shard", None)
    return jax.shard_map(
        per_device,
        mesh=mesh,
        in_specs=(
            row,
            matrix,
            vector,
            matrix,
            matrix,
            matrix,
            vector,
            vector,
            matrix,
            vector,
            matrix,
            matrix,
            matrix,
            row,
        ),
        out_specs=(
            row,
            row,
            vector,
            matrix,
            matrix,
            matrix,
            vector,
            vector,
            matrix,
            vector,
            matrix,
            matrix,
            matrix,
        ),
        check_vma=False,
    )
```
